32 devices in a mesh: dp: 2 (over y), gx: 4 (over x, core), gy: 4 (over z).
Axes of the slice: x: 2, y: 2, z: 4, core: 2. Of those that a mesh axis runs over, the one named last changes fastest.
Arguments:
- cell_values: float32 [2, 20, 32, 16, 512], P('dp', None, 'gx', 'gy'), may hold values from -6 to 6
- cotangent: float32 [2, 20, 32, 16, 512], P('dp', None, 'gx', 'gy'), may hold values from -6 to 6
- spectral_weight: float32 [2, 20, 20, 128, 256], P(None, None, None, ('gx', 'gy')), may hold values from -9 to 9
- channel_weight: float32 [20, 20], replicated, may hold values from -1.25 to 1.25
- channel_bias: float32 [20], replicated, may hold values from -4 to 4
Outputs:
- cell_grads: float32 [2, 20, 32, 16, 512], P('dp', None, 'gx', 'gy')
- spectral_grads: float32 [2, 20, 20, 128, 256], P(None, None, None, ('gx', 'gy'))
The draws below stay inside these ranges and needn't reach their ends.
All inputs are finite; a program needn't handle non-finite values.
Results may differ from the reference program's by a relative error of at most 0.00016.
Values sent between devices are 32-bit elements; how exact they have to be, the bound alone decides.
No kernel may reach another device: no remote copies, remote signals or barrier semaphores. Data moves between devices by JAX's collectives and lax.ppermute only.
A program may use at most 192 MiB of HBM per device.

```python
import jax
import jax.numpy as jnp
from jax import lax

CH = 20
NZ = 32
NT = 16
KX = 16
KY = 16
KZ = 16
KT = 8
NX = 32
NY = 16
ZT = 512
KZT = 128
KXY = 256
BATCH = 2


def block_scale(own_key, shape, cuts, low, high):
    level = 1.0
    for dim, shards_of in cuts:
        draws = jax.random.uniform(jax.random.fold_in(jax.random.fold_in(own_key, 6), dim), (shards_of,), jnp.float32, low / len(cuts), high / len(cuts))
        level = level * jnp.repeat(jnp.exp(draws), shape[dim] // shards_of).reshape((-1,) + (1,) * (len(shape) - 1 - dim))
    return level


def normal_values(stream_key, shape, width, most, cuts=(), kind=jnp.bfloat16):
    drawn = jax.random.normal(stream_key, shape, jnp.float32) * width
    if len(cuts) > 0:
        drawn = block_scale(stream_key, shape, cuts, -0.22, 0.18) * drawn
    return jnp.clip(drawn, min=-most, max=most).astype(kind)


def setup_inputs(seed: int = 0) -> dict:
    splits = jax.random.split(jax.random.key(seed), 6)
    return {
        "cell_values": normal_values(splits[0], (BATCH, CH, NX, NY, ZT), 1.0, 6.0, ((0, 2), (2, 4), (3, 4)), jnp.float32),
        "cotangent": normal_values(splits[1], (BATCH, CH, NX, NY, ZT), 1.0, 6.0, ((0, 2), (2, 4), (3, 4)), jnp.float32),
        "spectral_weight": normal_values(splits[2], (2, CH, CH, KZT, KXY), 1.5, 9.0, ((3, 16),), jnp.float32),
        "channel_weight": normal_values(splits[3], (CH, CH), CH ** -0.5, 1.25, (), jnp.float32),
        "channel_bias": normal_values(splits[4], (CH,), 1.0, 4.0, (), jnp.float32),
    }


highest = lax.Precision.HIGHEST


def gelu_slope(values):
    return 0.5 * (1.0 + lax.erf(values * 0.7071067811865476)) + values * jnp.exp(-0.5 * values * values) * 0.3989422804014327


def kept_index(length, kept_count):
    return jnp.concatenate([jnp.arange(kept_count // 2), jnp.arange(length - kept_count // 2, length)]).astype(jnp.int32)


def to_modes(sample_cells, counts):
    coeffs = sample_cells
    for axis_num in (4, 3, 2, 1):
        length = coeffs.shape[axis_num]
        coeffs = jnp.fft.fft(coeffs, axis=axis_num, norm="ortho")
        coeffs = jnp.take(coeffs, kept_index(length, counts[axis_num - 1]), axis=axis_num)
    return coeffs


def zero_fill(coeffs, axis_num, length):
    moved_axes = jnp.moveaxis(coeffs, axis_num, -1)
    kept_count = moved_axes.shape[-1]
    middle = jnp.zeros(moved_axes.shape[:-1] + (length - kept_count,), moved_axes.dtype)
    moved_axes = jnp.concatenate([moved_axes[..., : kept_count // 2], middle, moved_axes[..., kept_count // 2:]], axis=-1)
    return jnp.moveaxis(jnp.fft.ifft(moved_axes, axis=-1, norm="ortho"), -1, axis_num)


def to_cells(coeffs, lengths):
    values = coeffs
    for axis_num in (1, 2, 3, 4):
        values = zero_fill(values, axis_num, lengths[axis_num - 1])
    return values.real


def reference(cell_values, cotangent, spectral_weight, channel_weight, channel_bias):
    counts = (KX, KY, KZ, KT)
    lengths = (NX, NY, NZ, NT)
    weights = (spectral_weight[0] + 1j * spectral_weight[1]).reshape(CH, CH, KZ, KT, KY, KX)
    cell_grads = []
    partials = []
    for sample in range(BATCH):
        sample_cells = cell_values[sample].reshape(CH, NX, NY, NZ, NT)
        spectra = to_modes(sample_cells, counts)
        mixed = jnp.einsum("iabcd,iocdba->oabcd", spectra, weights)
        pre_act = jnp.einsum("oi,ixyzt->oxyzt", channel_weight, sample_cells, precision=highest) + channel_bias[:, None, None, None, None] + to_cells(mixed, lengths)
        grad_pre = cotangent[sample].reshape(CH, NX, NY, NZ, NT) * gelu_slope(pre_act)
        grad_spectra = to_modes(grad_pre, counts)
        partials.append(jnp.einsum("oabcd,iabcd->iocdba", grad_spectra, jnp.conj(spectra)))
        back_modes = jnp.einsum("iocdba,oabcd->iabcd", jnp.conj(weights), grad_spectra)
        cell_grad = jnp.einsum("oi,oxyzt->ixyzt", channel_weight, grad_pre, precision=highest) + to_cells(back_modes, lengths)
        cell_grads.append(cell_grad.reshape(CH, NX, NY, ZT).astype(jnp.float32))
    summed = partials[0]
    for further in partials[1:]:
        summed = summed + further
    spectral_grads = jnp.stack([summed.real, summed.imag]).reshape(2, CH, CH, KZT, KXY).astype(jnp.float32)
    return jnp.stack(cell_grads), spectral_grads
```

```python
import math

import jax
import jax.numpy as jnp
import numpy as np
from jax import lax
from jax.experimental import pallas as pl
from jax.experimental.pallas import tpu as pltpu
from jax.sharding import PartitionSpec as P

NZ = 32
NT = 16
KX = 16
KY = 16
KZ = 16
KT = 8


highest = lax.Precision.HIGHEST


def gelu_slope(values):
    return (
        0.5 * (1.0 + lax.erf(values * 0.7071067811865476))
        + values * jnp.exp(-0.5 * values * values) * 0.3989422804014327
    )


def signed_freq(number, kept_count):
    return jnp.where(number < kept_count // 2, number, number - kept_count)


def line_table(length, kept_count):
    positions = jnp.arange(length, dtype=jnp.int32)
    frequency = signed_freq(jnp.arange(kept_count, dtype=jnp.int32), kept_count)
    phases = positions[:, None] * frequency[None, :] % length
    angles = phases.astype(jnp.float32) * (-2.0 * math.pi / length)
    return jnp.stack([jnp.cos(angles), jnp.sin(angles)]) / math.sqrt(length)


def block_table(length, kept_count):
    table = line_table(length, kept_count)
    upper = jnp.stack([table[0], table[1]], axis=1)
    lower = jnp.stack([-table[1], table[0]], axis=1)
    return jnp.stack([upper, lower]).reshape(2 * length, 2 * kept_count)


def plane_table(mode_index):
    row_index = jnp.arange(NZ * NT, dtype=jnp.int32)
    depth = row_index // NT
    time_step = row_index % NT
    depth_freq = signed_freq(mode_index // KT, KZ)
    time_freq = signed_freq(mode_index % KT, KT)
    fraction = (depth[:, None] * depth_freq[None, :] % NZ).astype(jnp.float32) / NZ
    fraction = fraction + (time_step[:, None] * time_freq[None, :] % NT).astype(jnp.float32) / NT
    angles = fraction * (-2.0 * math.pi)
    table = jnp.stack([jnp.cos(angles), jnp.sin(angles)]) / math.sqrt(NZ * NT)
    return jnp.moveaxis(table, 0, -1).reshape(NZ * NT, -1)


def line_forward(data, block):
    return jnp.einsum("mpr,pk->mkr", data, block, precision=highest)


def line_adjoint(data, block):
    return jnp.einsum("mkr,pk->mpr", data, block, precision=highest)


def plane_front(real_field, planar, form):
    coeffs = jnp.einsum("cxyn,nk->" + form, real_field, planar, precision=highest)
    return coeffs.reshape(KZ * KT, 2, -1)


def plane_back(stacked, planar, form, first_cells, second_cells, channels):
    rows = stacked.reshape(-1, first_cells, second_cells, channels)
    return jnp.einsum(form + ",nk->cxyn", rows, planar, precision=highest)


def swap_inner(data, first, second, channels):
    leading = data.shape[0]
    moved = jnp.transpose(data.reshape(leading, 2, first, second, channels), (0, 1, 3, 2, 4))
    return moved.reshape(leading, 2, -1)


def mode_mix(weight, spectrum):

    def single(left_arg, right_arg):
        return jnp.einsum("imn,iomn->omn", left_arg, right_arg, precision=highest)

    real_part = single(spectrum[0], weight[0]) - single(spectrum[1], weight[1])
    imag_part = single(spectrum[1], weight[0]) + single(spectrum[0], weight[1])
    return jnp.stack([real_part, imag_part])


def mode_unmix(weight, spectrum):

    def single(left_arg, right_arg):
        return jnp.einsum("omn,iomn->imn", left_arg, right_arg, precision=highest)

    real_part = single(spectrum[0], weight[0]) + single(spectrum[1], weight[1])
    imag_part = single(spectrum[1], weight[0]) - single(spectrum[0], weight[1])
    return jnp.stack([real_part, imag_part])


def mode_outer(grad_spectrum, spectrum):

    def single(left_arg, right_arg):
        return jnp.einsum("omn,imn->iomn", left_arg, right_arg, precision=highest)

    real_part = single(grad_spectrum[0], spectrum[0]) + single(grad_spectrum[1], spectrum[1])
    imag_part = single(grad_spectrum[1], spectrum[0]) - single(grad_spectrum[0], spectrum[1])
    return jnp.stack([real_part, imag_part])


def on_device(cell_values, cotangent, spectral_weight, channel_weight, channel_bias):
    sample_cells = cell_values[0]
    upstream = cotangent[0]
    count_x = lax.axis_size("gx")
    count_y = lax.axis_size("gy")
    channels, cells_x, cells_y, depth_time = sample_cells.shape
    length_x = count_x * cells_x
    length_y = count_y * cells_y
    local_modes = KZ * KT // (count_x * count_y)
    block_x = block_table(length_x, KX)
    block_y = block_table(length_y, KY)
    column = jnp.arange(KZ * KT, dtype=jnp.int32)

    def to_spectrum(last):
        shaped = jnp.transpose(last.reshape(local_modes, 2, KX, KY, channels), (1, 4, 0, 3, 2))
        return shaped.reshape(2, channels, local_modes, KY * KX)

    def from_spectrum(spectrum):
        shaped = spectrum.reshape(2, channels, local_modes, KY, KX)
        return jnp.transpose(shaped, (2, 0, 4, 3, 1)).reshape(local_modes, 2 * KX, KY * channels)

    planar = plane_table(column)

    def forward(real_field):
        gathered = lax.all_to_all(
            plane_front(real_field, planar, "kyxc"),
            ("gx", "gy"),
            split_axis=0,
            concat_axis=2,
            tiled=True,
        )
        arranged = gathered.reshape(local_modes, 2, count_x, count_y, cells_y, cells_x * channels)
        arranged = jnp.transpose(arranged, (0, 1, 3, 4, 2, 5)).reshape(
            local_modes, 2 * length_y, length_x * channels
        )
        along_y = line_forward(arranged, block_y)
        along_y = swap_inner(along_y, KY, length_x, channels).reshape(
            local_modes, 2 * length_x, KY * channels
        )
        along_x = line_forward(along_y, block_x)
        return to_spectrum(along_x)

    def inverse(spectrum):
        back_x = line_adjoint(from_spectrum(spectrum), block_x)
        back_x = swap_inner(back_x, length_x, KY, channels).reshape(
            local_modes, 2 * KY, length_x * channels
        )
        back_y = line_adjoint(back_x, block_y)
        ordered = back_y.reshape(local_modes, 2, count_y, cells_y, count_x, cells_x * channels)
        ordered = jnp.transpose(ordered, (0, 1, 4, 2, 3, 5)).reshape(local_modes, 2, -1)
        spread = lax.all_to_all(ordered, ("gx", "gy"), split_axis=2, concat_axis=0, tiled=True)
        return plane_back(spread, planar, "kyxc", cells_y, cells_x, channels)

    spectra = forward(sample_cells)
    mixed = mode_mix(spectral_weight, spectra)
    pre_act = jnp.einsum("oi,ixyn->oxyn", channel_weight, sample_cells, precision=highest)
    pre_act = pre_act + channel_bias[:, None, None, None] + inverse(mixed)
    grad_pre = upstream * gelu_slope(pre_act)
    grad_spectra = forward(grad_pre)
    back_modes = mode_unmix(spectral_weight, grad_spectra)
    cell_grad = jnp.einsum("oi,oxyn->ixyn", channel_weight, grad_pre, precision=highest) + inverse(
        back_modes
    )
    spectral_grads = lax.psum(mode_outer(grad_spectra, spectra), "dp")
    return (cell_grad[None], spectral_grads)


LANES = 128
VMEM_LIMIT = 56 * 1024 * 1024


def params():
    return pltpu.CompilerParams(vmem_limit_bytes=VMEM_LIMIT)


def halves(values):
    upper = values.astype(jnp.bfloat16)
    return upper, (values - upper.astype(jnp.float32)).astype(jnp.bfloat16)


def host_halves(table):
    upper = table.astype(jnp.bfloat16)
    lower = (table - upper.astype(np.float64)).astype(jnp.bfloat16)
    return upper, lower


def host_freq(number, kept_count):
    return np.where(number < kept_count // 2, number, number - kept_count)


def host_plane(owners, local_modes):
    mode = np.arange(owners * local_modes)
    cell = np.arange(NZ * NT)
    turns = np.outer(host_freq(mode // KT, KZ), cell // NT) / NZ
    turns = turns + np.outer(host_freq(mode % KT, KT), cell % NT) / NT
    angles = 2.0 * np.pi * turns
    table = np.stack([np.cos(angles), -np.sin(angles)]) / np.sqrt(NZ * NT)
    table = table.reshape(2, owners, local_modes, NZ * NT)
    return np.swapaxes(table, 0, 1).reshape(owners * 2 * local_modes, NZ * NT)


def host_cross(count_x, count_y, cells_x, cells_y):
    length_x = count_x * cells_x
    length_y = count_y * cells_y
    row = np.arange(length_x * length_y)
    cell = row % (cells_x * cells_y)
    owner = row // (cells_x * cells_y)
    place_x = owner // count_y * cells_x + cell // cells_y
    place_y = owner % count_y * cells_y + cell % cells_y
    mode = np.arange(KY * KX)
    turns = np.outer(place_x, host_freq(mode % KX, KX)) / length_x
    turns = turns + np.outer(place_y, host_freq(mode // KX, KY)) / length_y
    angles = 2.0 * np.pi * turns
    return np.concatenate([np.cos(angles), np.sin(angles)], axis=1) / np.sqrt(length_x * length_y)


def product(left, right, left_dim, right_dim):
    dims = (((left_dim,), (right_dim,)), ((), ()))

    def single(one, other):
        return lax.dot_general(one, other, dims, preferred_element_type=jnp.float32)

    return single(left[0], right[0]) + (single(left[0], right[1]) + single(left[1], right[0]))


def swap_groups(parts):
    width = LANES // 4
    lane = lax.broadcasted_iota(jnp.int32, parts[0].shape, 1)
    low_half = lane < 2 * width
    low_quarter = lane % (2 * width) < width

    def trade(one, other, mask, shift):
        return (
            jnp.where(mask, one, pltpu.roll(other, shift, 1)),
            jnp.where(mask, pltpu.roll(one, LANES - shift, 1), other),
        )

    first, third = trade(parts[0], parts[2], low_half, 2 * width)
    second, fourth = trade(parts[1], parts[3], low_half, 2 * width)
    first, second = trade(first, second, low_quarter, width)
    third, fourth = trade(third, fourth, low_quarter, width)
    return first, second, third, fourth


def pack_rows(field_ref, rows_ref):
    channels, cells_x, cells_y, _ = field_ref.shape
    for channel in range(channels):
        for place in range(cells_x):
            row = (channel * cells_x + place) * cells_y
            rows_ref[row : row + cells_y, :] = field_ref[channel, place]


def front_kernel(field_ref, high_ref, low_ref, out_ref, rows_ref):
    pack_rows(field_ref, rows_ref)
    out_ref[...] = product((high_ref[...], low_ref[...]), halves(rows_ref[...]), 1, 1)


def mode_kernel(conjugate, got_ref, weight_ref, high_ref, low_ref, out_ref, spectra_ref, field_ref, mixed_ref):
    _, channels, local_modes, modes = spectra_ref.shape
    rows = channels * local_modes
    cells = high_ref.shape[0]
    owners = got_ref.shape[0] // (2 * local_modes)
    block = 2 * local_modes
    table = (high_ref[...], low_ref[...])
    for quad in range(owners // 4):
        for group in range(channels // 4):
            parts = [
                got_ref[(4 * quad + j) * block : (4 * quad + j + 1) * block, group * LANES : (group + 1) * LANES]
                for j in range(4)
            ]
            for m, part in enumerate(swap_groups(parts)):
                row = (4 * group + m) * local_modes
                for side in range(2):
                    field_ref[side * rows + row : side * rows + row + local_modes, quad * LANES : (quad + 1) * LANES] = part[
                        side * local_modes : (side + 1) * local_modes
                    ]
    waves = product(halves(field_ref[...]), table, 1, 0)
    real = waves[:rows, :modes] + waves[rows:, modes:]
    imag = waves[rows:, :modes] - waves[:rows, modes:]
    spectra_ref[0] = real.reshape(channels, local_modes, modes)
    spectra_ref[1] = imag.reshape(channels, local_modes, modes)
    for start in range(0, modes, LANES):
        span = slice(start, start + LANES)
        ins = [(spectra_ref[0, c, :, span], spectra_ref[1, c, :, span]) for c in range(channels)]

        def one(result, carry, span=span, ins=ins):
            total_real = jnp.zeros((local_modes, LANES), jnp.float32)
            total_imag = jnp.zeros((local_modes, LANES), jnp.float32)
            for c, (in_real, in_imag) in enumerate(ins):
                if conjugate:
                    w_real = weight_ref[0, result, c, :, span]
                    w_imag = weight_ref[1, result, c, :, span]
                    total_real = total_real + (in_real * w_real + in_imag * w_imag)
                    total_imag = total_imag + (in_imag * w_real - in_real * w_imag)
                else:
                    w_real = weight_ref[0, c, result, :, span]
                    w_imag = weight_ref[1, c, result, :, span]
                    total_real = total_real + (in_real * w_real - in_imag * w_imag)
                    total_imag = total_imag + (in_imag * w_real + in_real * w_imag)
            row = pl.multiple_of(result * local_modes, local_modes)
            other = pl.multiple_of(rows + result * local_modes, local_modes)
            mixed_ref[pl.ds(row, local_modes), start : start + LANES] = total_real
            mixed_ref[pl.ds(other, local_modes), start : start + LANES] = total_imag
            mixed_ref[pl.ds(row, local_modes), modes + start : modes + start + LANES] = -total_imag
            mixed_ref[pl.ds(other, local_modes), modes + start : modes + start + LANES] = total_real
            return carry

        lax.fori_loop(0, channels, one, 0)
    field_ref[...] = product(halves(mixed_ref[...]), table, 1, 1)
    for quad in range(owners // 4):
        for group in range(channels // 4):
            for side in range(2):
                first = side * rows + 4 * group * local_modes
                parts = [
                    field_ref[first + m * local_modes : first + (m + 1) * local_modes, quad * LANES : (quad + 1) * LANES]
                    for m in range(4)
                ]
                for j, part in enumerate(swap_groups(parts)):
                    row = (4 * quad + j) * block + side * local_modes
                    out_ref[row : row + local_modes, group * LANES : (group + 1) * LANES] = part


def channel_sums(transposed, rows_ref, weight_ref, bias_ref, out_ref, channels):
    height = rows_ref.shape[0] // channels
    for start in range(0, rows_ref.shape[1], LANES):
        span = slice(start, start + LANES)

        def one(step, carry, span=span):
            ins = [rows_ref[pl.ds(pl.multiple_of(i * height + step * 8, 8), 8), span] for i in range(channels)]
            for o in range(channels):
                total = None
                for i in range(channels):
                    factor = weight_ref[i, o] if transposed else weight_ref[o, i]
                    term = ins[i] * factor
                    total = term if total is None else total + term
                if bias_ref is not None:
                    total = total + bias_ref[o]
                out_ref[pl.ds(pl.multiple_of(o * height + step * 8, 8), 8), span] = total
            return carry

        lax.fori_loop(0, height // 8, one, 0)


def local_kernel(field_ref, upstream_ref, weight_ref, bias_ref, out_ref, packed_ref, rows_ref):
    pack_rows(field_ref, rows_ref)
    pack_rows(upstream_ref, packed_ref)
    channel_sums(False, rows_ref, weight_ref, bias_ref, out_ref, field_ref.shape[0])


def middle_kernel(got_ref, local_ref, upstream_ref, high_ref, low_ref, out_ref, grad_ref):
    table = (high_ref[...], low_ref[...])
    pre_act = product(halves(got_ref[...]), table, 0, 0) + local_ref[...]
    grad_ref[...] = upstream_ref[...] * gelu_slope(pre_act)
    out_ref[...] = product(table, halves(grad_ref[...]), 1, 1)


def grads_kernel(rows_ref, weight_ref, out_ref):
    channel_sums(True, rows_ref, weight_ref, None, out_ref, weight_ref.shape[0])


def last_kernel(got_ref, local_ref, high_ref, low_ref, out_ref, rows_ref):
    channels, cells_x, cells_y, _ = out_ref.shape
    rows_ref[...] = product(halves(got_ref[...]), (high_ref[...], low_ref[...]), 0, 0) + local_ref[...]
    for channel in range(channels):
        for place in range(cells_x):
            row = (channel * cells_x + place) * cells_y
            out_ref[channel, place] = rows_ref[row : row + cells_y, :]


def outer_kernel(spectra_ref, grads_ref, out_ref):
    _, _, channels, local_modes, modes = spectra_ref.shape
    source = pl.program_id(0)
    for start in range(0, modes, LANES):
        span = slice(start, start + LANES)
        ins = [(spectra_ref[s, 0, source, :, span], spectra_ref[s, 1, source, :, span]) for s in range(2)]
        for o in range(channels):
            total_real = None
            total_imag = None
            for s, (in_real, in_imag) in enumerate(ins):
                g_real = grads_ref[s, 0, o, :, span]
                g_imag = grads_ref[s, 1, o, :, span]
                real = g_real * in_real + g_imag * in_imag
                imag = g_imag * in_real - g_real * in_imag
                total_real = real if total_real is None else total_real + real
                total_imag = imag if total_imag is None else total_imag + imag
            out_ref[0, 0, o, :, span] = total_real
            out_ref[1, 0, o, :, span] = total_imag


def in_order(own):
    other = lax.ppermute(own, "dp", [(0, 1), (1, 0)])
    first = lax.axis_index("dp") == 0
    return jnp.stack([jnp.where(first, own, other), jnp.where(first, other, own)])


def on_tiles(cell_values, cotangent, spectral_weight, channel_weight, channel_bias):
    sample_cells = cell_values[0]
    upstream = cotangent[0]
    count_x = lax.axis_size("gx")
    count_y = lax.axis_size("gy")
    owners = count_x * count_y
    channels, cells_x, cells_y, depth_time = sample_cells.shape
    local_modes = spectral_weight.shape[3]
    modes = spectral_weight.shape[4]
    rows = channels * cells_x * cells_y
    plane = [jnp.asarray(t) for t in host_halves(host_plane(owners, local_modes))]
    cross = [jnp.asarray(t) for t in host_halves(host_cross(count_x, count_y, cells_x, cells_y))]
    f32 = jnp.float32
    whole = pl.BlockSpec(memory_space=pltpu.VMEM)
    scalars = pl.BlockSpec(memory_space=pltpu.SMEM)
    sent = jax.ShapeDtypeStruct((owners * 2 * local_modes, rows), f32)
    cells = jax.ShapeDtypeStruct((rows, depth_time), f32)
    spectrum = jax.ShapeDtypeStruct((2, channels, local_modes, modes), f32)

    def trade(values):
        return lax.all_to_all(values, ("gx", "gy"), split_axis=0, concat_axis=0, tiled=True)

    def across(values, conjugate):
        def body(*refs):
            mode_kernel(conjugate, *refs)

        return pl.pallas_call(
            body,
            out_shape=(sent, spectrum),
            in_specs=[whole] * 4,
            out_specs=(whole, whole),
            scratch_shapes=[
                pltpu.VMEM((2 * channels * local_modes, owners * cells_x * cells_y), f32),
                pltpu.VMEM((2 * channels * local_modes, 2 * modes), f32),
            ],
            compiler_params=params(),
            name="unmix_modes" if conjugate else "mix_modes",
        )(values, spectral_weight, *cross)

    front = pl.pallas_call(
        front_kernel,
        out_shape=sent,
        in_specs=[whole] * 3,
        out_specs=whole,
        scratch_shapes=[pltpu.VMEM((rows, depth_time), f32)],
        compiler_params=params(),
        name="front",
    )(sample_cells, *plane)
    got = trade(front)
    local, packed = pl.pallas_call(
        local_kernel,
        out_shape=(cells, cells),
        in_specs=[whole, whole, scalars, scalars],
        out_specs=(whole, whole),
        scratch_shapes=[pltpu.VMEM((rows, depth_time), f32)],
        compiler_params=params(),
        name="local_pre",
    )(sample_cells, upstream, channel_weight, channel_bias)
    mixed, spectra = across(got, False)
    both_spectra = in_order(spectra)
    got = trade(mixed)
    front, grad_pre = pl.pallas_call(
        middle_kernel,
        out_shape=(sent, cells),
        in_specs=[whole] * 5,
        out_specs=(whole, whole),
        compiler_params=params(),
        name="middle",
    )(got, local, packed, *plane)
    got = trade(front)
    back, grad_spectra = across(got, True)
    both_grads = in_order(grad_spectra)
    got = trade(back)
    local_grad = pl.pallas_call(
        grads_kernel,
        out_shape=cells,
        in_specs=[whole, scalars],
        out_specs=whole,
        compiler_params=params(),
        name="local_grad",
    )(grad_pre, channel_weight)
    full = pl.BlockSpec((2, 2, channels, local_modes, modes), lambda i: (0, 0, 0, 0, 0))
    spectral_grads = pl.pallas_call(
        outer_kernel,
        out_shape=jax.ShapeDtypeStruct(spectral_weight.shape, f32),
        grid=(channels,),
        in_specs=[full, full],
        out_specs=pl.BlockSpec((2, 1, channels, local_modes, modes), lambda i: (0, i, 0, 0, 0)),
        compiler_params=params(),
        name="outer",
    )(both_spectra, both_grads)
    cell_grad = pl.pallas_call(
        last_kernel,
        out_shape=jax.ShapeDtypeStruct(sample_cells.shape, f32),
        in_specs=[whole] * 4,
        out_specs=whole,
        scratch_shapes=[pltpu.VMEM((rows, depth_time), f32)],
        compiler_params=params(),
        name="last",
    )(got, local_grad, *plane)
    return (cell_grad[None], spectral_grads)


def solution(mesh):
    placed = (
        P("dp", None, "gx", "gy", None),
        P("dp", None, "gx", "gy", None),
        P(None, None, None, ("gx", "gy"), None),
        P(),
        P(),
    )

    def on_any(*args):
        _, channels, cells_x, cells_y, _ = args[0].shape
        owners = lax.axis_size("gx") * lax.axis_size("gy")
        fits = args[2].shape[3] == 8 and cells_x * cells_y == LANES // 4
        fits = fits and channels % 4 == 0 and owners % 4 == 0 and lax.axis_size("dp") == 2
        return on_tiles(*args) if fits else on_device(*args)

    return jax.shard_map(
        on_any,
        mesh=mesh,
        in_specs=placed,
        out_specs=(P("dp", None, "gx", "gy", None), P(None, None, None, ("gx", "gy"), None)),
        check_vma=False,
    )
```

```python
import math

import jax
import jax.numpy as jnp
import numpy as np
from jax import lax
from jax.experimental import pallas as pl
from jax.experimental.pallas import tpu as pltpu
from jax.sharding import PartitionSpec as P

NZ = 32
NT = 16
KX = 16
KY = 16
KZ = 16
KT = 8


highest = lax.Precision.HIGHEST


def gelu_slope(values):
    return (
        0.5 * (1.0 + lax.erf(values * 0.7071067811865476))
        + values * jnp.exp(-0.5 * values * values) * 0.3989422804014327
    )


def signed_freq(number, kept_count):
    return jnp.where(number < kept_count // 2, number, number - kept_count)


def line_table(length, kept_count):
    positions = jnp.arange(length, dtype=jnp.int32)
    frequency = signed_freq(jnp.arange(kept_count, dtype=jnp.int32), kept_count)
    phases = positions[:, None] * frequency[None, :] % length
    angles = phases.astype(jnp.float32) * (-2.0 * math.pi / length)
    return jnp.stack([jnp.cos(angles), jnp.sin(angles)]) / math.sqrt(length)


def block_table(length, kept_count):
    table = line_table(length, kept_count)
    upper = jnp.stack([table[0], table[1]], axis=1)
    lower = jnp.stack([-table[1], table[0]], axis=1)
    return jnp.stack([upper, lower]).reshape(2 * length, 2 * kept_count)


def plane_table(mode_index):
    row_index = jnp.arange(NZ * NT, dtype=jnp.int32)
    depth = row_index // NT
    time_step = row_index % NT
    depth_freq = signed_freq(mode_index // KT, KZ)
    time_freq = signed_freq(mode_index % KT, KT)
    fraction = (depth[:, None] * depth_freq[None, :] % NZ).astype(jnp.float32) / NZ
    fraction = fraction + (time_step[:, None] * time_freq[None, :] % NT).astype(jnp.float32) / NT
    angles = fraction * (-2.0 * math.pi)
    table = jnp.stack([jnp.cos(angles), jnp.sin(angles)]) / math.sqrt(NZ * NT)
    return jnp.moveaxis(table, 0, -1).reshape(NZ * NT, -1)


def line_forward(data, block):
    return jnp.einsum("mpr,pk->mkr", data, block, precision=highest)


def line_adjoint(data, block):
    return jnp.einsum("mkr,pk->mpr", data, block, precision=highest)


def plane_front(real_field, planar, form):
    coeffs = jnp.einsum("cxyn,nk->" + form, real_field, planar, precision=highest)
    return coeffs.reshape(KZ * KT, 2, -1)


def plane_back(stacked, planar, form, first_cells, second_cells, channels):
    rows = stacked.reshape(-1, first_cells, second_cells, channels)
    return jnp.einsum(form + ",nk->cxyn", rows, planar, precision=highest)


def swap_inner(data, first, second, channels):
    leading = data.shape[0]
    moved = jnp.transpose(data.reshape(leading, 2, first, second, channels), (0, 1, 3, 2, 4))
    return moved.reshape(leading, 2, -1)


def mode_mix(weight, spectrum):

    def single(left_arg, right_arg):
        return jnp.einsum("imn,iomn->omn", left_arg, right_arg, precision=highest)

    real_part = single(spectrum[0], weight[0]) - single(spectrum[1], weight[1])
    imag_part = single(spectrum[1], weight[0]) + single(spectrum[0], weight[1])
    return jnp.stack([real_part, imag_part])


def mode_unmix(weight, spectrum):

    def single(left_arg, right_arg):
        return jnp.einsum("omn,iomn->imn", left_arg, right_arg, precision=highest)

    real_part = single(spectrum[0], weight[0]) + single(spectrum[1], weight[1])
    imag_part = single(spectrum[1], weight[0]) - single(spectrum[0], weight[1])
    return jnp.stack([real_part, imag_part])


def mode_outer(grad_spectrum, spectrum):

    def single(left_arg, right_arg):
        return jnp.einsum("omn,imn->iomn", left_arg, right_arg, precision=highest)

    real_part = single(grad_spectrum[0], spectrum[0]) + single(grad_spectrum[1], spectrum[1])
    imag_part = single(grad_spectrum[1], spectrum[0]) - single(grad_spectrum[0], spectrum[1])
    return jnp.stack([real_part, imag_part])


def on_device(cell_values, cotangent, spectral_weight, channel_weight, channel_bias):
    sample_cells = cell_values[0]
    upstream = cotangent[0]
    count_x = lax.axis_size("gx")
    count_y = lax.axis_size("gy")
    channels, cells_x, cells_y, depth_time = sample_cells.shape
    length_x = count_x * cells_x
    length_y = count_y * cells_y
    local_modes = KZ * KT // (count_x * count_y)
    block_x = block_table(length_x, KX)
    block_y = block_table(length_y, KY)
    column = jnp.arange(KZ * KT, dtype=jnp.int32)

    def to_spectrum(last):
        shaped = jnp.transpose(last.reshape(local_modes, 2, KX, KY, channels), (1, 4, 0, 3, 2))
        return shaped.reshape(2, channels, local_modes, KY * KX)

    def from_spectrum(spectrum):
        shaped = spectrum.reshape(2, channels, local_modes, KY, KX)
        return jnp.transpose(shaped, (2, 0, 4, 3, 1)).reshape(local_modes, 2 * KX, KY * channels)

    planar = plane_table(column)

    def forward(real_field):
        gathered = lax.all_to_all(
            plane_front(real_field, planar, "kyxc"),
            ("gx", "gy"),
            split_axis=0,
            concat_axis=2,
            tiled=True,
        )
        arranged = gathered.reshape(local_modes, 2, count_x, count_y, cells_y, cells_x * channels)
        arranged = jnp.transpose(arranged, (0, 1, 3, 4, 2, 5)).reshape(
            local_modes, 2 * length_y, length_x * channels
        )
        along_y = line_forward(arranged, block_y)
        along_y = swap_inner(along_y, KY, length_x, channels).reshape(
            local_modes, 2 * length_x, KY * channels
        )
        along_x = line_forward(along_y, block_x)
        return to_spectrum(along_x)

    def inverse(spectrum):
        back_x = line_adjoint(from_spectrum(spectrum), block_x)
        back_x = swap_inner(back_x, length_x, KY, channels).reshape(
            local_modes, 2 * KY, length_x * channels
        )
        back_y = line_adjoint(back_x, block_y)
        ordered = back_y.reshape(local_modes, 2, count_y, cells_y, count_x, cells_x * channels)
        ordered = jnp.transpose(ordered, (0, 1, 4, 2, 3, 5)).reshape(local_modes, 2, -1)
        spread = lax.all_to_all(ordered, ("gx", "gy"), split_axis=2, concat_axis=0, tiled=True)
        return plane_back(spread, planar, "kyxc", cells_y, cells_x, channels)

    spectra = forward(sample_cells)
    mixed = mode_mix(spectral_weight, spectra)
    pre_act = jnp.einsum("oi,ixyn->oxyn", channel_weight, sample_cells, precision=highest)
    pre_act = pre_act + channel_bias[:, None, None, None] + inverse(mixed)
    grad_pre = upstream * gelu_slope(pre_act)
    grad_spectra = forward(grad_pre)
    back_modes = mode_unmix(spectral_weight, grad_spectra)
    cell_grad = jnp.einsum("oi,oxyn->ixyn", channel_weight, grad_pre, precision=highest) + inverse(
        back_modes
    )
    spectral_grads = lax.psum(mode_outer(grad_spectra, spectra), "dp")
    return (cell_grad[None], spectral_grads)


LANES = 128
VMEM_LIMIT = 24 * 1024 * 1024


def params():
    return pltpu.CompilerParams(vmem_limit_bytes=VMEM_LIMIT)


def halves(values):
    upper = values.astype(jnp.bfloat16)
    return upper, (values - upper.astype(jnp.float32)).astype(jnp.bfloat16)


def host_halves(table):
    upper = table.astype(jnp.bfloat16)
    lower = (table - upper.astype(np.float64)).astype(jnp.bfloat16)
    return upper, lower


def host_freq(number, kept_count):
    return np.where(number < kept_count // 2, number, number - kept_count)


def host_plane(owners, local_modes):
    mode = np.arange(owners * local_modes)
    cell = np.arange(NZ * NT)
    turns = np.outer(host_freq(mode // KT, KZ), cell // NT) / NZ
    turns = turns + np.outer(host_freq(mode % KT, KT), cell % NT) / NT
    angles = 2.0 * np.pi * turns
    table = np.stack([np.cos(angles), -np.sin(angles)]) / np.sqrt(NZ * NT)
    table = table.reshape(2, owners, local_modes, NZ * NT)
    return np.swapaxes(table, 0, 1).reshape(owners * 2 * local_modes, NZ * NT)


def host_cross(count_x, count_y, cells_x, cells_y):
    length_x = count_x * cells_x
    length_y = count_y * cells_y
    row = np.arange(length_x * length_y)
    cell = row % (cells_x * cells_y)
    owner = row // (cells_x * cells_y)
    place_x = owner // count_y * cells_x + cell // cells_y
    place_y = owner % count_y * cells_y + cell % cells_y
    mode = np.arange(KY * KX)
    turns = np.outer(place_x, host_freq(mode % KX, KX)) / length_x
    turns = turns + np.outer(place_y, host_freq(mode // KX, KY)) / length_y
    angles = 2.0 * np.pi * turns
    return np.concatenate([np.cos(angles), np.sin(angles)], axis=1) / np.sqrt(length_x * length_y)


def product(left, right, left_dim, right_dim):
    dims = (((left_dim,), (right_dim,)), ((), ()))

    def single(one, other):
        return lax.dot_general(one, other, dims, preferred_element_type=jnp.float32)

    return single(left[0], right[0]) + (single(left[0], right[1]) + single(left[1], right[0]))


def swap_groups(parts):
    width = LANES // 4
    lane = lax.broadcasted_iota(jnp.int32, parts[0].shape, 1)
    low_half = lane < 2 * width
    low_quarter = lane % (2 * width) < width

    def trade(one, other, mask, shift):
        return (
            jnp.where(mask, one, pltpu.roll(other, shift, 1)),
            jnp.where(mask, pltpu.roll(one, LANES - shift, 1), other),
        )

    first, third = trade(parts[0], parts[2], low_half, 2 * width)
    second, fourth = trade(parts[1], parts[3], low_half, 2 * width)
    first, second = trade(first, second, low_quarter, width)
    third, fourth = trade(third, fourth, low_quarter, width)
    return first, second, third, fourth


def pack_rows(field_ref, rows_ref):
    channels, cells_x, cells_y, _ = field_ref.shape
    for channel in range(channels):
        for place in range(cells_x):
            row = (channel * cells_x + place) * cells_y
            rows_ref[row : row + cells_y, :] = field_ref[channel, place]


def start(source, target, semaphore):
    copy = pltpu.make_async_copy(source, target, semaphore)
    copy.start()
    return copy


def front_kernel(field_hbm, high_hbm, low_hbm, out_ref, field_ref, high_ref, low_ref, rows_ref, table_sems, field_sems):
    channels, cells_x, cells_y, _ = field_ref.shape
    tables = [start(high_hbm, high_ref, table_sems.at[0]), start(low_hbm, low_ref, table_sems.at[1])]
    pieces = []
    for first in range(0, channels, 8):
        span = pl.ds(first, min(8, channels - first))
        pieces.append((span, start(field_hbm.at[span], field_ref.at[span], field_sems.at[len(pieces)])))
    for copy in tables:
        copy.wait()
    table = (high_ref[...], low_ref[...])
    for span, copy in pieces:
        copy.wait()
        first = span.start * cells_x * cells_y
        last = first + span.size * cells_x * cells_y
        for channel in range(span.start, span.start + span.size):
            for place in range(cells_x):
                row = (channel * cells_x + place) * cells_y
                rows_ref[row : row + cells_y, :] = field_ref[channel, place]
        out_ref[:, first:last] = product(table, halves(rows_ref[first:last, :]), 1, 1)


def mode_kernel(
    conjugate,
    got_ref,
    weight_hbm,
    high_ref,
    low_ref,
    out_hbm,
    spectra_hbm,
    weight_ref,
    out_ref,
    spectra_ref,
    field_ref,
    mixed_ref,
    weight_sems,
    spectra_sem,
    out_sems,
):
    _, channels, local_modes, modes = spectra_ref.shape
    chunk = channels // weight_sems.shape[0]
    weight_copies = []
    for k in range(weight_sems.shape[0]):
        span = pl.ds(k * chunk, chunk)
        place = (slice(None), span) if conjugate else (slice(None), slice(None), span)
        weight_copies.append(start(weight_hbm.at[place], weight_ref.at[place], weight_sems.at[k]))
    rows = channels * local_modes
    cells = high_ref.shape[0]
    owners = got_ref.shape[0] // (2 * local_modes)
    block = 2 * local_modes
    table = (high_ref[...], low_ref[...])
    for quad in range(owners // 4):
        for group in range(channels // 4):
            parts = [
                got_ref[(4 * quad + j) * block : (4 * quad + j + 1) * block, group * LANES : (group + 1) * LANES]
                for j in range(4)
            ]
            for m, part in enumerate(swap_groups(parts)):
                row = (4 * group + m) * local_modes
                for side in range(2):
                    field_ref[side * rows + row : side * rows + row + local_modes, quad * LANES : (quad + 1) * LANES] = part[
                        side * local_modes : (side + 1) * local_modes
                    ]
    waves = product(halves(field_ref[...]), table, 1, 0)
    real = waves[:rows, :modes] + waves[rows:, modes:]
    imag = waves[rows:, :modes] - waves[:rows, modes:]
    spectra_ref[0] = real.reshape(channels, local_modes, modes)
    spectra_ref[1] = imag.reshape(channels, local_modes, modes)
    spectra_copy = start(spectra_ref, spectra_hbm, spectra_sem)
    for part in range(len(weight_copies) * modes // LANES):
        first_lane = part % (modes // LANES) * LANES
        first_result = part // (modes // LANES) * chunk
        span = slice(first_lane, first_lane + LANES)
        ins = [(spectra_ref[0, c, :, span], spectra_ref[1, c, :, span]) for c in range(channels)]
        if first_lane == 0:
            weight_copies[part // (modes // LANES)].wait()

        def one(step, carry, span=span, ins=ins, first_lane=first_lane, first_result=first_result):
            result = first_result + step
            total_real = jnp.zeros((local_modes, LANES), jnp.float32)
            total_imag = jnp.zeros((local_modes, LANES), jnp.float32)
            for c, (in_real, in_imag) in enumerate(ins):
                if conjugate:
                    w_real = weight_ref[0, result, c, :, span]
                    w_imag = weight_ref[1, result, c, :, span]
                    total_real = total_real + (in_real * w_real + in_imag * w_imag)
                    total_imag = total_imag + (in_imag * w_real - in_real * w_imag)
                else:
                    w_real = weight_ref[0, c, result, :, span]
                    w_imag = weight_ref[1, c, result, :, span]
                    total_real = total_real + (in_real * w_real - in_imag * w_imag)
                    total_imag = total_imag + (in_imag * w_real + in_real * w_imag)
            row = pl.multiple_of(result * local_modes, local_modes)
            other = pl.multiple_of(rows + result * local_modes, local_modes)
            mixed_ref[pl.ds(row, local_modes), first_lane : first_lane + LANES] = total_real
            mixed_ref[pl.ds(other, local_modes), first_lane : first_lane + LANES] = total_imag
            mixed_ref[pl.ds(row, local_modes), modes + first_lane : modes + first_lane + LANES] = -total_imag
            mixed_ref[pl.ds(other, local_modes), modes + first_lane : modes + first_lane + LANES] = total_real
            return carry

        lax.fori_loop(0, chunk, one, 0)
    field_ref[...] = product(halves(mixed_ref[...]), table, 1, 1)
    out_copies = []
    for quad in range(owners // 4):
        for group in range(channels // 4):
            for side in range(2):
                first = side * rows + 4 * group * local_modes
                parts = [
                    field_ref[first + m * local_modes : first + (m + 1) * local_modes, quad * LANES : (quad + 1) * LANES]
                    for m in range(4)
                ]
                for j, part in enumerate(swap_groups(parts)):
                    row = (4 * quad + j) * block + side * local_modes
                    out_ref[row : row + local_modes, group * LANES : (group + 1) * LANES] = part
        span = pl.ds(4 * quad * block, 4 * block)
        out_copies.append(start(out_ref.at[span], out_hbm.at[span], out_sems.at[quad]))
    spectra_copy.wait()
    for copy in out_copies:
        copy.wait()


def channel_sums(transposed, rows_ref, weight_ref, bias_ref, out_ref, channels):
    height = rows_ref.shape[0] // channels
    for lane in range(0, rows_ref.shape[1], LANES):
        span = slice(lane, lane + LANES)

        def one(step, carry, span=span):
            ins = [rows_ref[pl.ds(pl.multiple_of(i * height + step * 8, 8), 8), span] for i in range(channels)]
            for o in range(channels):
                total = None
                for i in range(channels):
                    factor = weight_ref[i, o] if transposed else weight_ref[o, i]
                    term = ins[i] * factor
                    total = term if total is None else total + term
                if bias_ref is not None:
                    total = total + bias_ref[o]
                out_ref[pl.ds(pl.multiple_of(o * height + step * 8, 8), 8), span] = total
            return carry

        lax.fori_loop(0, height // 8, one, 0)


def local_kernel(field_ref, upstream_ref, weight_ref, bias_ref, out_ref, packed_ref, rows_ref):
    pack_rows(field_ref, rows_ref)
    pack_rows(upstream_ref, packed_ref)
    channel_sums(False, rows_ref, weight_ref, bias_ref, out_ref, field_ref.shape[0])


def middle_kernel(got_ref, local_hbm, upstream_hbm, high_ref, low_ref, out_ref, grad_hbm, local_ref, upstream_ref, grad_ref, sems):
    copies = [start(local_hbm, local_ref, sems.at[0]), start(upstream_hbm, upstream_ref, sems.at[1])]
    table = (high_ref[...], low_ref[...])
    grad_ref[...] = product(halves(got_ref[...]), table, 0, 0)
    for copy in copies:
        copy.wait()
    grad_ref[...] = upstream_ref[...] * gelu_slope(grad_ref[...] + local_ref[...])
    copy = start(grad_ref, grad_hbm, sems.at[2])
    out_ref[...] = product(table, halves(grad_ref[...]), 1, 1)
    copy.wait()


def grads_kernel(rows_ref, weight_ref, out_ref):
    channel_sums(True, rows_ref, weight_ref, None, out_ref, weight_ref.shape[0])


def last_kernel(got_ref, local_hbm, high_ref, low_ref, out_hbm, local_ref, out_ref, local_sem, out_sems):
    channels, cells_x, cells_y, _ = out_ref.shape
    local_copy = start(local_hbm, local_ref, local_sem)
    table = (high_ref[...], low_ref[...])
    copies = []
    for first in range(0, channels, 4):
        begin = first * cells_x * cells_y
        end = (first + 4) * cells_x * cells_y
        values = product(halves(got_ref[:, begin:end]), table, 0, 0)
        if first == 0:
            local_copy.wait()
        local_ref[begin:end, :] = local_ref[begin:end, :] + values
        for channel in range(first, first + 4):
            for place in range(cells_x):
                row = (channel * cells_x + place) * cells_y
                out_ref[channel, place] = local_ref[row : row + cells_y, :]
        span = pl.ds(first, 4)
        copies.append(start(out_ref.at[span], out_hbm.at[span], out_sems.at[len(copies)]))
    for copy in copies:
        copy.wait()


def outer_kernel(first_spectra, second_spectra, first_grads, second_grads, out_ref):
    _, channels, local_modes, modes = first_spectra.shape
    sources = out_ref.shape[1]
    pairs = ((first_spectra, first_grads), (second_spectra, second_grads))

    def one(step, carry):
        source = pl.program_id(0) * sources + step
        for lane in range(0, modes, LANES):
            span = slice(lane, lane + LANES)
            ins = [(spectra[0, source, :, span], spectra[1, source, :, span]) for spectra, _ in pairs]
            for o in range(channels):
                total_real = None
                total_imag = None
                for (_, grads), (in_real, in_imag) in zip(pairs, ins):
                    g_real = grads[0, o, :, span]
                    g_imag = grads[1, o, :, span]
                    real = g_real * in_real + g_imag * in_imag
                    imag = g_imag * in_real - g_real * in_imag
                    total_real = real if total_real is None else total_real + real
                    total_imag = imag if total_imag is None else total_imag + imag
                out_ref[0, step, o, :, span] = total_real
                out_ref[1, step, o, :, span] = total_imag
        return carry

    lax.fori_loop(0, sources, one, 0)


def in_order(own):
    other = lax.ppermute(own, "dp", [(0, 1), (1, 0)])
    first = lax.axis_index("dp") == 0
    return jnp.where(first, own, other), jnp.where(first, other, own)


def far(*values):
    return [pltpu.with_memory_space_constraint(v, pltpu.HBM) for v in values]


def near(*values):
    return [pltpu.with_memory_space_constraint(v, pltpu.VMEM) for v in values]


def on_tiles(cell_values, cotangent, spectral_weight, channel_weight, channel_bias):
    sample_cells = cell_values[0]
    upstream = cotangent[0]
    count_x = lax.axis_size("gx")
    count_y = lax.axis_size("gy")
    owners = count_x * count_y
    channels, cells_x, cells_y, depth_time = sample_cells.shape
    local_modes = spectral_weight.shape[3]
    modes = spectral_weight.shape[4]
    rows = channels * cells_x * cells_y
    plane = [jnp.asarray(t) for t in host_halves(host_plane(owners, local_modes))]
    cross = [jnp.asarray(t) for t in host_halves(host_cross(count_x, count_y, cells_x, cells_y))]
    f32 = jnp.float32
    bf16 = jnp.bfloat16
    whole = pl.BlockSpec(memory_space=pltpu.VMEM)
    scalars = pl.BlockSpec(memory_space=pltpu.SMEM)
    stays = pl.BlockSpec(memory_space=pltpu.HBM)
    copies = pltpu.SemaphoreType.DMA
    vmem = pltpu.VMEM
    sent = (owners * 2 * local_modes, rows)
    cells = (rows, depth_time)
    spectrum = (2, channels, local_modes, modes)
    group = next(g for g in (4, 2, 1) if channels % g == 0)

    def held(shape):
        return pltpu.HBM(shape, f32)

    def trade(values):
        return lax.all_to_all(values, ("gx", "gy"), split_axis=0, concat_axis=0, tiled=True)

    def across(values, conjugate):
        def body(*refs):
            mode_kernel(conjugate, *refs)

        return pl.pallas_call(
            body,
            out_shape=(held(sent), held(spectrum)),
            in_specs=[whole, stays, whole, whole],
            out_specs=(stays, stays),
            scratch_shapes=[
                vmem(spectral_weight.shape, f32),
                vmem(sent, f32),
                vmem(spectrum, f32),
                vmem((2 * channels * local_modes, owners * cells_x * cells_y), f32),
                vmem((2 * channels * local_modes, 2 * modes), f32),
                copies((4,)),
                copies,
                copies((owners // 4,)),
            ],
            compiler_params=params(),
            name="unmix_modes" if conjugate else "mix_modes",
        )(*near(values), *far(spectral_weight), *near(*cross))

    front = pl.pallas_call(
        front_kernel,
        out_shape=vmem(sent, f32),
        in_specs=[stays] * 3,
        out_specs=whole,
        scratch_shapes=[
            vmem(sample_cells.shape, f32),
            vmem(plane[0].shape, bf16),
            vmem(plane[1].shape, bf16),
            vmem(cells, f32),
            copies((2,)),
            copies((-(-channels // 8),)),
        ],
        compiler_params=params(),
        name="front",
    )(*far(sample_cells, *plane))
    got = trade(front)
    local, packed = pl.pallas_call(
        local_kernel,
        out_shape=(held(cells), held(cells)),
        in_specs=[whole, whole, scalars, scalars],
        out_specs=(whole, whole),
        scratch_shapes=[vmem(cells, f32)],
        compiler_params=params(),
        name="local_pre",
    )(*far(sample_cells, upstream), channel_weight, channel_bias)
    mixed, spectra = across(got, False)
    both_spectra = in_order(spectra)
    got, both_spectra = lax.optimization_barrier((trade(mixed), both_spectra))
    front, grad_pre = pl.pallas_call(
        middle_kernel,
        out_shape=(vmem(sent, f32), held(cells)),
        in_specs=[whole, stays, stays, whole, whole],
        out_specs=(whole, stays),
        scratch_shapes=[vmem(cells, f32), vmem(cells, f32), vmem(cells, f32), copies((3,))],
        compiler_params=params(),
        name="middle",
    )(*near(got), *far(local, packed), *near(*plane))
    got = trade(front)
    back, grad_spectra = across(got, True)
    both_grads = in_order(grad_spectra)
    got = trade(back)
    local_grad = pl.pallas_call(
        grads_kernel,
        out_shape=held(cells),
        in_specs=[whole, scalars],
        out_specs=whole,
        compiler_params=params(),
        name="local_grad",
    )(*far(grad_pre), channel_weight)
    spectral_grads = pl.pallas_call(
        outer_kernel,
        out_shape=held(spectral_weight.shape),
        grid=(channels // group,),
        in_specs=[whole] * 4,
        out_specs=pl.BlockSpec((2, group, channels, local_modes, modes), lambda i: (0, i, 0, 0, 0)),
        compiler_params=params(),
        name="outer",
    )(*far(*both_spectra), *near(*both_grads))
    cell_grad = pl.pallas_call(
        last_kernel,
        out_shape=held(sample_cells.shape),
        in_specs=[whole, stays, whole, whole],
        out_specs=stays,
        scratch_shapes=[vmem(cells, f32), vmem(sample_cells.shape, f32), copies, copies((channels // 4,))],
        compiler_params=params(),
        name="last",
    )(*near(got), *far(local_grad), *near(*plane))
    return (cell_grad[None], spectral_grads)


def solution(mesh):
    placed = (
        P("dp", None, "gx", "gy", None),
        P("dp", None, "gx", "gy", None),
        P(None, None, None, ("gx", "gy"), None),
        P(),
        P(),
    )

    def on_any(*args):
        _, channels, cells_x, cells_y, _ = args[0].shape
        owners = lax.axis_size("gx") * lax.axis_size("gy")
        fits = args[2].shape[3] == 8 and cells_x * cells_y == LANES // 4
        fits = fits and channels % 4 == 0 and owners % 4 == 0 and lax.axis_size("dp") == 2
        return on_tiles(*args) if fits else on_device(*args)

    return jax.shard_map(
        on_any,
        mesh=mesh,
        in_specs=placed,
        out_specs=(P("dp", None, "gx", "gy", None), P(None, None, None, ("gx", "gy"), None)),
        check_vma=False,
    )
```

```python
import math

import jax
import jax.numpy as jnp
import numpy as np
from jax import lax
from jax.experimental import pallas as pl
from jax.experimental.pallas import tpu as pltpu
from jax.sharding import PartitionSpec as P

NZ = 32
NT = 16
KX = 16
KY = 16
KZ = 16
KT = 8


highest = lax.Precision.HIGHEST


def gelu_slope(values):
    return (
        0.5 * (1.0 + lax.erf(values * 0.7071067811865476))
        + values * jnp.exp(-0.5 * values * values) * 0.3989422804014327
    )


def signed_freq(number, kept_count):
    return jnp.where(number < kept_count // 2, number, number - kept_count)


def line_table(length, kept_count):
    positions = jnp.arange(length, dtype=jnp.int32)
    frequency = signed_freq(jnp.arange(kept_count, dtype=jnp.int32), kept_count)
    phases = positions[:, None] * frequency[None, :] % length
    angles = phases.astype(jnp.float32) * (-2.0 * math.pi / length)
    return jnp.stack([jnp.cos(angles), jnp.sin(angles)]) / math.sqrt(length)


def block_table(length, kept_count):
    table = line_table(length, kept_count)
    upper = jnp.stack([table[0], table[1]], axis=1)
    lower = jnp.stack([-table[1], table[0]], axis=1)
    return jnp.stack([upper, lower]).reshape(2 * length, 2 * kept_count)


def plane_table(mode_index):
    row_index = jnp.arange(NZ * NT, dtype=jnp.int32)
    depth = row_index // NT
    time_step = row_index % NT
    depth_freq = signed_freq(mode_index // KT, KZ)
    time_freq = signed_freq(mode_index % KT, KT)
    fraction = (depth[:, None] * depth_freq[None, :] % NZ).astype(jnp.float32) / NZ
    fraction = fraction + (time_step[:, None] * time_freq[None, :] % NT).astype(jnp.float32) / NT
    angles = fraction * (-2.0 * math.pi)
    table = jnp.stack([jnp.cos(angles), jnp.sin(angles)]) / math.sqrt(NZ * NT)
    return jnp.moveaxis(table, 0, -1).reshape(NZ * NT, -1)


def line_forward(data, block):
    return jnp.einsum("mpr,pk->mkr", data, block, precision=highest)


def line_adjoint(data, block):
    return jnp.einsum("mkr,pk->mpr", data, block, precision=highest)


def plane_front(real_field, planar, form):
    coeffs = jnp.einsum("cxyn,nk->" + form, real_field, planar, precision=highest)
    return coeffs.reshape(KZ * KT, 2, -1)


def plane_back(stacked, planar, form, first_cells, second_cells, channels):
    rows = stacked.reshape(-1, first_cells, second_cells, channels)
    return jnp.einsum(form + ",nk->cxyn", rows, planar, precision=highest)


def swap_inner(data, first, second, channels):
    leading = data.shape[0]
    moved = jnp.transpose(data.reshape(leading, 2, first, second, channels), (0, 1, 3, 2, 4))
    return moved.reshape(leading, 2, -1)


def mode_mix(weight, spectrum):

    def single(left_arg, right_arg):
        return jnp.einsum("imn,iomn->omn", left_arg, right_arg, precision=highest)

    real_part = single(spectrum[0], weight[0]) - single(spectrum[1], weight[1])
    imag_part = single(spectrum[1], weight[0]) + single(spectrum[0], weight[1])
    return jnp.stack([real_part, imag_part])


def mode_unmix(weight, spectrum):

    def single(left_arg, right_arg):
        return jnp.einsum("omn,iomn->imn", left_arg, right_arg, precision=highest)

    real_part = single(spectrum[0], weight[0]) + single(spectrum[1], weight[1])
    imag_part = single(spectrum[1], weight[0]) - single(spectrum[0], weight[1])
    return jnp.stack([real_part, imag_part])


def mode_outer(grad_spectrum, spectrum):

    def single(left_arg, right_arg):
        return jnp.einsum("omn,imn->iomn", left_arg, right_arg, precision=highest)

    real_part = single(grad_spectrum[0], spectrum[0]) + single(grad_spectrum[1], spectrum[1])
    imag_part = single(grad_spectrum[1], spectrum[0]) - single(grad_spectrum[0], spectrum[1])
    return jnp.stack([real_part, imag_part])


def on_device(cell_values, cotangent, spectral_weight, channel_weight, channel_bias):
    sample_cells = cell_values[0]
    upstream = cotangent[0]
    count_x = lax.axis_size("gx")
    count_y = lax.axis_size("gy")
    channels, cells_x, cells_y, depth_time = sample_cells.shape
    length_x = count_x * cells_x
    length_y = count_y * cells_y
    local_modes = KZ * KT // (count_x * count_y)
    block_x = block_table(length_x, KX)
    block_y = block_table(length_y, KY)
    column = jnp.arange(KZ * KT, dtype=jnp.int32)

    def to_spectrum(last):
        shaped = jnp.transpose(last.reshape(local_modes, 2, KX, KY, channels), (1, 4, 0, 3, 2))
        return shaped.reshape(2, channels, local_modes, KY * KX)

    def from_spectrum(spectrum):
        shaped = spectrum.reshape(2, channels, local_modes, KY, KX)
        return jnp.transpose(shaped, (2, 0, 4, 3, 1)).reshape(local_modes, 2 * KX, KY * channels)

    planar = plane_table(column)

    def forward(real_field):
        gathered = lax.all_to_all(
            plane_front(real_field, planar, "kyxc"),
            ("gx", "gy"),
            split_axis=0,
            concat_axis=2,
            tiled=True,
        )
        arranged = gathered.reshape(local_modes, 2, count_x, count_y, cells_y, cells_x * channels)
        arranged = jnp.transpose(arranged, (0, 1, 3, 4, 2, 5)).reshape(
            local_modes, 2 * length_y, length_x * channels
        )
        along_y = line_forward(arranged, block_y)
        along_y = swap_inner(along_y, KY, length_x, channels).reshape(
            local_modes, 2 * length_x, KY * channels
        )
        along_x = line_forward(along_y, block_x)
        return to_spectrum(along_x)

    def inverse(spectrum):
        back_x = line_adjoint(from_spectrum(spectrum), block_x)
        back_x = swap_inner(back_x, length_x, KY, channels).reshape(
            local_modes, 2 * KY, length_x * channels
        )
        back_y = line_adjoint(back_x, block_y)
        ordered = back_y.reshape(local_modes, 2, count_y, cells_y, count_x, cells_x * channels)
        ordered = jnp.transpose(ordered, (0, 1, 4, 2, 3, 5)).reshape(local_modes, 2, -1)
        spread = lax.all_to_all(ordered, ("gx", "gy"), split_axis=2, concat_axis=0, tiled=True)
        return plane_back(spread, planar, "kyxc", cells_y, cells_x, channels)

    spectra = forward(sample_cells)
    mixed = mode_mix(spectral_weight, spectra)
    pre_act = jnp.einsum("oi,ixyn->oxyn", channel_weight, sample_cells, precision=highest)
    pre_act = pre_act + channel_bias[:, None, None, None] + inverse(mixed)
    grad_pre = upstream * gelu_slope(pre_act)
    grad_spectra = forward(grad_pre)
    back_modes = mode_unmix(spectral_weight, grad_spectra)
    cell_grad = jnp.einsum("oi,oxyn->ixyn", channel_weight, grad_pre, precision=highest) + inverse(
        back_modes
    )
    spectral_grads = lax.psum(mode_outer(grad_spectra, spectra), "dp")
    return (cell_grad[None], spectral_grads)


LANES = 128
VMEM_LIMIT = 24 * 1024 * 1024


def params():
    return pltpu.CompilerParams(vmem_limit_bytes=VMEM_LIMIT)


def halves(values):
    upper = values.astype(jnp.bfloat16)
    return upper, (values - upper.astype(jnp.float32)).astype(jnp.bfloat16)


def host_halves(table):
    upper = table.astype(jnp.bfloat16)
    lower = (table - upper.astype(np.float64)).astype(jnp.bfloat16)
    return upper, lower


def host_freq(number, kept_count):
    return np.where(number < kept_count // 2, number, number - kept_count)


def host_plane(owners, local_modes):
    mode = np.arange(owners * local_modes)
    cell = np.arange(NZ * NT)
    turns = np.outer(host_freq(mode // KT, KZ), cell // NT) / NZ
    turns = turns + np.outer(host_freq(mode % KT, KT), cell % NT) / NT
    angles = 2.0 * np.pi * turns
    table = np.stack([np.cos(angles), -np.sin(angles)]) / np.sqrt(NZ * NT)
    table = table.reshape(2, owners, local_modes, NZ * NT)
    return np.swapaxes(table, 0, 1).reshape(owners * 2 * local_modes, NZ * NT)


def host_cross(count_x, count_y, cells_x, cells_y):
    length_x = count_x * cells_x
    length_y = count_y * cells_y
    row = np.arange(length_x * length_y)
    cell = row % (cells_x * cells_y)
    owner = row // (cells_x * cells_y)
    place_x = owner // count_y * cells_x + cell // cells_y
    place_y = owner % count_y * cells_y + cell % cells_y
    mode = np.arange(KY * KX)
    turns = np.outer(place_x, host_freq(mode % KX, KX)) / length_x
    turns = turns + np.outer(place_y, host_freq(mode // KX, KY)) / length_y
    angles = 2.0 * np.pi * turns
    return np.concatenate([np.cos(angles), np.sin(angles)], axis=1) / np.sqrt(length_x * length_y)


def product(left, right, left_dim, right_dim):
    dims = (((left_dim,), (right_dim,)), ((), ()))

    def single(one, other):
        return lax.dot_general(one, other, dims, preferred_element_type=jnp.float32)

    return single(left[0], right[0]) + (single(left[0], right[1]) + single(left[1], right[0]))


def swap_groups(parts):
    width = LANES // 4
    lane = lax.broadcasted_iota(jnp.int32, parts[0].shape, 1)
    low_half = lane < 2 * width
    low_quarter = lane % (2 * width) < width

    def trade(one, other, mask, shift):
        return (
            jnp.where(mask, one, pltpu.roll(other, shift, 1)),
            jnp.where(mask, pltpu.roll(one, LANES - shift, 1), other),
        )

    first, third = trade(parts[0], parts[2], low_half, 2 * width)
    second, fourth = trade(parts[1], parts[3], low_half, 2 * width)
    first, second = trade(first, second, low_quarter, width)
    third, fourth = trade(third, fourth, low_quarter, width)
    return first, second, third, fourth


def pack_rows(field_ref, rows_ref):
    channels, cells_x, cells_y, _ = field_ref.shape
    for channel in range(channels):
        for place in range(cells_x):
            row = (channel * cells_x + place) * cells_y
            rows_ref[row : row + cells_y, :] = field_ref[channel, place]


def start(source, target, semaphore):
    copy = pltpu.make_async_copy(source, target, semaphore)
    copy.start()
    return copy


def spans_of(channels, step):
    return [(first, min(first + step, channels)) for first in range(0, channels, step)]


def front_kernel(field_hbm, high_hbm, low_hbm, out_ref, field_ref, high_ref, low_ref, rows_ref, table_sems, field_sems):
    channels, cells_x, cells_y, _ = field_ref.shape
    cells = cells_x * cells_y
    pieces = []
    for first, last in spans_of(channels, 4):
        span = pl.ds(first, last - first)
        pieces.append(start(field_hbm.at[span], field_ref.at[span], field_sems.at[len(pieces)]))
        if first == 0:
            tables = [start(high_hbm, high_ref, table_sems.at[0]), start(low_hbm, low_ref, table_sems.at[1])]
    for piece, (first, last) in enumerate(spans_of(channels, 4)):
        pieces[piece].wait()
        for channel in range(first, last):
            for place in range(cells_x):
                row = channel * cells + place * cells_y
                rows_ref[row : row + cells_y, :] = field_ref[channel, place]
    for copy in tables:
        copy.wait()
    out_ref[...] = product((high_ref[...], low_ref[...]), halves(rows_ref[...]), 1, 1)


def mode_kernel(
    conjugate,
    got_ref,
    weight_hbm,
    high_ref,
    low_ref,
    out_hbm,
    spectra_hbm,
    weight_ref,
    out_ref,
    spectra_ref,
    field_ref,
    mixed_ref,
    weight_sems,
    spectra_sem,
    out_sems,
):
    _, channels, local_modes, modes = spectra_ref.shape
    chunk = channels // weight_sems.shape[0]
    weight_copies = []
    for k in range(weight_sems.shape[0]):
        span = pl.ds(k * chunk, chunk)
        place = (slice(None), span) if conjugate else (slice(None), slice(None), span)
        weight_copies.append(start(weight_hbm.at[place], weight_ref.at[place], weight_sems.at[k]))
    rows = channels * local_modes
    cells = high_ref.shape[0]
    owners = got_ref.shape[0] // (2 * local_modes)
    block = 2 * local_modes
    table = (high_ref[...], low_ref[...])
    for quad in range(owners // 4):
        for group in range(channels // 4):
            parts = [
                got_ref[(4 * quad + j) * block : (4 * quad + j + 1) * block, group * LANES : (group + 1) * LANES]
                for j in range(4)
            ]
            for m, part in enumerate(swap_groups(parts)):
                row = (4 * group + m) * local_modes
                for side in range(2):
                    field_ref[side * rows + row : side * rows + row + local_modes, quad * LANES : (quad + 1) * LANES] = part[
                        side * local_modes : (side + 1) * local_modes
                    ]
    waves = product(halves(field_ref[...]), table, 1, 0)
    real = waves[:rows, :modes] + waves[rows:, modes:]
    imag = waves[rows:, :modes] - waves[:rows, modes:]
    spectra_ref[0] = real.reshape(channels, local_modes, modes)
    spectra_ref[1] = imag.reshape(channels, local_modes, modes)
    spectra_copy = start(spectra_ref, spectra_hbm, spectra_sem)
    for part in range(len(weight_copies) * modes // LANES):
        first_lane = part % (modes // LANES) * LANES
        first_result = part // (modes // LANES) * chunk
        span = slice(first_lane, first_lane + LANES)
        ins = [(spectra_ref[0, c, :, span], spectra_ref[1, c, :, span]) for c in range(channels)]
        if first_lane == 0:
            weight_copies[part // (modes // LANES)].wait()

        def one(step, carry, span=span, ins=ins, first_lane=first_lane, first_result=first_result):
            result = first_result + step
            total_real = jnp.zeros((local_modes, LANES), jnp.float32)
            total_imag = jnp.zeros((local_modes, LANES), jnp.float32)
            for c, (in_real, in_imag) in enumerate(ins):
                if conjugate:
                    w_real = weight_ref[0, result, c, :, span]
                    w_imag = weight_ref[1, result, c, :, span]
                    total_real = total_real + (in_real * w_real + in_imag * w_imag)
                    total_imag = total_imag + (in_imag * w_real - in_real * w_imag)
                else:
                    w_real = weight_ref[0, c, result, :, span]
                    w_imag = weight_ref[1, c, result, :, span]
                    total_real = total_real + (in_real * w_real - in_imag * w_imag)
                    total_imag = total_imag + (in_imag * w_real + in_real * w_imag)
            row = pl.multiple_of(result * local_modes, local_modes)
            other = pl.multiple_of(rows + result * local_modes, local_modes)
            mixed_ref[pl.ds(row, local_modes), first_lane : first_lane + LANES] = total_real
            mixed_ref[pl.ds(other, local_modes), first_lane : first_lane + LANES] = total_imag
            mixed_ref[pl.ds(row, local_modes), modes + first_lane : modes + first_lane + LANES] = -total_imag
            mixed_ref[pl.ds(other, local_modes), modes + first_lane : modes + first_lane + LANES] = total_real
            return carry

        lax.fori_loop(0, chunk, one, 0, unroll=True)
    mixed = halves(mixed_ref[...])
    out_copies = []
    for quad in range(owners // 4):
        if quad % 2 == 0:
            span = slice(quad * LANES, min(quad + 2, owners // 4) * LANES)
            field_ref[:, span] = product(mixed, (high_ref[span, :], low_ref[span, :]), 1, 1)
        for group in range(channels // 4):
            for side in range(2):
                first = side * rows + 4 * group * local_modes
                parts = [
                    field_ref[first + m * local_modes : first + (m + 1) * local_modes, quad * LANES : (quad + 1) * LANES]
                    for m in range(4)
                ]
                for j, part in enumerate(swap_groups(parts)):
                    row = (4 * quad + j) * block + side * local_modes
                    out_ref[row : row + local_modes, group * LANES : (group + 1) * LANES] = part
        span = pl.ds(4 * quad * block, 4 * block)
        out_copies.append(start(out_ref.at[span], out_hbm.at[span], out_sems.at[quad]))
    spectra_copy.wait()
    for copy in out_copies:
        copy.wait()


def channel_sums(transposed, rows_ref, weight_ref, bias_ref, out_ref, channels):
    height = rows_ref.shape[0] // channels
    for lane in range(0, rows_ref.shape[1], LANES):
        span = slice(lane, lane + LANES)

        def one(step, carry, span=span):
            ins = [rows_ref[pl.ds(pl.multiple_of(i * height + step * 8, 8), 8), span] for i in range(channels)]
            for o in range(channels):
                total = None
                for i in range(channels):
                    factor = weight_ref[i, o] if transposed else weight_ref[o, i]
                    term = ins[i] * factor
                    total = term if total is None else total + term
                if bias_ref is not None:
                    total = total + bias_ref[o]
                out_ref[pl.ds(pl.multiple_of(o * height + step * 8, 8), 8), span] = total
            return carry

        lax.fori_loop(0, height // 8, one, 0)


def local_kernel(field_ref, upstream_ref, weight_ref, bias_ref, out_ref, packed_ref, rows_ref):
    pack_rows(field_ref, rows_ref)
    pack_rows(upstream_ref, packed_ref)
    channel_sums(False, rows_ref, weight_ref, bias_ref, out_ref, field_ref.shape[0])


def middle_kernel(got_ref, local_hbm, upstream_hbm, high_ref, low_ref, out_ref, grad_ref, local_ref, upstream_ref, sems):
    spans = [pl.ds(first, last - first) for first, last in spans_of(local_ref.shape[0], 128)]
    copies = [
        (start(local_hbm.at[span], local_ref.at[span], sems.at[0, k]), start(upstream_hbm.at[span], upstream_ref.at[span], sems.at[1, k]))
        for k, span in enumerate(spans)
    ]
    table = (high_ref[...], low_ref[...])
    grad_ref[...] = product(halves(got_ref[...]), table, 0, 0)
    for k, span in enumerate(spans):
        rows = slice(span.start, span.start + span.size)
        for copy in copies[k]:
            copy.wait()
        grad_ref[rows, :] = upstream_ref[rows, :] * gelu_slope(grad_ref[rows, :] + local_ref[rows, :])
    out_ref[...] = product(table, halves(grad_ref[...]), 1, 1)


def grads_kernel(rows_ref, weight_ref, out_ref):
    channel_sums(True, rows_ref, weight_ref, None, out_ref, weight_ref.shape[0])


def last_kernel(got_ref, local_ref, high_ref, low_ref, out_hbm, rows_ref, out_ref, sems):
    channels, cells_x, cells_y, _ = out_ref.shape
    cells = cells_x * cells_y
    rows_ref[...] = product(halves(got_ref[...]), (high_ref[...], low_ref[...]), 0, 0)
    leaving = []
    for first, last in spans_of(channels, 4):
        rows = slice(first * cells, last * cells)
        rows_ref[rows, :] = rows_ref[rows, :] + local_ref[rows, :]
        for channel in range(first, last):
            for place in range(cells_x):
                row = channel * cells + place * cells_y
                out_ref[channel, place] = rows_ref[row : row + cells_y, :]
        span = pl.ds(first, last - first)
        leaving.append(start(out_ref.at[span], out_hbm.at[span], sems.at[len(leaving)]))
    for copy in leaving:
        copy.wait()


def outer_kernel(first_spectra, second_spectra, first_grads, second_grads, out_ref):
    _, channels, local_modes, modes = first_spectra.shape
    sources = out_ref.shape[1]
    pairs = ((first_spectra, first_grads), (second_spectra, second_grads))

    def one(step, carry):
        source = pl.program_id(0) * sources + step
        for lane in range(0, modes, LANES):
            span = slice(lane, lane + LANES)
            ins = [(spectra[0, source, :, span], spectra[1, source, :, span]) for spectra, _ in pairs]
            for o in range(channels):
                total_real = None
                total_imag = None
                for (_, grads), (in_real, in_imag) in zip(pairs, ins):
                    g_real = grads[0, o, :, span]
                    g_imag = grads[1, o, :, span]
                    real = g_real * in_real + g_imag * in_imag
                    imag = g_imag * in_real - g_real * in_imag
                    total_real = real if total_real is None else total_real + real
                    total_imag = imag if total_imag is None else total_imag + imag
                out_ref[0, step, o, :, span] = total_real
                out_ref[1, step, o, :, span] = total_imag
        return carry

    lax.fori_loop(0, sources, one, 0)


def in_order(own):
    other = lax.ppermute(own, "dp", [(0, 1), (1, 0)])
    first = lax.axis_index("dp") == 0
    return jnp.where(first, own, other), jnp.where(first, other, own)


def far(*values):
    return [pltpu.with_memory_space_constraint(v, pltpu.HBM) for v in values]


def near(*values):
    return [pltpu.with_memory_space_constraint(v, pltpu.VMEM) for v in values]


def on_tiles(cell_values, cotangent, spectral_weight, channel_weight, channel_bias):
    sample_cells = cell_values[0]
    upstream = cotangent[0]
    count_x = lax.axis_size("gx")
    count_y = lax.axis_size("gy")
    owners = count_x * count_y
    channels, cells_x, cells_y, depth_time = sample_cells.shape
    local_modes = spectral_weight.shape[3]
    modes = spectral_weight.shape[4]
    rows = channels * cells_x * cells_y
    plane = [jnp.asarray(t) for t in host_halves(host_plane(owners, local_modes))]
    cross = [jnp.asarray(t) for t in host_halves(host_cross(count_x, count_y, cells_x, cells_y))]
    f32 = jnp.float32
    bf16 = jnp.bfloat16
    whole = pl.BlockSpec(memory_space=pltpu.VMEM)
    scalars = pl.BlockSpec(memory_space=pltpu.SMEM)
    stays = pl.BlockSpec(memory_space=pltpu.HBM)
    copies = pltpu.SemaphoreType.DMA
    vmem = pltpu.VMEM
    sent = (owners * 2 * local_modes, rows)
    cells = (rows, depth_time)
    spectrum = (2, channels, local_modes, modes)
    group = next(g for g in (4, 2, 1) if channels % g == 0)

    def held(shape):
        return pltpu.HBM(shape, f32)

    def trade(values):
        return lax.all_to_all(values, ("gx", "gy"), split_axis=0, concat_axis=0, tiled=True)

    def across(values, conjugate):
        def body(*refs):
            mode_kernel(conjugate, *refs)

        return pl.pallas_call(
            body,
            out_shape=(held(sent), held(spectrum)),
            in_specs=[whole, stays, whole, whole],
            out_specs=(stays, stays),
            scratch_shapes=[
                vmem(spectral_weight.shape, f32),
                vmem(sent, f32),
                vmem(spectrum, f32),
                vmem((2 * channels * local_modes, owners * cells_x * cells_y), f32),
                vmem((2 * channels * local_modes, 2 * modes), f32),
                copies((4,)),
                copies,
                copies((owners // 4,)),
            ],
            compiler_params=params(),
            name="unmix_modes" if conjugate else "mix_modes",
        )(*near(values), *far(spectral_weight), *near(*cross))

    front = pl.pallas_call(
        front_kernel,
        out_shape=vmem(sent, f32),
        in_specs=[stays] * 3,
        out_specs=whole,
        scratch_shapes=[
            vmem(sample_cells.shape, f32),
            vmem(plane[0].shape, bf16),
            vmem(plane[1].shape, bf16),
            vmem(cells, f32),
            copies((2,)),
            copies((-(-channels // 4),)),
        ],
        compiler_params=params(),
        name="front",
    )(*far(sample_cells, *plane))
    got = trade(front)
    local, packed = pl.pallas_call(
        local_kernel,
        out_shape=(held(cells), held(cells)),
        in_specs=[whole, whole, scalars, scalars],
        out_specs=(whole, whole),
        scratch_shapes=[vmem(cells, f32)],
        compiler_params=params(),
        name="local_pre",
    )(*far(sample_cells, upstream), channel_weight, channel_bias)
    mixed, spectra = across(got, False)
    both_spectra = in_order(spectra)
    got, both_spectra = lax.optimization_barrier((trade(mixed), both_spectra))
    front, grad_pre = pl.pallas_call(
        middle_kernel,
        out_shape=(vmem(sent, f32), vmem(cells, f32)),
        in_specs=[whole, stays, stays, whole, whole],
        out_specs=(whole, whole),
        scratch_shapes=[vmem(cells, f32), vmem(cells, f32), copies((2, -(-rows // 128)))],
        compiler_params=params(),
        name="middle",
    )(*near(got), *far(local, packed), *near(*plane))
    got = trade(front)
    back, grad_spectra = across(got, True)
    both_grads = in_order(grad_spectra)
    got = trade(back)
    local_grad = pl.pallas_call(
        grads_kernel,
        out_shape=held(cells),
        in_specs=[whole, scalars],
        out_specs=whole,
        compiler_params=params(),
        name="local_grad",
    )(*far(grad_pre), channel_weight)
    spectral_grads = pl.pallas_call(
        outer_kernel,
        out_shape=held(spectral_weight.shape),
        grid=(channels // group,),
        in_specs=[whole] * 4,
        out_specs=pl.BlockSpec((2, group, channels, local_modes, modes), lambda i: (0, i, 0, 0, 0)),
        compiler_params=params(),
        name="outer",
    )(*far(*both_spectra), *near(*both_grads))
    cell_grad = pl.pallas_call(
        last_kernel,
        out_shape=held(sample_cells.shape),
        in_specs=[whole] * 4,
        out_specs=stays,
        scratch_shapes=[vmem(cells, f32), vmem(sample_cells.shape, f32), copies((-(-channels // 4),))],
        compiler_params=params(),
        name="last",
    )(*near(got, local_grad, *plane))
    return (cell_grad[None], spectral_grads)


def solution(mesh):
    placed = (
        P("dp", None, "gx", "gy", None),
        P("dp", None, "gx", "gy", None),
        P(None, None, None, ("gx", "gy"), None),
        P(),
        P(),
    )

    def on_any(*args):
        _, channels, cells_x, cells_y, _ = args[0].shape
        owners = lax.axis_size("gx") * lax.axis_size("gy")
        fits = args[2].shape[3] == 8 and cells_x * cells_y == LANES // 4
        fits = fits and channels % 4 == 0 and owners % 4 == 0 and lax.axis_size("dp") == 2
        return on_tiles(*args) if fits else on_device(*args)

    return jax.shard_map(
        on_any,
        mesh=mesh,
        in_specs=placed,
        out_specs=(P("dp", None, "gx", "gy", None), P(None, None, None, ("gx", "gy"), None)),
        check_vma=False,
    )
```

```python
import math

import jax
import jax.numpy as jnp
import numpy as np
from jax import lax
from jax.experimental import pallas as pl
from jax.experimental.pallas import tpu as pltpu
from jax.sharding import PartitionSpec as P

NZ = 32
NT = 16
KX = 16
KY = 16
KZ = 16
KT = 8


highest = lax.Precision.HIGHEST


def gelu_slope(values):
    return (
        0.5 * (1.0 + lax.erf(values * 0.7071067811865476))
        + values * jnp.exp(-0.5 * values * values) * 0.3989422804014327
    )


def signed_freq(number, kept_count):
    return jnp.where(number < kept_count // 2, number, number - kept_count)


def line_table(length, kept_count):
    positions = jnp.arange(length, dtype=jnp.int32)
    frequency = signed_freq(jnp.arange(kept_count, dtype=jnp.int32), kept_count)
    phases = positions[:, None] * frequency[None, :] % length
    angles = phases.astype(jnp.float32) * (-2.0 * math.pi / length)
    return jnp.stack([jnp.cos(angles), jnp.sin(angles)]) / math.sqrt(length)


def block_table(length, kept_count):
    table = line_table(length, kept_count)
    upper = jnp.stack([table[0], table[1]], axis=1)
    lower = jnp.stack([-table[1], table[0]], axis=1)
    return jnp.stack([upper, lower]).reshape(2 * length, 2 * kept_count)


def plane_table(mode_index):
    row_index = jnp.arange(NZ * NT, dtype=jnp.int32)
    depth = row_index // NT
    time_step = row_index % NT
    depth_freq = signed_freq(mode_index // KT, KZ)
    time_freq = signed_freq(mode_index % KT, KT)
    fraction = (depth[:, None] * depth_freq[None, :] % NZ).astype(jnp.float32) / NZ
    fraction = fraction + (time_step[:, None] * time_freq[None, :] % NT).astype(jnp.float32) / NT
    angles = fraction * (-2.0 * math.pi)
    table = jnp.stack([jnp.cos(angles), jnp.sin(angles)]) / math.sqrt(NZ * NT)
    return jnp.moveaxis(table, 0, -1).reshape(NZ * NT, -1)


def line_forward(data, block):
    return jnp.einsum("mpr,pk->mkr", data, block, precision=highest)


def line_adjoint(data, block):
    return jnp.einsum("mkr,pk->mpr", data, block, precision=highest)


def plane_front(real_field, planar, form):
    coeffs = jnp.einsum("cxyn,nk->" + form, real_field, planar, precision=highest)
    return coeffs.reshape(KZ * KT, 2, -1)


def plane_back(stacked, planar, form, first_cells, second_cells, channels):
    rows = stacked.reshape(-1, first_cells, second_cells, channels)
    return jnp.einsum(form + ",nk->cxyn", rows, planar, precision=highest)


def swap_inner(data, first, second, channels):
    leading = data.shape[0]
    moved = jnp.transpose(data.reshape(leading, 2, first, second, channels), (0, 1, 3, 2, 4))
    return moved.reshape(leading, 2, -1)


def mode_mix(weight, spectrum):

    def single(left_arg, right_arg):
        return jnp.einsum("imn,iomn->omn", left_arg, right_arg, precision=highest)

    real_part = single(spectrum[0], weight[0]) - single(spectrum[1], weight[1])
    imag_part = single(spectrum[1], weight[0]) + single(spectrum[0], weight[1])
    return jnp.stack([real_part, imag_part])


def mode_unmix(weight, spectrum):

    def single(left_arg, right_arg):
        return jnp.einsum("omn,iomn->imn", left_arg, right_arg, precision=highest)

    real_part = single(spectrum[0], weight[0]) + single(spectrum[1], weight[1])
    imag_part = single(spectrum[1], weight[0]) - single(spectrum[0], weight[1])
    return jnp.stack([real_part, imag_part])


def mode_outer(grad_spectrum, spectrum):

    def single(left_arg, right_arg):
        return jnp.einsum("omn,imn->iomn", left_arg, right_arg, precision=highest)

    real_part = single(grad_spectrum[0], spectrum[0]) + single(grad_spectrum[1], spectrum[1])
    imag_part = single(grad_spectrum[1], spectrum[0]) - single(grad_spectrum[0], spectrum[1])
    return jnp.stack([real_part, imag_part])


def on_device(cell_values, cotangent, spectral_weight, channel_weight, channel_bias):
    sample_cells = cell_values[0]
    upstream = cotangent[0]
    count_x = lax.axis_size("gx")
    count_y = lax.axis_size("gy")
    channels, cells_x, cells_y, depth_time = sample_cells.shape
    length_x = count_x * cells_x
    length_y = count_y * cells_y
    local_modes = KZ * KT // (count_x * count_y)
    block_x = block_table(length_x, KX)
    block_y = block_table(length_y, KY)
    column = jnp.arange(KZ * KT, dtype=jnp.int32)

    def to_spectrum(last):
        shaped = jnp.transpose(last.reshape(local_modes, 2, KX, KY, channels), (1, 4, 0, 3, 2))
        return shaped.reshape(2, channels, local_modes, KY * KX)

    def from_spectrum(spectrum):
        shaped = spectrum.reshape(2, channels, local_modes, KY, KX)
        return jnp.transpose(shaped, (2, 0, 4, 3, 1)).reshape(local_modes, 2 * KX, KY * channels)

    planar = plane_table(column)

    def forward(real_field):
        gathered = lax.all_to_all(
            plane_front(real_field, planar, "kyxc"),
            ("gx", "gy"),
            split_axis=0,
            concat_axis=2,
            tiled=True,
        )
        arranged = gathered.reshape(local_modes, 2, count_x, count_y, cells_y, cells_x * channels)
        arranged = jnp.transpose(arranged, (0, 1, 3, 4, 2, 5)).reshape(
            local_modes, 2 * length_y, length_x * channels
        )
        along_y = line_forward(arranged, block_y)
        along_y = swap_inner(along_y, KY, length_x, channels).reshape(
            local_modes, 2 * length_x, KY * channels
        )
        along_x = line_forward(along_y, block_x)
        return to_spectrum(along_x)

    def inverse(spectrum):
        back_x = line_adjoint(from_spectrum(spectrum), block_x)
        back_x = swap_inner(back_x, length_x, KY, channels).reshape(
            local_modes, 2 * KY, length_x * channels
        )
        back_y = line_adjoint(back_x, block_y)
        ordered = back_y.reshape(local_modes, 2, count_y, cells_y, count_x, cells_x * channels)
        ordered = jnp.transpose(ordered, (0, 1, 4, 2, 3, 5)).reshape(local_modes, 2, -1)
        spread = lax.all_to_all(ordered, ("gx", "gy"), split_axis=2, concat_axis=0, tiled=True)
        return plane_back(spread, planar, "kyxc", cells_y, cells_x, channels)

    spectra = forward(sample_cells)
    mixed = mode_mix(spectral_weight, spectra)
    pre_act = jnp.einsum("oi,ixyn->oxyn", channel_weight, sample_cells, precision=highest)
    pre_act = pre_act + channel_bias[:, None, None, None] + inverse(mixed)
    grad_pre = upstream * gelu_slope(pre_act)
    grad_spectra = forward(grad_pre)
    back_modes = mode_unmix(spectral_weight, grad_spectra)
    cell_grad = jnp.einsum("oi,oxyn->ixyn", channel_weight, grad_pre, precision=highest) + inverse(
        back_modes
    )
    spectral_grads = lax.psum(mode_outer(grad_spectra, spectra), "dp")
    return (cell_grad[None], spectral_grads)


LANES = 128
VMEM_LIMIT = 24 * 1024 * 1024


def params():
    return pltpu.CompilerParams(vmem_limit_bytes=VMEM_LIMIT)


def halves(values):
    upper = values.astype(jnp.bfloat16)
    return upper, (values - upper.astype(jnp.float32)).astype(jnp.bfloat16)


def host_halves(table):
    upper = table.astype(jnp.bfloat16)
    lower = (table - upper.astype(np.float64)).astype(jnp.bfloat16)
    return upper, lower


def host_freq(number, kept_count):
    return np.where(number < kept_count // 2, number, number - kept_count)


def host_plane(owners, local_modes):
    mode = np.arange(owners * local_modes)
    cell = np.arange(NZ * NT)
    turns = np.outer(host_freq(mode // KT, KZ), cell // NT) / NZ
    turns = turns + np.outer(host_freq(mode % KT, KT), cell % NT) / NT
    angles = 2.0 * np.pi * turns
    table = np.stack([np.cos(angles), -np.sin(angles)]) / np.sqrt(NZ * NT)
    table = table.reshape(2, owners, local_modes, NZ * NT)
    return np.swapaxes(table, 0, 1).reshape(owners * 2 * local_modes, NZ * NT)


def host_cross(count_x, count_y, cells_x, cells_y):
    length_x = count_x * cells_x
    length_y = count_y * cells_y
    row = np.arange(length_x * length_y // 2)
    cell = row % (cells_x * cells_y)
    owner = row // (cells_x * cells_y)
    place_x = owner // (count_y // 2) * cells_x + cell // cells_y
    place_y = owner % (count_y // 2) * cells_y + cell % cells_y
    column = np.arange(KY // 2 * KX)
    number_x = column % KX
    block = column // KX
    tables = []
    for number_y in (np.where(block % 2 == 0, block, block + 7), np.where(block % 2 == 1, block, block + 9)):
        turns = np.outer(place_x, host_freq(number_x, KX)) / length_x
        turns = turns + np.outer(place_y, host_freq(number_y, KY)) / length_y
        angles = 2.0 * np.pi * turns
        tables.append(np.concatenate([np.cos(angles), np.sin(angles)], axis=1))
    return np.stack(tables) / np.sqrt(length_x * length_y)


def product(left, right, left_dim, right_dim):
    dims = (((left_dim,), (right_dim,)), ((), ()))

    def single(one, other):
        return lax.dot_general(one, other, dims, preferred_element_type=jnp.float32)

    return single(left[0], right[0]) + (single(left[0], right[1]) + single(left[1], right[0]))


def swap_groups(parts):
    width = LANES // 4
    lane = lax.broadcasted_iota(jnp.int32, parts[0].shape, 1)
    low_half = lane < 2 * width
    low_quarter = lane % (2 * width) < width

    def trade(one, other, mask, shift):
        return (
            jnp.where(mask, one, pltpu.roll(other, shift, 1)),
            jnp.where(mask, pltpu.roll(one, LANES - shift, 1), other),
        )

    first, third = trade(parts[0], parts[2], low_half, 2 * width)
    second, fourth = trade(parts[1], parts[3], low_half, 2 * width)
    first, second = trade(first, second, low_quarter, width)
    third, fourth = trade(third, fourth, low_quarter, width)
    return first, second, third, fourth


def pack_rows(field_ref, rows_ref):
    channels, cells_x, cells_y, _ = field_ref.shape
    for channel in range(channels):
        for place in range(cells_x):
            row = (channel * cells_x + place) * cells_y
            rows_ref[row : row + cells_y, :] = field_ref[channel, place]


def start(source, target, semaphore):
    copy = pltpu.make_async_copy(source, target, semaphore)
    copy.start()
    return copy


def spans_of(channels, step):
    return [(first, min(first + step, channels)) for first in range(0, channels, step)]


def front_kernel(field_hbm, high_hbm, low_hbm, out_ref, field_ref, high_ref, low_ref, rows_ref, table_sems, field_sems):
    channels, cells_x, cells_y, _ = field_ref.shape
    cells = cells_x * cells_y
    pieces = []
    for first, last in spans_of(channels, 4):
        span = pl.ds(first, last - first)
        pieces.append(start(field_hbm.at[span], field_ref.at[span], field_sems.at[len(pieces)]))
        if first == 0:
            tables = [start(high_hbm, high_ref, table_sems.at[0]), start(low_hbm, low_ref, table_sems.at[1])]
    for piece, (first, last) in enumerate(spans_of(channels, 4)):
        pieces[piece].wait()
        for channel in range(first, last):
            for place in range(cells_x):
                row = channel * cells + place * cells_y
                rows_ref[row : row + cells_y, :] = field_ref[channel, place]
    for copy in tables:
        copy.wait()
    out_ref[...] = product((high_ref[...], low_ref[...]), halves(rows_ref[...]), 1, 1)


def blocks_even(shape):
    return lax.broadcasted_iota(jnp.int32, shape, 1) // KX % 2 == 0


def in_ky_order(even, odd):
    mask = blocks_even(even.shape)
    low = jnp.where(mask, even, odd)
    high = jnp.where(mask, pltpu.roll(even, LANES - KX, 1), pltpu.roll(odd, KX, 1))
    return low, high


def by_ky_parity(low, high):
    mask = blocks_even(low.shape)
    even = jnp.where(mask, low, pltpu.roll(high, KX, 1))
    odd = jnp.where(mask, pltpu.roll(high, LANES - KX, 1), low)
    return even, odd


def mode_kernel(
    conjugate,
    got_ref,
    weight_hbm,
    high_ref,
    low_ref,
    out_hbm,
    spectra_hbm,
    weight_ref,
    out_ref,
    spectra_ref,
    field_ref,
    mixed_ref,
    weight_sems,
    spectra_sem,
    out_sems,
):
    _, channels, local_modes, modes = spectra_ref.shape
    chunk = channels // weight_sems.shape[0]
    weight_copies = []
    for k in range(weight_sems.shape[0]):
        span = pl.ds(k * chunk, chunk)
        place = (slice(None), span) if conjugate else (slice(None), slice(None), span)
        weight_copies.append(start(weight_hbm.at[place], weight_ref.at[place], weight_sems.at[k]))
    rows = channels * local_modes
    block = 2 * local_modes
    quads = got_ref.shape[0] // (4 * block)
    groups = channels // 4

    def owner_rows(quad, j):
        return slice((4 * quad + j) * block, (4 * quad + j + 1) * block)

    for pair in range(quads // 2):
        for group in range(groups):
            lanes = slice(group * LANES, (group + 1) * LANES)
            near_half, far_half = [
                [got_ref[owner_rows(2 * pair + i, 2 * half + j), lanes] for i in range(2) for j in range(2)] for half in range(2)
            ]
            sums = [one + other for one, other in zip(near_half, far_half)]
            gaps = [one - other for one, other in zip(near_half, far_half)]
            for parity, parts in enumerate((sums, gaps)):
                for m, part in enumerate(swap_groups(parts)):
                    row = (4 * group + m) * local_modes
                    for side in range(2):
                        field_ref[
                            parity, side * rows + row : side * rows + row + local_modes, pair * LANES : (pair + 1) * LANES
                        ] = part[side * local_modes : (side + 1) * local_modes]
    real = []
    imag = []
    for parity in range(2):
        waves = product(halves(field_ref[parity]), (high_ref[parity], low_ref[parity]), 1, 0)
        real.append(waves[:rows, :LANES] + waves[rows:, LANES:])
        imag.append(waves[rows:, :LANES] - waves[:rows, LANES:])
    for part, pair in enumerate((real, imag)):
        for k, values in enumerate(in_ky_order(*pair)):
            spectra_ref[part, :, :, k * LANES : (k + 1) * LANES] = values.reshape(channels, local_modes, LANES)
    spectra_copy = start(spectra_ref, spectra_hbm, spectra_sem)
    for part in range(len(weight_copies) * 2):
        first_lane = part % 2 * LANES
        first_result = part // 2 * chunk
        span = slice(first_lane, first_lane + LANES)
        ins = [(spectra_ref[0, c, :, span], spectra_ref[1, c, :, span]) for c in range(channels)]
        if first_lane == 0:
            weight_copies[part // 2].wait()

        def one(step, carry, span=span, ins=ins, first_result=first_result):
            result = first_result + step
            total_real = jnp.zeros((local_modes, LANES), jnp.float32)
            total_imag = jnp.zeros((local_modes, LANES), jnp.float32)
            for c, (in_real, in_imag) in enumerate(ins):
                if conjugate:
                    w_real = weight_ref[0, result, c, :, span]
                    w_imag = weight_ref[1, result, c, :, span]
                    total_real = total_real + (in_real * w_real + in_imag * w_imag)
                    total_imag = total_imag + (in_imag * w_real - in_real * w_imag)
                else:
                    w_real = weight_ref[0, c, result, :, span]
                    w_imag = weight_ref[1, c, result, :, span]
                    total_real = total_real + (in_real * w_real - in_imag * w_imag)
                    total_imag = total_imag + (in_imag * w_real + in_real * w_imag)
            row = pl.multiple_of(result * local_modes, local_modes)
            mixed_ref[0, pl.ds(row, local_modes), span] = total_real
            mixed_ref[1, pl.ds(row, local_modes), span] = total_imag
            return carry

        lax.fori_loop(0, chunk, one, 0, unroll=True)
    out_copies = []
    for first, last in spans_of(groups, -(-groups // 2)):
        begin, end = 4 * first * local_modes, 4 * last * local_modes
        reals = by_ky_parity(mixed_ref[0, begin:end, :LANES], mixed_ref[0, begin:end, LANES:])
        imags = by_ky_parity(mixed_ref[1, begin:end, :LANES], mixed_ref[1, begin:end, LANES:])
        for parity in range(2):
            left = jnp.concatenate([reals[parity], imags[parity]], axis=0)
            right = jnp.concatenate([-imags[parity], reals[parity]], axis=0)
            both = halves(jnp.concatenate([left, right], axis=1))
            field_ref[parity, 2 * begin : 2 * end, :] = product(both, (high_ref[parity], low_ref[parity]), 1, 1)
        for pair in range(quads // 2):
            for group in range(first, last):
                lanes = slice(group * LANES, (group + 1) * LANES)
                for side in range(2):
                    base = 2 * begin + side * (end - begin) + 4 * (group - first) * local_modes
                    sums, gaps = [
                        swap_groups(
                            [
                                field_ref[
                                    parity,
                                    base + m * local_modes : base + (m + 1) * local_modes,
                                    pair * LANES : (pair + 1) * LANES,
                                ]
                                for m in range(4)
                            ]
                        )
                        for parity in range(2)
                    ]
                    for k in range(4):
                        row = (4 * (2 * pair + k // 2) + k % 2) * block + side * local_modes
                        other = row + 2 * block
                        out_ref[row : row + local_modes, lanes] = sums[k] + gaps[k]
                        out_ref[other : other + local_modes, lanes] = sums[k] - gaps[k]
        place = (slice(None), pl.ds(first * LANES, (last - first) * LANES))
        out_copies.append(start(out_ref.at[place], out_hbm.at[place], out_sems.at[len(out_copies)]))
    spectra_copy.wait()
    for copy in out_copies:
        copy.wait()


def channel_sums(transposed, rows_ref, weight_ref, bias_ref, out_ref, channels):
    height = rows_ref.shape[0] // channels
    for lane in range(0, rows_ref.shape[1], LANES):
        span = slice(lane, lane + LANES)

        def one(step, carry, span=span):
            ins = [rows_ref[pl.ds(pl.multiple_of(i * height + step * 8, 8), 8), span] for i in range(channels)]
            for o in range(channels):
                total = None
                for i in range(channels):
                    factor = weight_ref[i, o] if transposed else weight_ref[o, i]
                    term = ins[i] * factor
                    total = term if total is None else total + term
                if bias_ref is not None:
                    total = total + bias_ref[o]
                out_ref[pl.ds(pl.multiple_of(o * height + step * 8, 8), 8), span] = total
            return carry

        lax.fori_loop(0, height // 8, one, 0)


def local_kernel(field_ref, upstream_ref, weight_ref, bias_ref, out_ref, packed_ref, rows_ref):
    pack_rows(field_ref, rows_ref)
    pack_rows(upstream_ref, packed_ref)
    channel_sums(False, rows_ref, weight_ref, bias_ref, out_ref, field_ref.shape[0])


def middle_kernel(got_ref, local_hbm, upstream_hbm, high_ref, low_ref, out_ref, grad_ref, local_ref, upstream_ref, sems):
    spans = [pl.ds(first, last - first) for first, last in spans_of(local_ref.shape[0], 128)]
    copies = [
        (start(local_hbm.at[span], local_ref.at[span], sems.at[0, k]), start(upstream_hbm.at[span], upstream_ref.at[span], sems.at[1, k]))
        for k, span in enumerate(spans)
    ]
    table = (high_ref[...], low_ref[...])
    grad_ref[...] = product(halves(got_ref[...]), table, 0, 0)
    for k, span in enumerate(spans):
        rows = slice(span.start, span.start + span.size)
        for copy in copies[k]:
            copy.wait()
        grad_ref[rows, :] = upstream_ref[rows, :] * gelu_slope(grad_ref[rows, :] + local_ref[rows, :])
    out_ref[...] = product(table, halves(grad_ref[...]), 1, 1)


def grads_kernel(rows_ref, weight_ref, out_ref):
    channel_sums(True, rows_ref, weight_ref, None, out_ref, weight_ref.shape[0])


def last_kernel(got_ref, local_ref, high_ref, low_ref, out_hbm, rows_ref, out_ref, sems):
    channels, cells_x, cells_y, _ = out_ref.shape
    cells = cells_x * cells_y
    rows_ref[...] = product(halves(got_ref[...]), (high_ref[...], low_ref[...]), 0, 0)
    leaving = []
    for first, last in spans_of(channels, 4):
        rows = slice(first * cells, last * cells)
        rows_ref[rows, :] = rows_ref[rows, :] + local_ref[rows, :]
        for channel in range(first, last):
            for place in range(cells_x):
                row = channel * cells + place * cells_y
                out_ref[channel, place] = rows_ref[row : row + cells_y, :]
        span = pl.ds(first, last - first)
        leaving.append(start(out_ref.at[span], out_hbm.at[span], sems.at[len(leaving)]))
    for copy in leaving:
        copy.wait()


def outer_kernel(first_spectra, second_spectra, first_grads, second_grads, out_ref):
    _, channels, local_modes, modes = first_spectra.shape
    sources = out_ref.shape[1]
    pairs = ((first_spectra, first_grads), (second_spectra, second_grads))

    def one(step, carry):
        source = pl.program_id(0) * sources + step
        for lane in range(0, modes, LANES):
            span = slice(lane, lane + LANES)
            ins = [(spectra[0, source, :, span], spectra[1, source, :, span]) for spectra, _ in pairs]
            for o in range(channels):
                total_real = None
                total_imag = None
                for (_, grads), (in_real, in_imag) in zip(pairs, ins):
                    g_real = grads[0, o, :, span]
                    g_imag = grads[1, o, :, span]
                    real = g_real * in_real + g_imag * in_imag
                    imag = g_imag * in_real - g_real * in_imag
                    total_real = real if total_real is None else total_real + real
                    total_imag = imag if total_imag is None else total_imag + imag
                out_ref[0, step, o, :, span] = total_real
                out_ref[1, step, o, :, span] = total_imag
        return carry

    lax.fori_loop(0, sources, one, 0)


def in_order(own):
    other = lax.ppermute(own, "dp", [(0, 1), (1, 0)])
    first = lax.axis_index("dp") == 0
    return jnp.where(first, own, other), jnp.where(first, other, own)


def far(*values):
    return [pltpu.with_memory_space_constraint(v, pltpu.HBM) for v in values]


def near(*values):
    return [pltpu.with_memory_space_constraint(v, pltpu.VMEM) for v in values]


def on_tiles(cell_values, cotangent, spectral_weight, channel_weight, channel_bias):
    sample_cells = cell_values[0]
    upstream = cotangent[0]
    count_x = lax.axis_size("gx")
    count_y = lax.axis_size("gy")
    owners = count_x * count_y
    channels, cells_x, cells_y, depth_time = sample_cells.shape
    local_modes = spectral_weight.shape[3]
    modes = spectral_weight.shape[4]
    rows = channels * cells_x * cells_y
    plane = [jnp.asarray(t) for t in host_halves(host_plane(owners, local_modes))]
    cross = [jnp.asarray(t) for t in host_halves(host_cross(count_x, count_y, cells_x, cells_y))]
    f32 = jnp.float32
    bf16 = jnp.bfloat16
    whole = pl.BlockSpec(memory_space=pltpu.VMEM)
    scalars = pl.BlockSpec(memory_space=pltpu.SMEM)
    stays = pl.BlockSpec(memory_space=pltpu.HBM)
    copies = pltpu.SemaphoreType.DMA
    vmem = pltpu.VMEM
    sent = (owners * 2 * local_modes, rows)
    cells = (rows, depth_time)
    spectrum = (2, channels, local_modes, modes)
    group = next(g for g in (4, 2, 1) if channels % g == 0)

    def held(shape):
        return pltpu.HBM(shape, f32)

    def trade(values):
        return lax.all_to_all(values, ("gx", "gy"), split_axis=0, concat_axis=0, tiled=True)

    def across(values, conjugate):
        def body(*refs):
            mode_kernel(conjugate, *refs)

        return pl.pallas_call(
            body,
            out_shape=(held(sent), held(spectrum)),
            in_specs=[whole, stays, whole, whole],
            out_specs=(stays, stays),
            scratch_shapes=[
                vmem(spectral_weight.shape, f32),
                vmem(sent, f32),
                vmem(spectrum, f32),
                vmem((2, 2 * channels * local_modes, owners * cells_x * cells_y // 2), f32),
                vmem((2, channels * local_modes, modes), f32),
                copies((5,)),
                copies,
                copies((2,)),
            ],
            compiler_params=params(),
            name="unmix_modes" if conjugate else "mix_modes",
        )(*near(values), *far(spectral_weight), *near(*cross))

    front = pl.pallas_call(
        front_kernel,
        out_shape=vmem(sent, f32),
        in_specs=[stays] * 3,
        out_specs=whole,
        scratch_shapes=[
            vmem(sample_cells.shape, f32),
            vmem(plane[0].shape, bf16),
            vmem(plane[1].shape, bf16),
            vmem(cells, f32),
            copies((2,)),
            copies((-(-channels // 4),)),
        ],
        compiler_params=params(),
        name="front",
    )(*far(sample_cells, *plane))
    got = trade(front)
    local, packed = pl.pallas_call(
        local_kernel,
        out_shape=(held(cells), held(cells)),
        in_specs=[whole, whole, scalars, scalars],
        out_specs=(whole, whole),
        scratch_shapes=[vmem(cells, f32)],
        compiler_params=params(),
        name="local_pre",
    )(*far(sample_cells, upstream), channel_weight, channel_bias)
    mixed, spectra = across(got, False)
    both_spectra = in_order(spectra)
    got, both_spectra = lax.optimization_barrier((trade(mixed), both_spectra))
    front, grad_pre = pl.pallas_call(
        middle_kernel,
        out_shape=(vmem(sent, f32), vmem(cells, f32)),
        in_specs=[whole, stays, stays, whole, whole],
        out_specs=(whole, whole),
        scratch_shapes=[vmem(cells, f32), vmem(cells, f32), copies((2, -(-rows // 128)))],
        compiler_params=params(),
        name="middle",
    )(*near(got), *far(local, packed), *near(*plane))
    got = trade(front)
    back, grad_spectra = across(got, True)
    both_grads = in_order(grad_spectra)
    got = trade(back)
    local_grad = pl.pallas_call(
        grads_kernel,
        out_shape=held(cells),
        in_specs=[whole, scalars],
        out_specs=whole,
        compiler_params=params(),
        name="local_grad",
    )(*far(grad_pre), channel_weight)
    spectral_grads = pl.pallas_call(
        outer_kernel,
        out_shape=held(spectral_weight.shape),
        grid=(channels // group,),
        in_specs=[whole] * 4,
        out_specs=pl.BlockSpec((2, group, channels, local_modes, modes), lambda i: (0, i, 0, 0, 0)),
        compiler_params=params(),
        name="outer",
    )(*far(*both_spectra), *near(*both_grads))
    cell_grad = pl.pallas_call(
        last_kernel,
        out_shape=held(sample_cells.shape),
        in_specs=[whole] * 4,
        out_specs=stays,
        scratch_shapes=[vmem(cells, f32), vmem(sample_cells.shape, f32), copies((-(-channels // 4),))],
        compiler_params=params(),
        name="last",
    )(*near(got, local_grad, *plane))
    return (cell_grad[None], spectral_grads)


def solution(mesh):
    placed = (
        P("dp", None, "gx", "gy", None),
        P("dp", None, "gx", "gy", None),
        P(None, None, None, ("gx", "gy"), None),
        P(),
        P(),
    )

    def on_any(*args):
        _, channels, cells_x, cells_y, _ = args[0].shape
        fits = args[2].shape[3] == 8 and args[2].shape[4] == 2 * LANES and KX * KY == 2 * LANES and cells_x * cells_y == LANES // 4
        fits = fits and channels % 20 == 0 and lax.axis_size("dp") == 2
        fits = fits and lax.axis_size("gx") % 2 == 0 and lax.axis_size("gy") == 4 and cells_y * 4 == KY
        return on_tiles(*args) if fits else on_device(*args)

    return jax.shard_map(
        on_any,
        mesh=mesh,
        in_specs=placed,
        out_specs=(P("dp", None, "gx", "gy", None), P(None, None, None, ("gx", "gy"), None)),
        check_vma=False,
    )
```

```python
import math

import jax
import jax.numpy as jnp
import numpy as np
from jax import lax
from jax.experimental import pallas as pl
from jax.experimental.pallas import tpu as pltpu
from jax.sharding import PartitionSpec as P

NZ = 32
NT = 16
KX = 16
KY = 16
KZ = 16
KT = 8


highest = lax.Precision.HIGHEST


def gelu_slope(values):
    return (
        0.5 * (1.0 + lax.erf(values * 0.7071067811865476))
        + values * jnp.exp(-0.5 * values * values) * 0.3989422804014327
    )


def signed_freq(number, kept_count):
    return jnp.where(number < kept_count // 2, number, number - kept_count)


def line_table(length, kept_count):
    positions = jnp.arange(length, dtype=jnp.int32)
    frequency = signed_freq(jnp.arange(kept_count, dtype=jnp.int32), kept_count)
    phases = positions[:, None] * frequency[None, :] % length
    angles = phases.astype(jnp.float32) * (-2.0 * math.pi / length)
    return jnp.stack([jnp.cos(angles), jnp.sin(angles)]) / math.sqrt(length)


def block_table(length, kept_count):
    table = line_table(length, kept_count)
    upper = jnp.stack([table[0], table[1]], axis=1)
    lower = jnp.stack([-table[1], table[0]], axis=1)
    return jnp.stack([upper, lower]).reshape(2 * length, 2 * kept_count)


def plane_table(mode_index):
    row_index = jnp.arange(NZ * NT, dtype=jnp.int32)
    depth = row_index // NT
    time_step = row_index % NT
    depth_freq = signed_freq(mode_index // KT, KZ)
    time_freq = signed_freq(mode_index % KT, KT)
    fraction = (depth[:, None] * depth_freq[None, :] % NZ).astype(jnp.float32) / NZ
    fraction = fraction + (time_step[:, None] * time_freq[None, :] % NT).astype(jnp.float32) / NT
    angles = fraction * (-2.0 * math.pi)
    table = jnp.stack([jnp.cos(angles), jnp.sin(angles)]) / math.sqrt(NZ * NT)
    return jnp.moveaxis(table, 0, -1).reshape(NZ * NT, -1)


def line_forward(data, block):
    return jnp.einsum("mpr,pk->mkr", data, block, precision=highest)


def line_adjoint(data, block):
    return jnp.einsum("mkr,pk->mpr", data, block, precision=highest)


def plane_front(real_field, planar, form):
    coeffs = jnp.einsum("cxyn,nk->" + form, real_field, planar, precision=highest)
    return coeffs.reshape(KZ * KT, 2, -1)


def plane_back(stacked, planar, form, first_cells, second_cells, channels):
    rows = stacked.reshape(-1, first_cells, second_cells, channels)
    return jnp.einsum(form + ",nk->cxyn", rows, planar, precision=highest)


def swap_inner(data, first, second, channels):
    leading = data.shape[0]
    moved = jnp.transpose(data.reshape(leading, 2, first, second, channels), (0, 1, 3, 2, 4))
    return moved.reshape(leading, 2, -1)


def mode_mix(weight, spectrum):

    def single(left_arg, right_arg):
        return jnp.einsum("imn,iomn->omn", left_arg, right_arg, precision=highest)

    real_part = single(spectrum[0], weight[0]) - single(spectrum[1], weight[1])
    imag_part = single(spectrum[1], weight[0]) + single(spectrum[0], weight[1])
    return jnp.stack([real_part, imag_part])


def mode_unmix(weight, spectrum):

    def single(left_arg, right_arg):
        return jnp.einsum("omn,iomn->imn", left_arg, right_arg, precision=highest)

    real_part = single(spectrum[0], weight[0]) + single(spectrum[1], weight[1])
    imag_part = single(spectrum[1], weight[0]) - single(spectrum[0], weight[1])
    return jnp.stack([real_part, imag_part])


def mode_outer(grad_spectrum, spectrum):

    def single(left_arg, right_arg):
        return jnp.einsum("omn,imn->iomn", left_arg, right_arg, precision=highest)

    real_part = single(grad_spectrum[0], spectrum[0]) + single(grad_spectrum[1], spectrum[1])
    imag_part = single(grad_spectrum[1], spectrum[0]) - single(grad_spectrum[0], spectrum[1])
    return jnp.stack([real_part, imag_part])


def on_device(cell_values, cotangent, spectral_weight, channel_weight, channel_bias):
    sample_cells = cell_values[0]
    upstream = cotangent[0]
    count_x = lax.axis_size("gx")
    count_y = lax.axis_size("gy")
    channels, cells_x, cells_y, depth_time = sample_cells.shape
    length_x = count_x * cells_x
    length_y = count_y * cells_y
    local_modes = KZ * KT // (count_x * count_y)
    block_x = block_table(length_x, KX)
    block_y = block_table(length_y, KY)
    column = jnp.arange(KZ * KT, dtype=jnp.int32)

    def to_spectrum(last):
        shaped = jnp.transpose(last.reshape(local_modes, 2, KX, KY, channels), (1, 4, 0, 3, 2))
        return shaped.reshape(2, channels, local_modes, KY * KX)

    def from_spectrum(spectrum):
        shaped = spectrum.reshape(2, channels, local_modes, KY, KX)
        return jnp.transpose(shaped, (2, 0, 4, 3, 1)).reshape(local_modes, 2 * KX, KY * channels)

    planar = plane_table(column)

    def forward(real_field):
        gathered = lax.all_to_all(
            plane_front(real_field, planar, "kyxc"),
            ("gx", "gy"),
            split_axis=0,
            concat_axis=2,
            tiled=True,
        )
        arranged = gathered.reshape(local_modes, 2, count_x, count_y, cells_y, cells_x * channels)
        arranged = jnp.transpose(arranged, (0, 1, 3, 4, 2, 5)).reshape(
            local_modes, 2 * length_y, length_x * channels
        )
        along_y = line_forward(arranged, block_y)
        along_y = swap_inner(along_y, KY, length_x, channels).reshape(
            local_modes, 2 * length_x, KY * channels
        )
        along_x = line_forward(along_y, block_x)
        return to_spectrum(along_x)

    def inverse(spectrum):
        back_x = line_adjoint(from_spectrum(spectrum), block_x)
        back_x = swap_inner(back_x, length_x, KY, channels).reshape(
            local_modes, 2 * KY, length_x * channels
        )
        back_y = line_adjoint(back_x, block_y)
        ordered = back_y.reshape(local_modes, 2, count_y, cells_y, count_x, cells_x * channels)
        ordered = jnp.transpose(ordered, (0, 1, 4, 2, 3, 5)).reshape(local_modes, 2, -1)
        spread = lax.all_to_all(ordered, ("gx", "gy"), split_axis=2, concat_axis=0, tiled=True)
        return plane_back(spread, planar, "kyxc", cells_y, cells_x, channels)

    spectra = forward(sample_cells)
    mixed = mode_mix(spectral_weight, spectra)
    pre_act = jnp.einsum("oi,ixyn->oxyn", channel_weight, sample_cells, precision=highest)
    pre_act = pre_act + channel_bias[:, None, None, None] + inverse(mixed)
    grad_pre = upstream * gelu_slope(pre_act)
    grad_spectra = forward(grad_pre)
    back_modes = mode_unmix(spectral_weight, grad_spectra)
    cell_grad = jnp.einsum("oi,oxyn->ixyn", channel_weight, grad_pre, precision=highest) + inverse(
        back_modes
    )
    spectral_grads = lax.psum(mode_outer(grad_spectra, spectra), "dp")
    return (cell_grad[None], spectral_grads)


LANES = 128
VMEM_LIMIT = 24 * 1024 * 1024


def params():
    return pltpu.CompilerParams(vmem_limit_bytes=VMEM_LIMIT)


def halves(values):
    upper = values.astype(jnp.bfloat16)
    return upper, (values - upper.astype(jnp.float32)).astype(jnp.bfloat16)


def host_halves(table):
    upper = table.astype(jnp.bfloat16)
    lower = (table - upper.astype(np.float64)).astype(jnp.bfloat16)
    return upper, lower


def host_freq(number, kept_count):
    return np.where(number < kept_count // 2, number, number - kept_count)


def host_plane(owners, local_modes):
    mode = np.arange(owners * local_modes)
    cell = np.arange(NZ * NT // 2)
    turns = np.outer(host_freq(mode // KT, KZ), cell // NT) / NZ
    turns = turns + np.outer(host_freq(mode % KT, KT), cell % NT) / NT
    angles = 2.0 * np.pi * turns
    table = np.stack([np.cos(angles), -np.sin(angles)]) / np.sqrt(NZ * NT)
    table = table.reshape(2, owners // 2, 2, local_modes, NZ * NT // 2)
    return table.transpose(2, 1, 0, 3, 4).reshape(2, owners * local_modes, NZ * NT // 2)


def host_cross(count_x, count_y, cells_x, cells_y):
    length_x = count_x * cells_x
    length_y = count_y * cells_y
    row = np.arange(length_x * length_y // 2)
    cell = row % (cells_x * cells_y)
    owner = row // (cells_x * cells_y)
    place_x = owner // (count_y // 2) * cells_x + cell // cells_y
    place_y = owner % (count_y // 2) * cells_y + cell % cells_y
    column = np.arange(KY // 2 * KX)
    number_x = column % KX
    block = column // KX
    tables = []
    for number_y in (np.where(block % 2 == 0, block, block + 7), np.where(block % 2 == 1, block, block + 9)):
        turns = np.outer(place_x, host_freq(number_x, KX)) / length_x
        turns = turns + np.outer(place_y, host_freq(number_y, KY)) / length_y
        angles = 2.0 * np.pi * turns
        tables.append(np.concatenate([np.cos(angles), np.sin(angles)], axis=1))
    return np.stack(tables) / np.sqrt(length_x * length_y)


def product(left, right, left_dim, right_dim):
    dims = (((left_dim,), (right_dim,)), ((), ()))

    def single(one, other):
        return lax.dot_general(one, other, dims, preferred_element_type=jnp.float32)

    return single(left[0], right[0]) + (single(left[0], right[1]) + single(left[1], right[0]))


def swap_groups(parts):
    width = LANES // 4
    lane = lax.broadcasted_iota(jnp.int32, parts[0].shape, 1)
    low_half = lane < 2 * width
    low_quarter = lane % (2 * width) < width

    def trade(one, other, mask, shift):
        return (
            jnp.where(mask, one, pltpu.roll(other, shift, 1)),
            jnp.where(mask, pltpu.roll(one, LANES - shift, 1), other),
        )

    first, third = trade(parts[0], parts[2], low_half, 2 * width)
    second, fourth = trade(parts[1], parts[3], low_half, 2 * width)
    first, second = trade(first, second, low_quarter, width)
    third, fourth = trade(third, fourth, low_quarter, width)
    return first, second, third, fourth


def pack_rows(field_ref, rows_ref):
    channels, cells_x, cells_y, _ = field_ref.shape
    for channel in range(channels):
        for place in range(cells_x):
            row = (channel * cells_x + place) * cells_y
            rows_ref[row : row + cells_y, :] = field_ref[channel, place]


def start(source, target, semaphore):
    copy = pltpu.make_async_copy(source, target, semaphore)
    copy.start()
    return copy


def to_plane_modes(rows_ref, high_ref, low_ref, out_ref):
    half = rows_ref.shape[1] // 2
    block = out_ref.shape[0] // 16
    for parity in range(2):
        one, other = rows_ref[:, :half], rows_ref[:, half:]
        values = one - other if parity else one + other
        waves = product((high_ref[parity], low_ref[parity]), halves(values), 1, 1)
        for k in range(8):
            row = (2 * k + parity) * block
            out_ref[row : row + block, :] = waves[k * block : (k + 1) * block]


def from_plane_modes(got_ref, high_ref, low_ref):
    block = got_ref.shape[0] // 16
    waves = []
    for parity in range(2):
        parts = [got_ref[(2 * k + parity) * block : (2 * k + parity + 1) * block, :] for k in range(8)]
        waves.append(product(halves(jnp.concatenate(parts, axis=0)), (high_ref[parity], low_ref[parity]), 0, 0))
    return jnp.concatenate([waves[0] + waves[1], waves[0] - waves[1]], axis=1)


def spans_of(channels, step):
    return [(first, min(first + step, channels)) for first in range(0, channels, step)]


def front_kernel(field_hbm, high_hbm, low_hbm, out_ref, field_ref, high_ref, low_ref, rows_ref, table_sems, field_sems):
    channels, cells_x, cells_y, _ = field_ref.shape
    cells = cells_x * cells_y
    pieces = []
    for first, last in spans_of(channels, 4):
        span = pl.ds(first, last - first)
        pieces.append(start(field_hbm.at[span], field_ref.at[span], field_sems.at[len(pieces)]))
        if first == 0:
            tables = [start(high_hbm, high_ref, table_sems.at[0]), start(low_hbm, low_ref, table_sems.at[1])]
    for piece, (first, last) in enumerate(spans_of(channels, 4)):
        pieces[piece].wait()
        for channel in range(first, last):
            for place in range(cells_x):
                row = channel * cells + place * cells_y
                rows_ref[row : row + cells_y, :] = field_ref[channel, place]
    for copy in tables:
        copy.wait()
    to_plane_modes(rows_ref, high_ref, low_ref, out_ref)


def blocks_even(shape):
    return lax.broadcasted_iota(jnp.int32, shape, 1) // KX % 2 == 0


def in_ky_order(even, odd):
    mask = blocks_even(even.shape)
    low = jnp.where(mask, even, odd)
    high = jnp.where(mask, pltpu.roll(even, LANES - KX, 1), pltpu.roll(odd, KX, 1))
    return low, high


def by_ky_parity(low, high):
    mask = blocks_even(low.shape)
    even = jnp.where(mask, low, pltpu.roll(high, KX, 1))
    odd = jnp.where(mask, pltpu.roll(high, LANES - KX, 1), low)
    return even, odd


def mode_kernel(
    conjugate,
    got_ref,
    weight_hbm,
    high_ref,
    low_ref,
    out_hbm,
    spectra_hbm,
    weight_ref,
    out_ref,
    spectra_ref,
    field_ref,
    mixed_ref,
    weight_sems,
    spectra_sem,
    out_sems,
):
    _, channels, local_modes, modes = spectra_ref.shape
    chunk = channels // weight_sems.shape[0]
    weight_copies = []
    for k in range(weight_sems.shape[0]):
        span = pl.ds(k * chunk, chunk)
        place = (slice(None), span) if conjugate else (slice(None), slice(None), span)
        weight_copies.append(start(weight_hbm.at[place], weight_ref.at[place], weight_sems.at[k]))
    rows = channels * local_modes
    block = 2 * local_modes
    quads = got_ref.shape[0] // (4 * block)
    groups = channels // 4

    def owner_rows(quad, j):
        return slice((4 * quad + j) * block, (4 * quad + j + 1) * block)

    for pair in range(quads // 2):
        for group in range(groups):
            lanes = slice(group * LANES, (group + 1) * LANES)
            near_half, far_half = [
                [got_ref[owner_rows(2 * pair + i, 2 * half + j), lanes] for i in range(2) for j in range(2)] for half in range(2)
            ]
            sums = [one + other for one, other in zip(near_half, far_half)]
            gaps = [one - other for one, other in zip(near_half, far_half)]
            for parity, parts in enumerate((sums, gaps)):
                for m, part in enumerate(swap_groups(parts)):
                    row = (4 * group + m) * local_modes
                    for side in range(2):
                        field_ref[
                            parity, side * rows + row : side * rows + row + local_modes, pair * LANES : (pair + 1) * LANES
                        ] = part[side * local_modes : (side + 1) * local_modes]
    real = []
    imag = []
    for parity in range(2):
        waves = product(halves(field_ref[parity]), (high_ref[parity], low_ref[parity]), 1, 0)
        real.append(waves[:rows, :LANES] + waves[rows:, LANES:])
        imag.append(waves[rows:, :LANES] - waves[:rows, LANES:])
    for part, pair in enumerate((real, imag)):
        for k, values in enumerate(in_ky_order(*pair)):
            spectra_ref[part, :, :, k * LANES : (k + 1) * LANES] = values.reshape(channels, local_modes, LANES)
    spectra_copy = start(spectra_ref, spectra_hbm, spectra_sem)
    for part in range(len(weight_copies) * 2):
        first_lane = part % 2 * LANES
        first_result = part // 2 * chunk
        span = slice(first_lane, first_lane + LANES)
        ins = [(spectra_ref[0, c, :, span], spectra_ref[1, c, :, span]) for c in range(channels)]
        if first_lane == 0:
            weight_copies[part // 2].wait()

        def one(step, carry, span=span, ins=ins, first_result=first_result):
            result = first_result + step
            total_real = jnp.zeros((local_modes, LANES), jnp.float32)
            total_imag = jnp.zeros((local_modes, LANES), jnp.float32)
            for c, (in_real, in_imag) in enumerate(ins):
                if conjugate:
                    w_real = weight_ref[0, result, c, :, span]
                    w_imag = weight_ref[1, result, c, :, span]
                    total_real = total_real + (in_real * w_real + in_imag * w_imag)
                    total_imag = total_imag + (in_imag * w_real - in_real * w_imag)
                else:
                    w_real = weight_ref[0, c, result, :, span]
                    w_imag = weight_ref[1, c, result, :, span]
                    total_real = total_real + (in_real * w_real - in_imag * w_imag)
                    total_imag = total_imag + (in_imag * w_real + in_real * w_imag)
            row = pl.multiple_of(result * local_modes, local_modes)
            mixed_ref[0, pl.ds(row, local_modes), span] = total_real
            mixed_ref[1, pl.ds(row, local_modes), span] = total_imag
            return carry

        lax.fori_loop(0, chunk, one, 0, unroll=True)
    out_copies = []
    for first, last in spans_of(groups, -(-groups // 2)):
        begin, end = 4 * first * local_modes, 4 * last * local_modes
        reals = by_ky_parity(mixed_ref[0, begin:end, :LANES], mixed_ref[0, begin:end, LANES:])
        imags = by_ky_parity(mixed_ref[1, begin:end, :LANES], mixed_ref[1, begin:end, LANES:])
        for parity in range(2):
            left = jnp.concatenate([reals[parity], imags[parity]], axis=0)
            right = jnp.concatenate([-imags[parity], reals[parity]], axis=0)
            both = halves(jnp.concatenate([left, right], axis=1))
            field_ref[parity, 2 * begin : 2 * end, :] = product(both, (high_ref[parity], low_ref[parity]), 1, 1)
        for pair in range(quads // 2):
            for group in range(first, last):
                lanes = slice(group * LANES, (group + 1) * LANES)
                for side in range(2):
                    base = 2 * begin + side * (end - begin) + 4 * (group - first) * local_modes
                    sums, gaps = [
                        swap_groups(
                            [
                                field_ref[
                                    parity,
                                    base + m * local_modes : base + (m + 1) * local_modes,
                                    pair * LANES : (pair + 1) * LANES,
                                ]
                                for m in range(4)
                            ]
                        )
                        for parity in range(2)
                    ]
                    for k in range(4):
                        row = (4 * (2 * pair + k // 2) + k % 2) * block + side * local_modes
                        other = row + 2 * block
                        out_ref[row : row + local_modes, lanes] = sums[k] + gaps[k]
                        out_ref[other : other + local_modes, lanes] = sums[k] - gaps[k]
        place = (slice(None), pl.ds(first * LANES, (last - first) * LANES))
        out_copies.append(start(out_ref.at[place], out_hbm.at[place], out_sems.at[len(out_copies)]))
    spectra_copy.wait()
    for copy in out_copies:
        copy.wait()


def channel_sums(transposed, rows_ref, weight_ref, bias_ref, out_ref, channels):
    height = rows_ref.shape[0] // channels
    for lane in range(0, rows_ref.shape[1], LANES):
        span = slice(lane, lane + LANES)

        def one(step, carry, span=span):
            ins = [rows_ref[pl.ds(pl.multiple_of(i * height + step * 8, 8), 8), span] for i in range(channels)]
            for o in range(channels):
                total = None
                for i in range(channels):
                    factor = weight_ref[i, o] if transposed else weight_ref[o, i]
                    term = ins[i] * factor
                    total = term if total is None else total + term
                if bias_ref is not None:
                    total = total + bias_ref[o]
                out_ref[pl.ds(pl.multiple_of(o * height + step * 8, 8), 8), span] = total
            return carry

        lax.fori_loop(0, height // 8, one, 0)


def local_kernel(field_ref, upstream_ref, weight_ref, bias_ref, out_ref, packed_ref, rows_ref):
    pack_rows(field_ref, rows_ref)
    pack_rows(upstream_ref, packed_ref)
    channel_sums(False, rows_ref, weight_ref, bias_ref, out_ref, field_ref.shape[0])


def middle_kernel(got_ref, local_hbm, upstream_hbm, high_ref, low_ref, out_ref, grad_ref, local_ref, upstream_ref, sems):
    spans = [pl.ds(first, last - first) for first, last in spans_of(local_ref.shape[0], 128)]
    copies = [
        (start(local_hbm.at[span], local_ref.at[span], sems.at[0, k]), start(upstream_hbm.at[span], upstream_ref.at[span], sems.at[1, k]))
        for k, span in enumerate(spans)
    ]
    grad_ref[...] = from_plane_modes(got_ref, high_ref, low_ref)
    for k, span in enumerate(spans):
        rows = slice(span.start, span.start + span.size)
        for copy in copies[k]:
            copy.wait()
        grad_ref[rows, :] = upstream_ref[rows, :] * gelu_slope(grad_ref[rows, :] + local_ref[rows, :])
    to_plane_modes(grad_ref, high_ref, low_ref, out_ref)


def grads_kernel(rows_ref, weight_ref, out_ref):
    channel_sums(True, rows_ref, weight_ref, None, out_ref, weight_ref.shape[0])


def last_kernel(got_ref, local_ref, high_ref, low_ref, out_hbm, rows_ref, out_ref, sems):
    channels, cells_x, cells_y, _ = out_ref.shape
    cells = cells_x * cells_y
    rows_ref[...] = from_plane_modes(got_ref, high_ref, low_ref)
    leaving = []
    for first, last in spans_of(channels, 4):
        rows = slice(first * cells, last * cells)
        rows_ref[rows, :] = rows_ref[rows, :] + local_ref[rows, :]
        for channel in range(first, last):
            for place in range(cells_x):
                row = channel * cells + place * cells_y
                out_ref[channel, place] = rows_ref[row : row + cells_y, :]
        span = pl.ds(first, last - first)
        leaving.append(start(out_ref.at[span], out_hbm.at[span], sems.at[len(leaving)]))
    for copy in leaving:
        copy.wait()


def outer_kernel(first_spectra, second_spectra, first_grads, second_grads, out_ref):
    _, channels, local_modes, modes = first_spectra.shape
    sources = out_ref.shape[1]
    pairs = ((first_spectra, first_grads), (second_spectra, second_grads))

    def one(step, carry):
        source = pl.program_id(0) * sources + step
        for lane in range(0, modes, LANES):
            span = slice(lane, lane + LANES)
            ins = [(spectra[0, source, :, span], spectra[1, source, :, span]) for spectra, _ in pairs]
            for o in range(channels):
                total_real = None
                total_imag = None
                for (_, grads), (in_real, in_imag) in zip(pairs, ins):
                    g_real = grads[0, o, :, span]
                    g_imag = grads[1, o, :, span]
                    real = g_real * in_real + g_imag * in_imag
                    imag = g_imag * in_real - g_real * in_imag
                    total_real = real if total_real is None else total_real + real
                    total_imag = imag if total_imag is None else total_imag + imag
                out_ref[0, step, o, :, span] = total_real
                out_ref[1, step, o, :, span] = total_imag
        return carry

    lax.fori_loop(0, sources, one, 0)


def in_order(own):
    other = lax.ppermute(own, "dp", [(0, 1), (1, 0)])
    first = lax.axis_index("dp") == 0
    return jnp.where(first, own, other), jnp.where(first, other, own)


def far(*values):
    return [pltpu.with_memory_space_constraint(v, pltpu.HBM) for v in values]


def near(*values):
    return [pltpu.with_memory_space_constraint(v, pltpu.VMEM) for v in values]


def on_tiles(cell_values, cotangent, spectral_weight, channel_weight, channel_bias):
    sample_cells = cell_values[0]
    upstream = cotangent[0]
    count_x = lax.axis_size("gx")
    count_y = lax.axis_size("gy")
    owners = count_x * count_y
    channels, cells_x, cells_y, depth_time = sample_cells.shape
    local_modes = spectral_weight.shape[3]
    modes = spectral_weight.shape[4]
    rows = channels * cells_x * cells_y
    plane = [jnp.asarray(t) for t in host_halves(host_plane(owners, local_modes))]
    cross = [jnp.asarray(t) for t in host_halves(host_cross(count_x, count_y, cells_x, cells_y))]
    f32 = jnp.float32
    bf16 = jnp.bfloat16
    whole = pl.BlockSpec(memory_space=pltpu.VMEM)
    scalars = pl.BlockSpec(memory_space=pltpu.SMEM)
    stays = pl.BlockSpec(memory_space=pltpu.HBM)
    copies = pltpu.SemaphoreType.DMA
    vmem = pltpu.VMEM
    sent = (owners * 2 * local_modes, rows)
    cells = (rows, depth_time)
    spectrum = (2, channels, local_modes, modes)
    group = next(g for g in (4, 2, 1) if channels % g == 0)

    def held(shape):
        return pltpu.HBM(shape, f32)

    def trade(values):
        return lax.all_to_all(values, ("gx", "gy"), split_axis=0, concat_axis=0, tiled=True)

    def across(values, conjugate):
        def body(*refs):
            mode_kernel(conjugate, *refs)

        return pl.pallas_call(
            body,
            out_shape=(held(sent), held(spectrum)),
            in_specs=[whole, stays, whole, whole],
            out_specs=(stays, stays),
            scratch_shapes=[
                vmem(spectral_weight.shape, f32),
                vmem(sent, f32),
                vmem(spectrum, f32),
                vmem((2, 2 * channels * local_modes, owners * cells_x * cells_y // 2), f32),
                vmem((2, channels * local_modes, modes), f32),
                copies((5,)),
                copies,
                copies((2,)),
            ],
            compiler_params=params(),
            name="unmix_modes" if conjugate else "mix_modes",
        )(*near(values), *far(spectral_weight), *near(*cross))

    front = pl.pallas_call(
        front_kernel,
        out_shape=vmem(sent, f32),
        in_specs=[stays] * 3,
        out_specs=whole,
        scratch_shapes=[
            vmem(sample_cells.shape, f32),
            vmem(plane[0].shape, bf16),
            vmem(plane[1].shape, bf16),
            vmem(cells, f32),
            copies((2,)),
            copies((-(-channels // 4),)),
        ],
        compiler_params=params(),
        name="front",
    )(*far(sample_cells, *plane))
    got = trade(front)
    local, packed = pl.pallas_call(
        local_kernel,
        out_shape=(held(cells), held(cells)),
        in_specs=[whole, whole, scalars, scalars],
        out_specs=(whole, whole),
        scratch_shapes=[vmem(cells, f32)],
        compiler_params=params(),
        name="local_pre",
    )(*far(sample_cells, upstream), channel_weight, channel_bias)
    mixed, spectra = across(got, False)
    both_spectra = in_order(spectra)
    got, both_spectra = lax.optimization_barrier((trade(mixed), both_spectra))
    front, grad_pre = pl.pallas_call(
        middle_kernel,
        out_shape=(vmem(sent, f32), vmem(cells, f32)),
        in_specs=[whole, stays, stays, whole, whole],
        out_specs=(whole, whole),
        scratch_shapes=[vmem(cells, f32), vmem(cells, f32), copies((2, -(-rows // 128)))],
        compiler_params=params(),
        name="middle",
    )(*near(got), *far(local, packed), *near(*plane))
    got = trade(front)
    back, grad_spectra = across(got, True)
    both_grads = in_order(grad_spectra)
    got = trade(back)
    local_grad = pl.pallas_call(
        grads_kernel,
        out_shape=held(cells),
        in_specs=[whole, scalars],
        out_specs=whole,
        compiler_params=params(),
        name="local_grad",
    )(*far(grad_pre), channel_weight)
    spectral_grads = pl.pallas_call(
        outer_kernel,
        out_shape=held(spectral_weight.shape),
        grid=(channels // group,),
        in_specs=[whole] * 4,
        out_specs=pl.BlockSpec((2, group, channels, local_modes, modes), lambda i: (0, i, 0, 0, 0)),
        compiler_params=params(),
        name="outer",
    )(*far(*both_spectra), *near(*both_grads))
    cell_grad = pl.pallas_call(
        last_kernel,
        out_shape=held(sample_cells.shape),
        in_specs=[whole] * 4,
        out_specs=stays,
        scratch_shapes=[vmem(cells, f32), vmem(sample_cells.shape, f32), copies((-(-channels // 4),))],
        compiler_params=params(),
        name="last",
    )(*near(got, local_grad, *plane))
    return (cell_grad[None], spectral_grads)


def solution(mesh):
    placed = (
        P("dp", None, "gx", "gy", None),
        P("dp", None, "gx", "gy", None),
        P(None, None, None, ("gx", "gy"), None),
        P(),
        P(),
    )

    def on_any(*args):
        _, channels, cells_x, cells_y, _ = args[0].shape
        fits = args[2].shape[3] == 8 and args[2].shape[4] == 2 * LANES and KX * KY == 2 * LANES and cells_x * cells_y == LANES // 4
        fits = fits and channels % 20 == 0 and args[2].shape[3] == KT and KZ * KT == 16 * 8 and lax.axis_size("dp") == 2
        fits = fits and lax.axis_size("gx") == 4 and lax.axis_size("gy") == 4 and cells_y * 4 == KY
        return on_tiles(*args) if fits else on_device(*args)

    return jax.shard_map(
        on_any,
        mesh=mesh,
        in_specs=placed,
        out_specs=(P("dp", None, "gx", "gy", None), P(None, None, None, ("gx", "gy"), None)),
        check_vma=False,
    )
```

```python
import math

import jax
import jax.numpy as jnp
import numpy as np
from jax import lax
from jax.experimental import pallas as pl
from jax.experimental.pallas import tpu as pltpu
from jax.sharding import PartitionSpec as P

NZ = 32
NT = 16
KX = 16
KY = 16
KZ = 16
KT = 8


highest = lax.Precision.HIGHEST


def gelu_slope(values):
    return (
        0.5 * (1.0 + lax.erf(values * 0.7071067811865476))
        + values * jnp.exp(-0.5 * values * values) * 0.3989422804014327
    )


def signed_freq(number, kept_count):
    return jnp.where(number < kept_count // 2, number, number - kept_count)


def line_table(length, kept_count):
    positions = jnp.arange(length, dtype=jnp.int32)
    frequency = signed_freq(jnp.arange(kept_count, dtype=jnp.int32), kept_count)
    phases = positions[:, None] * frequency[None, :] % length
    angles = phases.astype(jnp.float32) * (-2.0 * math.pi / length)
    return jnp.stack([jnp.cos(angles), jnp.sin(angles)]) / math.sqrt(length)


def block_table(length, kept_count):
    table = line_table(length, kept_count)
    upper = jnp.stack([table[0], table[1]], axis=1)
    lower = jnp.stack([-table[1], table[0]], axis=1)
    return jnp.stack([upper, lower]).reshape(2 * length, 2 * kept_count)


def plane_table(mode_index):
    row_index = jnp.arange(NZ * NT, dtype=jnp.int32)
    depth = row_index // NT
    time_step = row_index % NT
    depth_freq = signed_freq(mode_index // KT, KZ)
    time_freq = signed_freq(mode_index % KT, KT)
    fraction = (depth[:, None] * depth_freq[None, :] % NZ).astype(jnp.float32) / NZ
    fraction = fraction + (time_step[:, None] * time_freq[None, :] % NT).astype(jnp.float32) / NT
    angles = fraction * (-2.0 * math.pi)
    table = jnp.stack([jnp.cos(angles), jnp.sin(angles)]) / math.sqrt(NZ * NT)
    return jnp.moveaxis(table, 0, -1).reshape(NZ * NT, -1)


def line_forward(data, block):
    return jnp.einsum("mpr,pk->mkr", data, block, precision=highest)


def line_adjoint(data, block):
    return jnp.einsum("mkr,pk->mpr", data, block, precision=highest)


def plane_front(real_field, planar, form):
    coeffs = jnp.einsum("cxyn,nk->" + form, real_field, planar, precision=highest)
    return coeffs.reshape(KZ * KT, 2, -1)


def plane_back(stacked, planar, form, first_cells, second_cells, channels):
    rows = stacked.reshape(-1, first_cells, second_cells, channels)
    return jnp.einsum(form + ",nk->cxyn", rows, planar, precision=highest)


def swap_inner(data, first, second, channels):
    leading = data.shape[0]
    moved = jnp.transpose(data.reshape(leading, 2, first, second, channels), (0, 1, 3, 2, 4))
    return moved.reshape(leading, 2, -1)


def mode_mix(weight, spectrum):

    def single(left_arg, right_arg):
        return jnp.einsum("imn,iomn->omn", left_arg, right_arg, precision=highest)

    real_part = single(spectrum[0], weight[0]) - single(spectrum[1], weight[1])
    imag_part = single(spectrum[1], weight[0]) + single(spectrum[0], weight[1])
    return jnp.stack([real_part, imag_part])


def mode_unmix(weight, spectrum):

    def single(left_arg, right_arg):
        return jnp.einsum("omn,iomn->imn", left_arg, right_arg, precision=highest)

    real_part = single(spectrum[0], weight[0]) + single(spectrum[1], weight[1])
    imag_part = single(spectrum[1], weight[0]) - single(spectrum[0], weight[1])
    return jnp.stack([real_part, imag_part])


def mode_outer(grad_spectrum, spectrum):

    def single(left_arg, right_arg):
        return jnp.einsum("omn,imn->iomn", left_arg, right_arg, precision=highest)

    real_part = single(grad_spectrum[0], spectrum[0]) + single(grad_spectrum[1], spectrum[1])
    imag_part = single(grad_spectrum[1], spectrum[0]) - single(grad_spectrum[0], spectrum[1])
    return jnp.stack([real_part, imag_part])


def on_device(cell_values, cotangent, spectral_weight, channel_weight, channel_bias):
    sample_cells = cell_values[0]
    upstream = cotangent[0]
    count_x = lax.axis_size("gx")
    count_y = lax.axis_size("gy")
    channels, cells_x, cells_y, depth_time = sample_cells.shape
    length_x = count_x * cells_x
    length_y = count_y * cells_y
    local_modes = KZ * KT // (count_x * count_y)
    block_x = block_table(length_x, KX)
    block_y = block_table(length_y, KY)
    column = jnp.arange(KZ * KT, dtype=jnp.int32)

    def to_spectrum(last):
        shaped = jnp.transpose(last.reshape(local_modes, 2, KX, KY, channels), (1, 4, 0, 3, 2))
        return shaped.reshape(2, channels, local_modes, KY * KX)

    def from_spectrum(spectrum):
        shaped = spectrum.reshape(2, channels, local_modes, KY, KX)
        return jnp.transpose(shaped, (2, 0, 4, 3, 1)).reshape(local_modes, 2 * KX, KY * channels)

    planar = plane_table(column)

    def forward(real_field):
        gathered = lax.all_to_all(
            plane_front(real_field, planar, "kyxc"),
            ("gx", "gy"),
            split_axis=0,
            concat_axis=2,
            tiled=True,
        )
        arranged = gathered.reshape(local_modes, 2, count_x, count_y, cells_y, cells_x * channels)
        arranged = jnp.transpose(arranged, (0, 1, 3, 4, 2, 5)).reshape(
            local_modes, 2 * length_y, length_x * channels
        )
        along_y = line_forward(arranged, block_y)
        along_y = swap_inner(along_y, KY, length_x, channels).reshape(
            local_modes, 2 * length_x, KY * channels
        )
        along_x = line_forward(along_y, block_x)
        return to_spectrum(along_x)

    def inverse(spectrum):
        back_x = line_adjoint(from_spectrum(spectrum), block_x)
        back_x = swap_inner(back_x, length_x, KY, channels).reshape(
            local_modes, 2 * KY, length_x * channels
        )
        back_y = line_adjoint(back_x, block_y)
        ordered = back_y.reshape(local_modes, 2, count_y, cells_y, count_x, cells_x * channels)
        ordered = jnp.transpose(ordered, (0, 1, 4, 2, 3, 5)).reshape(local_modes, 2, -1)
        spread = lax.all_to_all(ordered, ("gx", "gy"), split_axis=2, concat_axis=0, tiled=True)
        return plane_back(spread, planar, "kyxc", cells_y, cells_x, channels)

    spectra = forward(sample_cells)
    mixed = mode_mix(spectral_weight, spectra)
    pre_act = jnp.einsum("oi,ixyn->oxyn", channel_weight, sample_cells, precision=highest)
    pre_act = pre_act + channel_bias[:, None, None, None] + inverse(mixed)
    grad_pre = upstream * gelu_slope(pre_act)
    grad_spectra = forward(grad_pre)
    back_modes = mode_unmix(spectral_weight, grad_spectra)
    cell_grad = jnp.einsum("oi,oxyn->ixyn", channel_weight, grad_pre, precision=highest) + inverse(
        back_modes
    )
    spectral_grads = lax.psum(mode_outer(grad_spectra, spectra), "dp")
    return (cell_grad[None], spectral_grads)


LANES = 128
VMEM_LIMIT = 24 * 1024 * 1024


def params():
    return pltpu.CompilerParams(vmem_limit_bytes=VMEM_LIMIT)


def halves(values):
    upper = values.astype(jnp.bfloat16)
    return upper, (values - upper.astype(jnp.float32)).astype(jnp.bfloat16)


def host_halves(table):
    upper = table.astype(jnp.bfloat16)
    lower = (table - upper.astype(np.float64)).astype(jnp.bfloat16)
    return upper, lower


def host_freq(number, kept_count):
    return np.where(number < kept_count // 2, number, number - kept_count)


def host_plane(owners, local_modes):
    mode = np.arange(owners * local_modes)
    cell = np.arange(NZ * NT // 2)
    turns = np.outer(host_freq(mode // KT, KZ), cell // NT) / NZ
    turns = turns + np.outer(host_freq(mode % KT, KT), cell % NT) / NT
    angles = 2.0 * np.pi * turns
    table = np.stack([np.cos(angles), -np.sin(angles)]) / np.sqrt(NZ * NT)
    table = table.reshape(2, owners // 2, 2, local_modes, NZ * NT // 2)
    return table.transpose(2, 1, 0, 3, 4).reshape(2, owners * local_modes, NZ * NT // 2)


def host_cross(count_x, count_y, cells_x, cells_y):
    length_x = count_x * cells_x
    length_y = count_y * cells_y
    row = np.arange(length_x * length_y // 2)
    cell = row % (cells_x * cells_y)
    owner = row // (cells_x * cells_y)
    place_x = owner // (count_y // 2) * cells_x + cell // cells_y
    place_y = owner % (count_y // 2) * cells_y + cell % cells_y
    column = np.arange(KY // 2 * KX)
    number_x = column % KX
    block = column // KX
    tables = []
    for number_y in (np.where(block % 2 == 0, block, block + 7), np.where(block % 2 == 1, block, block + 9)):
        turns = np.outer(place_x, host_freq(number_x, KX)) / length_x
        turns = turns + np.outer(place_y, host_freq(number_y, KY)) / length_y
        angles = 2.0 * np.pi * turns
        tables.append(np.concatenate([np.cos(angles), np.sin(angles)], axis=1))
    return np.stack(tables) / np.sqrt(length_x * length_y)


def product(left, right, left_dim, right_dim):
    dims = (((left_dim,), (right_dim,)), ((), ()))

    def single(one, other):
        return lax.dot_general(one, other, dims, preferred_element_type=jnp.float32)

    return single(left[0], right[0]) + (single(left[0], right[1]) + single(left[1], right[0]))


def swap_groups(parts):
    width = LANES // 4
    lane = lax.broadcasted_iota(jnp.int32, parts[0].shape, 1)
    low_half = lane < 2 * width
    low_quarter = lane % (2 * width) < width

    def trade(one, other, mask, shift):
        return (
            jnp.where(mask, one, pltpu.roll(other, shift, 1)),
            jnp.where(mask, pltpu.roll(one, LANES - shift, 1), other),
        )

    first, third = trade(parts[0], parts[2], low_half, 2 * width)
    second, fourth = trade(parts[1], parts[3], low_half, 2 * width)
    first, second = trade(first, second, low_quarter, width)
    third, fourth = trade(third, fourth, low_quarter, width)
    return first, second, third, fourth


def pack_rows(field_ref, rows_ref):
    channels, cells_x, cells_y, _ = field_ref.shape
    for channel in range(channels):
        for place in range(cells_x):
            row = (channel * cells_x + place) * cells_y
            rows_ref[row : row + cells_y, :] = field_ref[channel, place]


def start(source, target, semaphore):
    copy = pltpu.make_async_copy(source, target, semaphore)
    copy.start()
    return copy


def to_plane_modes(rows_ref, high_ref, low_ref, out_ref):
    half = rows_ref.shape[1] // 2
    block = out_ref.shape[0] // 16
    for parity in range(2):
        one, other = rows_ref[:, :half], rows_ref[:, half:]
        values = one - other if parity else one + other
        waves = product((high_ref[parity], low_ref[parity]), halves(values), 1, 1)
        for k in range(8):
            row = slot(2 * k + parity) * block
            out_ref[row : row + block, :] = waves[k * block : (k + 1) * block]


def from_plane_modes(got_ref, high_ref, low_ref):
    block = got_ref.shape[0] // 16
    waves = []
    for parity in range(2):
        rows = [slot(2 * k + parity) * block for k in range(8)]
        parts = [got_ref[row : row + block, :] for row in rows]
        waves.append(product(halves(jnp.concatenate(parts, axis=0)), (high_ref[parity], low_ref[parity]), 0, 0))
    return jnp.concatenate([waves[0] + waves[1], waves[0] - waves[1]], axis=1)


def slot(owner):
    return owner % 4 * 4 + owner // 4


def spans_of(channels, step):
    return [(first, min(first + step, channels)) for first in range(0, channels, step)]


def front_kernel(field_hbm, high_hbm, low_hbm, out_ref, field_ref, high_ref, low_ref, rows_ref, table_sems, field_sems):
    channels, cells_x, cells_y, _ = field_ref.shape
    cells = cells_x * cells_y
    pieces = []
    for first, last in spans_of(channels, 4):
        span = pl.ds(first, last - first)
        pieces.append(start(field_hbm.at[span], field_ref.at[span], field_sems.at[len(pieces)]))
        if first == 0:
            tables = [start(high_hbm, high_ref, table_sems.at[0]), start(low_hbm, low_ref, table_sems.at[1])]
    for piece, (first, last) in enumerate(spans_of(channels, 4)):
        pieces[piece].wait()
        for channel in range(first, last):
            for place in range(cells_x):
                row = channel * cells + place * cells_y
                rows_ref[row : row + cells_y, :] = field_ref[channel, place]
    for copy in tables:
        copy.wait()
    to_plane_modes(rows_ref, high_ref, low_ref, out_ref)


def blocks_even(shape):
    return lax.broadcasted_iota(jnp.int32, shape, 1) // KX % 2 == 0


def in_ky_order(even, odd):
    mask = blocks_even(even.shape)
    low = jnp.where(mask, even, odd)
    high = jnp.where(mask, pltpu.roll(even, LANES - KX, 1), pltpu.roll(odd, KX, 1))
    return low, high


def by_ky_parity(low, high):
    mask = blocks_even(low.shape)
    even = jnp.where(mask, low, pltpu.roll(high, KX, 1))
    odd = jnp.where(mask, pltpu.roll(high, LANES - KX, 1), low)
    return even, odd


def mode_kernel(
    conjugate,
    got_ref,
    weight_hbm,
    high_ref,
    low_ref,
    out_hbm,
    spectra_hbm,
    weight_ref,
    out_ref,
    spectra_ref,
    field_ref,
    mixed_ref,
    weight_sems,
    spectra_sem,
    out_sems,
):
    _, channels, local_modes, modes = spectra_ref.shape
    chunk = channels // weight_sems.shape[0]
    weight_copies = []
    for k in range(weight_sems.shape[0]):
        span = pl.ds(k * chunk, chunk)
        place = (slice(None), span) if conjugate else (slice(None), slice(None), span)
        weight_copies.append(start(weight_hbm.at[place], weight_ref.at[place], weight_sems.at[k]))
    rows = channels * local_modes
    block = 2 * local_modes
    quads = got_ref.shape[0] // (4 * block)
    groups = channels // 4

    def owner_rows(quad, j):
        first = slot(4 * quad + j) * block
        return slice(first, first + block)

    for pair in range(quads // 2):
        for group in range(groups):
            lanes = slice(group * LANES, (group + 1) * LANES)
            near_half, far_half = [
                [got_ref[owner_rows(2 * pair + i, 2 * half + j), lanes] for i in range(2) for j in range(2)] for half in range(2)
            ]
            sums = [one + other for one, other in zip(near_half, far_half)]
            gaps = [one - other for one, other in zip(near_half, far_half)]
            for parity, parts in enumerate((sums, gaps)):
                for m, part in enumerate(swap_groups(parts)):
                    row = (4 * group + m) * local_modes
                    for side in range(2):
                        field_ref[
                            parity, side * rows + row : side * rows + row + local_modes, pair * LANES : (pair + 1) * LANES
                        ] = part[side * local_modes : (side + 1) * local_modes]
    real = []
    imag = []
    for parity in range(2):
        waves = product(halves(field_ref[parity]), (high_ref[parity], low_ref[parity]), 1, 0)
        real.append(waves[:rows, :LANES] + waves[rows:, LANES:])
        imag.append(waves[rows:, :LANES] - waves[:rows, LANES:])
    for part, pair in enumerate((real, imag)):
        for k, values in enumerate(in_ky_order(*pair)):
            spectra_ref[part, :, :, k * LANES : (k + 1) * LANES] = values.reshape(channels, local_modes, LANES)
    spectra_copy = start(spectra_ref, spectra_hbm, spectra_sem)
    for part in range(len(weight_copies) * 2):
        first_lane = part % 2 * LANES
        first_result = part // 2 * chunk
        span = slice(first_lane, first_lane + LANES)
        ins = [(spectra_ref[0, c, :, span], spectra_ref[1, c, :, span]) for c in range(channels)]
        if first_lane == 0:
            weight_copies[part // 2].wait()

        def one(step, carry, span=span, ins=ins, first_result=first_result):
            result = first_result + step
            total_real = jnp.zeros((local_modes, LANES), jnp.float32)
            total_imag = jnp.zeros((local_modes, LANES), jnp.float32)
            for c, (in_real, in_imag) in enumerate(ins):
                if conjugate:
                    w_real = weight_ref[0, result, c, :, span]
                    w_imag = weight_ref[1, result, c, :, span]
                    total_real = total_real + (in_real * w_real + in_imag * w_imag)
                    total_imag = total_imag + (in_imag * w_real - in_real * w_imag)
                else:
                    w_real = weight_ref[0, c, result, :, span]
                    w_imag = weight_ref[1, c, result, :, span]
                    total_real = total_real + (in_real * w_real - in_imag * w_imag)
                    total_imag = total_imag + (in_imag * w_real + in_real * w_imag)
            row = pl.multiple_of(result * local_modes, local_modes)
            mixed_ref[0, pl.ds(row, local_modes), span] = total_real
            mixed_ref[1, pl.ds(row, local_modes), span] = total_imag
            return carry

        lax.fori_loop(0, chunk, one, 0, unroll=True)
    out_copies = []
    for first, last in spans_of(groups, -(-groups // 2)):
        begin, end = 4 * first * local_modes, 4 * last * local_modes
        reals = by_ky_parity(mixed_ref[0, begin:end, :LANES], mixed_ref[0, begin:end, LANES:])
        imags = by_ky_parity(mixed_ref[1, begin:end, :LANES], mixed_ref[1, begin:end, LANES:])
        for parity in range(2):
            left = jnp.concatenate([reals[parity], imags[parity]], axis=0)
            right = jnp.concatenate([-imags[parity], reals[parity]], axis=0)
            both = halves(jnp.concatenate([left, right], axis=1))
            field_ref[parity, 2 * begin : 2 * end, :] = product(both, (high_ref[parity], low_ref[parity]), 1, 1)
        for pair in range(quads // 2):
            for group in range(first, last):
                lanes = slice(group * LANES, (group + 1) * LANES)
                for side in range(2):
                    base = 2 * begin + side * (end - begin) + 4 * (group - first) * local_modes
                    sums, gaps = [
                        swap_groups(
                            [
                                field_ref[
                                    parity,
                                    base + m * local_modes : base + (m + 1) * local_modes,
                                    pair * LANES : (pair + 1) * LANES,
                                ]
                                for m in range(4)
                            ]
                        )
                        for parity in range(2)
                    ]
                    for k in range(4):
                        owner = 4 * (2 * pair + k // 2) + k % 2
                        row = slot(owner) * block + side * local_modes
                        other = slot(owner + 2) * block + side * local_modes
                        out_ref[row : row + local_modes, lanes] = sums[k] + gaps[k]
                        out_ref[other : other + local_modes, lanes] = sums[k] - gaps[k]
        place = (slice(None), pl.ds(first * LANES, (last - first) * LANES))
        out_copies.append(start(out_ref.at[place], out_hbm.at[place], out_sems.at[len(out_copies)]))
    spectra_copy.wait()
    for copy in out_copies:
        copy.wait()


def channel_sums(transposed, rows_ref, weight_ref, bias_ref, out_ref, channels):
    height = rows_ref.shape[0] // channels
    for lane in range(0, rows_ref.shape[1], LANES):
        span = slice(lane, lane + LANES)

        def one(step, carry, span=span):
            ins = [rows_ref[pl.ds(pl.multiple_of(i * height + step * 8, 8), 8), span] for i in range(channels)]
            for o in range(channels):
                total = None
                for i in range(channels):
                    factor = weight_ref[i, o] if transposed else weight_ref[o, i]
                    term = ins[i] * factor
                    total = term if total is None else total + term
                if bias_ref is not None:
                    total = total + bias_ref[o]
                out_ref[pl.ds(pl.multiple_of(o * height + step * 8, 8), 8), span] = total
            return carry

        lax.fori_loop(0, height // 8, one, 0)


def local_kernel(field_ref, upstream_ref, weight_ref, bias_ref, out_ref, packed_ref, rows_ref):
    pack_rows(field_ref, rows_ref)
    pack_rows(upstream_ref, packed_ref)
    channel_sums(False, rows_ref, weight_ref, bias_ref, out_ref, field_ref.shape[0])


def middle_kernel(got_ref, local_hbm, upstream_hbm, high_ref, low_ref, out_ref, grad_ref, local_ref, upstream_ref, sems):
    spans = [pl.ds(first, last - first) for first, last in spans_of(local_ref.shape[0], 128)]
    copies = [
        (start(local_hbm.at[span], local_ref.at[span], sems.at[0, k]), start(upstream_hbm.at[span], upstream_ref.at[span], sems.at[1, k]))
        for k, span in enumerate(spans)
    ]
    grad_ref[...] = from_plane_modes(got_ref, high_ref, low_ref)
    for k, span in enumerate(spans):
        rows = slice(span.start, span.start + span.size)
        for copy in copies[k]:
            copy.wait()
        grad_ref[rows, :] = upstream_ref[rows, :] * gelu_slope(grad_ref[rows, :] + local_ref[rows, :])
    to_plane_modes(grad_ref, high_ref, low_ref, out_ref)


def grads_kernel(rows_ref, weight_ref, out_ref):
    channel_sums(True, rows_ref, weight_ref, None, out_ref, weight_ref.shape[0])


def last_kernel(got_ref, local_ref, high_ref, low_ref, out_hbm, rows_ref, out_ref, sems):
    channels, cells_x, cells_y, _ = out_ref.shape
    cells = cells_x * cells_y
    rows_ref[...] = from_plane_modes(got_ref, high_ref, low_ref)
    leaving = []
    for first, last in spans_of(channels, 4):
        rows = slice(first * cells, last * cells)
        rows_ref[rows, :] = rows_ref[rows, :] + local_ref[rows, :]
        for channel in range(first, last):
            for place in range(cells_x):
                row = channel * cells + place * cells_y
                out_ref[channel, place] = rows_ref[row : row + cells_y, :]
        span = pl.ds(first, last - first)
        leaving.append(start(out_ref.at[span], out_hbm.at[span], sems.at[len(leaving)]))
    for copy in leaving:
        copy.wait()


def outer_kernel(first_spectra, second_spectra, first_grads, second_grads, out_ref):
    _, channels, local_modes, modes = first_spectra.shape
    sources = out_ref.shape[1]
    pairs = ((first_spectra, first_grads), (second_spectra, second_grads))

    def one(step, carry):
        source = pl.program_id(0) * sources + step
        for lane in range(0, modes, LANES):
            span = slice(lane, lane + LANES)
            ins = [(spectra[0, source, :, span], spectra[1, source, :, span]) for spectra, _ in pairs]
            for o in range(channels):
                total_real = None
                total_imag = None
                for (_, grads), (in_real, in_imag) in zip(pairs, ins):
                    g_real = grads[0, o, :, span]
                    g_imag = grads[1, o, :, span]
                    real = g_real * in_real + g_imag * in_imag
                    imag = g_imag * in_real - g_real * in_imag
                    total_real = real if total_real is None else total_real + real
                    total_imag = imag if total_imag is None else total_imag + imag
                out_ref[0, step, o, :, span] = total_real
                out_ref[1, step, o, :, span] = total_imag
        return carry

    lax.fori_loop(0, sources, one, 0)


def in_order(own):
    other = lax.ppermute(own, "dp", [(0, 1), (1, 0)])
    first = lax.axis_index("dp") == 0
    return jnp.where(first, own, other), jnp.where(first, other, own)


def far(*values):
    return [pltpu.with_memory_space_constraint(v, pltpu.HBM) for v in values]


def near(*values):
    return [pltpu.with_memory_space_constraint(v, pltpu.VMEM) for v in values]


def on_tiles(cell_values, cotangent, spectral_weight, channel_weight, channel_bias):
    sample_cells = cell_values[0]
    upstream = cotangent[0]
    count_x = lax.axis_size("gx")
    count_y = lax.axis_size("gy")
    owners = count_x * count_y
    channels, cells_x, cells_y, depth_time = sample_cells.shape
    local_modes = spectral_weight.shape[3]
    modes = spectral_weight.shape[4]
    rows = channels * cells_x * cells_y
    plane = [jnp.asarray(t) for t in host_halves(host_plane(owners, local_modes))]
    cross = [jnp.asarray(t) for t in host_halves(host_cross(count_x, count_y, cells_x, cells_y))]
    f32 = jnp.float32
    bf16 = jnp.bfloat16
    whole = pl.BlockSpec(memory_space=pltpu.VMEM)
    scalars = pl.BlockSpec(memory_space=pltpu.SMEM)
    stays = pl.BlockSpec(memory_space=pltpu.HBM)
    copies = pltpu.SemaphoreType.DMA
    vmem = pltpu.VMEM
    sent = (owners * 2 * local_modes, rows)
    cells = (rows, depth_time)
    spectrum = (2, channels, local_modes, modes)
    group = next(g for g in (4, 2, 1) if channels % g == 0)

    def held(shape):
        return pltpu.HBM(shape, f32)

    def trade(values):
        return lax.all_to_all(values, ("gy", "gx"), split_axis=0, concat_axis=0, tiled=True)

    def across(values, conjugate):
        def body(*refs):
            mode_kernel(conjugate, *refs)

        return pl.pallas_call(
            body,
            out_shape=(held(sent), held(spectrum)),
            in_specs=[whole, stays, whole, whole],
            out_specs=(stays, stays),
            scratch_shapes=[
                vmem(spectral_weight.shape, f32),
                vmem(sent, f32),
                vmem(spectrum, f32),
                vmem((2, 2 * channels * local_modes, owners * cells_x * cells_y // 2), f32),
                vmem((2, channels * local_modes, modes), f32),
                copies((5,)),
                copies,
                copies((2,)),
            ],
            compiler_params=params(),
            name="unmix_modes" if conjugate else "mix_modes",
        )(*near(values), *far(spectral_weight), *near(*cross))

    front = pl.pallas_call(
        front_kernel,
        out_shape=vmem(sent, f32),
        in_specs=[stays] * 3,
        out_specs=whole,
        scratch_shapes=[
            vmem(sample_cells.shape, f32),
            vmem(plane[0].shape, bf16),
            vmem(plane[1].shape, bf16),
            vmem(cells, f32),
            copies((2,)),
            copies((-(-channels // 4),)),
        ],
        compiler_params=params(),
        name="front",
    )(*far(sample_cells, *plane))
    got = trade(front)
    local, packed = pl.pallas_call(
        local_kernel,
        out_shape=(held(cells), held(cells)),
        in_specs=[whole, whole, scalars, scalars],
        out_specs=(whole, whole),
        scratch_shapes=[vmem(cells, f32)],
        compiler_params=params(),
        name="local_pre",
    )(*far(sample_cells, upstream), channel_weight, channel_bias)
    mixed, spectra = across(got, False)
    both_spectra = in_order(spectra)
    got, both_spectra = lax.optimization_barrier((trade(mixed), both_spectra))
    front, grad_pre = pl.pallas_call(
        middle_kernel,
        out_shape=(vmem(sent, f32), vmem(cells, f32)),
        in_specs=[whole, stays, stays, whole, whole],
        out_specs=(whole, whole),
        scratch_shapes=[vmem(cells, f32), vmem(cells, f32), copies((2, -(-rows // 128)))],
        compiler_params=params(),
        name="middle",
    )(*near(got), *far(local, packed), *near(*plane))
    got = trade(front)
    back, grad_spectra = across(got, True)
    both_grads = in_order(grad_spectra)
    got = trade(back)
    local_grad = pl.pallas_call(
        grads_kernel,
        out_shape=held(cells),
        in_specs=[whole, scalars],
        out_specs=whole,
        compiler_params=params(),
        name="local_grad",
    )(*far(grad_pre), channel_weight)
    spectral_grads = pl.pallas_call(
        outer_kernel,
        out_shape=held(spectral_weight.shape),
        grid=(channels // group,),
        in_specs=[whole] * 4,
        out_specs=pl.BlockSpec((2, group, channels, local_modes, modes), lambda i: (0, i, 0, 0, 0)),
        compiler_params=params(),
        name="outer",
    )(*far(*both_spectra), *near(*both_grads))
    cell_grad = pl.pallas_call(
        last_kernel,
        out_shape=held(sample_cells.shape),
        in_specs=[whole] * 4,
        out_specs=stays,
        scratch_shapes=[vmem(cells, f32), vmem(sample_cells.shape, f32), copies((-(-channels // 4),))],
        compiler_params=params(),
        name="last",
    )(*near(got, local_grad, *plane))
    return (cell_grad[None], spectral_grads)


def solution(mesh):
    placed = (
        P("dp", None, "gx", "gy", None),
        P("dp", None, "gx", "gy", None),
        P(None, None, None, ("gx", "gy"), None),
        P(),
        P(),
    )

    def on_any(*args):
        _, channels, cells_x, cells_y, _ = args[0].shape
        fits = args[2].shape[3] == 8 and args[2].shape[4] == 2 * LANES and KX * KY == 2 * LANES and cells_x * cells_y == LANES // 4
        fits = fits and channels % 20 == 0 and args[2].shape[3] == KT and KZ * KT == 16 * 8 and lax.axis_size("dp") == 2
        fits = fits and lax.axis_size("gx") == 4 and lax.axis_size("gy") == 4 and cells_y * 4 == KY
        return on_tiles(*args) if fits else on_device(*args)

    return jax.shard_map(
        on_any,
        mesh=mesh,
        in_specs=placed,
        out_specs=(P("dp", None, "gx", "gy", None), P(None, None, None, ("gx", "gy"), None)),
        check_vma=False,
    )
```

```python
import math

import jax
import jax.numpy as jnp
import numpy as np
from jax import lax
from jax.experimental import pallas as pl
from jax.experimental.pallas import tpu as pltpu
from jax.sharding import PartitionSpec as P

NZ = 32
NT = 16
KX = 16
KY = 16
KZ = 16
KT = 8


highest = lax.Precision.HIGHEST


def gelu_slope(values):
    return (
        0.5 * (1.0 + lax.erf(values * 0.7071067811865476))
        + values * jnp.exp(-0.5 * values * values) * 0.3989422804014327
    )


def signed_freq(number, kept_count):
    return jnp.where(number < kept_count // 2, number, number - kept_count)


def line_table(length, kept_count):
    positions = jnp.arange(length, dtype=jnp.int32)
    frequency = signed_freq(jnp.arange(kept_count, dtype=jnp.int32), kept_count)
    phases = positions[:, None] * frequency[None, :] % length
    angles = phases.astype(jnp.float32) * (-2.0 * math.pi / length)
    return jnp.stack([jnp.cos(angles), jnp.sin(angles)]) / math.sqrt(length)


def block_table(length, kept_count):
    table = line_table(length, kept_count)
    upper = jnp.stack([table[0], table[1]], axis=1)
    lower = jnp.stack([-table[1], table[0]], axis=1)
    return jnp.stack([upper, lower]).reshape(2 * length, 2 * kept_count)


def plane_table(mode_index):
    row_index = jnp.arange(NZ * NT, dtype=jnp.int32)
    depth = row_index // NT
    time_step = row_index % NT
    depth_freq = signed_freq(mode_index // KT, KZ)
    time_freq = signed_freq(mode_index % KT, KT)
    fraction = (depth[:, None] * depth_freq[None, :] % NZ).astype(jnp.float32) / NZ
    fraction = fraction + (time_step[:, None] * time_freq[None, :] % NT).astype(jnp.float32) / NT
    angles = fraction * (-2.0 * math.pi)
    table = jnp.stack([jnp.cos(angles), jnp.sin(angles)]) / math.sqrt(NZ * NT)
    return jnp.moveaxis(table, 0, -1).reshape(NZ * NT, -1)


def line_forward(data, block):
    return jnp.einsum("mpr,pk->mkr", data, block, precision=highest)


def line_adjoint(data, block):
    return jnp.einsum("mkr,pk->mpr", data, block, precision=highest)


def plane_front(real_field, planar, form):
    coeffs = jnp.einsum("cxyn,nk->" + form, real_field, planar, precision=highest)
    return coeffs.reshape(KZ * KT, 2, -1)


def plane_back(stacked, planar, form, first_cells, second_cells, channels):
    rows = stacked.reshape(-1, first_cells, second_cells, channels)
    return jnp.einsum(form + ",nk->cxyn", rows, planar, precision=highest)


def swap_inner(data, first, second, channels):
    leading = data.shape[0]
    moved = jnp.transpose(data.reshape(leading, 2, first, second, channels), (0, 1, 3, 2, 4))
    return moved.reshape(leading, 2, -1)


def mode_mix(weight, spectrum):

    def single(left_arg, right_arg):
        return jnp.einsum("imn,iomn->omn", left_arg, right_arg, precision=highest)

    real_part = single(spectrum[0], weight[0]) - single(spectrum[1], weight[1])
    imag_part = single(spectrum[1], weight[0]) + single(spectrum[0], weight[1])
    return jnp.stack([real_part, imag_part])


def mode_unmix(weight, spectrum):

    def single(left_arg, right_arg):
        return jnp.einsum("omn,iomn->imn", left_arg, right_arg, precision=highest)

    real_part = single(spectrum[0], weight[0]) + single(spectrum[1], weight[1])
    imag_part = single(spectrum[1], weight[0]) - single(spectrum[0], weight[1])
    return jnp.stack([real_part, imag_part])


def mode_outer(grad_spectrum, spectrum):

    def single(left_arg, right_arg):
        return jnp.einsum("omn,imn->iomn", left_arg, right_arg, precision=highest)

    real_part = single(grad_spectrum[0], spectrum[0]) + single(grad_spectrum[1], spectrum[1])
    imag_part = single(grad_spectrum[1], spectrum[0]) - single(grad_spectrum[0], spectrum[1])
    return jnp.stack([real_part, imag_part])


def on_device(cell_values, cotangent, spectral_weight, channel_weight, channel_bias):
    sample_cells = cell_values[0]
    upstream = cotangent[0]
    count_x = lax.axis_size("gx")
    count_y = lax.axis_size("gy")
    channels, cells_x, cells_y, depth_time = sample_cells.shape
    length_x = count_x * cells_x
    length_y = count_y * cells_y
    local_modes = KZ * KT // (count_x * count_y)
    block_x = block_table(length_x, KX)
    block_y = block_table(length_y, KY)
    column = jnp.arange(KZ * KT, dtype=jnp.int32)

    def to_spectrum(last):
        shaped = jnp.transpose(last.reshape(local_modes, 2, KX, KY, channels), (1, 4, 0, 3, 2))
        return shaped.reshape(2, channels, local_modes, KY * KX)

    def from_spectrum(spectrum):
        shaped = spectrum.reshape(2, channels, local_modes, KY, KX)
        return jnp.transpose(shaped, (2, 0, 4, 3, 1)).reshape(local_modes, 2 * KX, KY * channels)

    planar = plane_table(column)

    def forward(real_field):
        gathered = lax.all_to_all(
            plane_front(real_field, planar, "kyxc"),
            ("gx", "gy"),
            split_axis=0,
            concat_axis=2,
            tiled=True,
        )
        arranged = gathered.reshape(local_modes, 2, count_x, count_y, cells_y, cells_x * channels)
        arranged = jnp.transpose(arranged, (0, 1, 3, 4, 2, 5)).reshape(
            local_modes, 2 * length_y, length_x * channels
        )
        along_y = line_forward(arranged, block_y)
        along_y = swap_inner(along_y, KY, length_x, channels).reshape(
            local_modes, 2 * length_x, KY * channels
        )
        along_x = line_forward(along_y, block_x)
        return to_spectrum(along_x)

    def inverse(spectrum):
        back_x = line_adjoint(from_spectrum(spectrum), block_x)
        back_x = swap_inner(back_x, length_x, KY, channels).reshape(
            local_modes, 2 * KY, length_x * channels
        )
        back_y = line_adjoint(back_x, block_y)
        ordered = back_y.reshape(local_modes, 2, count_y, cells_y, count_x, cells_x * channels)
        ordered = jnp.transpose(ordered, (0, 1, 4, 2, 3, 5)).reshape(local_modes, 2, -1)
        spread = lax.all_to_all(ordered, ("gx", "gy"), split_axis=2, concat_axis=0, tiled=True)
        return plane_back(spread, planar, "kyxc", cells_y, cells_x, channels)

    spectra = forward(sample_cells)
    mixed = mode_mix(spectral_weight, spectra)
    pre_act = jnp.einsum("oi,ixyn->oxyn", channel_weight, sample_cells, precision=highest)
    pre_act = pre_act + channel_bias[:, None, None, None] + inverse(mixed)
    grad_pre = upstream * gelu_slope(pre_act)
    grad_spectra = forward(grad_pre)
    back_modes = mode_unmix(spectral_weight, grad_spectra)
    cell_grad = jnp.einsum("oi,oxyn->ixyn", channel_weight, grad_pre, precision=highest) + inverse(
        back_modes
    )
    spectral_grads = lax.psum(mode_outer(grad_spectra, spectra), "dp")
    return (cell_grad[None], spectral_grads)


LANES = 128
VMEM_LIMIT = 24 * 1024 * 1024


def params():
    return pltpu.CompilerParams(vmem_limit_bytes=VMEM_LIMIT)


def halves(values):
    upper = values.astype(jnp.bfloat16)
    return upper, (values - upper.astype(jnp.float32)).astype(jnp.bfloat16)


def host_halves(table):
    upper = table.astype(jnp.bfloat16)
    lower = (table - upper.astype(np.float64)).astype(jnp.bfloat16)
    return upper, lower


def host_freq(number, kept_count):
    return np.where(number < kept_count // 2, number, number - kept_count)


def host_plane(owners, local_modes):
    mode = np.arange(owners * local_modes)
    cell = np.arange(NZ * NT // 2)
    turns = np.outer(host_freq(mode // KT, KZ), cell // NT) / NZ
    turns = turns + np.outer(host_freq(mode % KT, KT), cell % NT) / NT
    angles = 2.0 * np.pi * turns
    table = np.stack([np.cos(angles), -np.sin(angles)]) / np.sqrt(NZ * NT)
    table = table.reshape(2, owners // 2, 2, local_modes, NZ * NT // 2)
    return table.transpose(2, 1, 0, 3, 4).reshape(2, owners * local_modes, NZ * NT // 2)


def host_cross(count_x, count_y, cells_x, cells_y):
    length_x = count_x * cells_x
    length_y = count_y * cells_y
    row = np.arange(length_x * length_y // 2)
    cell = row % (cells_x * cells_y)
    owner = row // (cells_x * cells_y)
    place_x = owner // (count_y // 2) * cells_x + cell // cells_y
    place_y = owner % (count_y // 2) * cells_y + cell % cells_y
    column = np.arange(KY // 2 * KX)
    number_x = column % KX
    block = column // KX
    tables = []
    for number_y in (np.where(block % 2 == 0, block, block + 7), np.where(block % 2 == 1, block, block + 9)):
        turns = np.outer(place_x, host_freq(number_x, KX)) / length_x
        turns = turns + np.outer(place_y, host_freq(number_y, KY)) / length_y
        angles = 2.0 * np.pi * turns
        tables.append(np.concatenate([np.cos(angles), np.sin(angles)], axis=1))
    return np.stack(tables) / np.sqrt(length_x * length_y)


def product(left, right, left_dim, right_dim):
    dims = (((left_dim,), (right_dim,)), ((), ()))

    def single(one, other):
        return lax.dot_general(one, other, dims, preferred_element_type=jnp.float32)

    return single(left[0], right[0]) + (single(left[0], right[1]) + single(left[1], right[0]))


def swap_groups(parts):
    width = LANES // 4
    lane = lax.broadcasted_iota(jnp.int32, parts[0].shape, 1)
    low_half = lane < 2 * width
    low_quarter = lane % (2 * width) < width

    def trade(one, other, mask, shift):
        return (
            jnp.where(mask, one, pltpu.roll(other, shift, 1)),
            jnp.where(mask, pltpu.roll(one, LANES - shift, 1), other),
        )

    first, third = trade(parts[0], parts[2], low_half, 2 * width)
    second, fourth = trade(parts[1], parts[3], low_half, 2 * width)
    first, second = trade(first, second, low_quarter, width)
    third, fourth = trade(third, fourth, low_quarter, width)
    return first, second, third, fourth


def pack_rows(field_ref, rows_ref):
    channels, cells_x, cells_y, _ = field_ref.shape
    for channel in range(channels):
        for place in range(cells_x):
            row = (channel * cells_x + place) * cells_y
            rows_ref[row : row + cells_y, :] = field_ref[channel, place]


def start(source, target, semaphore):
    copy = pltpu.make_async_copy(source, target, semaphore)
    copy.start()
    return copy


def to_plane_modes(rows_ref, high_ref, low_ref, out_ref):
    half = rows_ref.shape[1] // 2
    block = out_ref.shape[0] // 16
    for parity in range(2):
        one, other = rows_ref[:, :half], rows_ref[:, half:]
        values = one - other if parity else one + other
        waves = product((high_ref[parity], low_ref[parity]), halves(values), 1, 1)
        for k in range(8):
            row = slot(2 * k + parity) * block
            out_ref[row : row + block, :] = waves[k * block : (k + 1) * block]


def from_plane_modes(got_ref, high_ref, low_ref):
    block = got_ref.shape[0] // 16
    waves = []
    for parity in range(2):
        rows = [slot(2 * k + parity) * block for k in range(8)]
        parts = [got_ref[row : row + block, :] for row in rows]
        waves.append(product(halves(jnp.concatenate(parts, axis=0)), (high_ref[parity], low_ref[parity]), 0, 0))
    return jnp.concatenate([waves[0] + waves[1], waves[0] - waves[1]], axis=1)


def slot(owner):
    return owner % 4 * 4 + owner // 4


def spans_of(channels, step):
    return [(first, min(first + step, channels)) for first in range(0, channels, step)]


def front_kernel(
    field_hbm, high_hbm, low_hbm, weight_hbm, out_ref, head_ref, field_ref, high_ref, low_ref, rows_ref, table_sems, field_sems, head_sem
):
    channels, cells_x, cells_y, _ = field_ref.shape
    cells = cells_x * cells_y
    pieces = []
    for first, last in spans_of(channels, 4):
        span = pl.ds(first, last - first)
        pieces.append(start(field_hbm.at[span], field_ref.at[span], field_sems.at[len(pieces)]))
        if first == 0:
            tables = [start(high_hbm, high_ref, table_sems.at[0]), start(low_hbm, low_ref, table_sems.at[1])]
    head = start(weight_hbm.at[:, :, pl.ds(0, head_ref.shape[2])], head_ref, head_sem)
    for piece, (first, last) in enumerate(spans_of(channels, 4)):
        pieces[piece].wait()
        for channel in range(first, last):
            for place in range(cells_x):
                row = channel * cells + place * cells_y
                rows_ref[row : row + cells_y, :] = field_ref[channel, place]
    for copy in tables:
        copy.wait()
    to_plane_modes(rows_ref, high_ref, low_ref, out_ref)
    head.wait()


def blocks_even(shape):
    return lax.broadcasted_iota(jnp.int32, shape, 1) // KX % 2 == 0


def in_ky_order(even, odd):
    mask = blocks_even(even.shape)
    low = jnp.where(mask, even, odd)
    high = jnp.where(mask, pltpu.roll(even, LANES - KX, 1), pltpu.roll(odd, KX, 1))
    return low, high


def by_ky_parity(low, high):
    mask = blocks_even(low.shape)
    even = jnp.where(mask, low, pltpu.roll(high, KX, 1))
    odd = jnp.where(mask, pltpu.roll(high, LANES - KX, 1), low)
    return even, odd


def mode_kernel(
    head_ref,
    got_ref,
    weight_hbm,
    high_ref,
    low_ref,
    out_hbm,
    spectra_hbm,
    weight_ref,
    out_ref,
    spectra_ref,
    field_ref,
    mixed_ref,
    weight_sems,
    spectra_sem,
    out_sems,
):
    _, channels, local_modes, modes = spectra_ref.shape
    conjugate = head_ref is None
    chunk = channels // weight_sems.shape[0]
    weight_copies = []
    for k in range(weight_sems.shape[0]):
        if k == 0 and not conjugate:
            continue
        span = pl.ds(k * chunk, chunk)
        place = (slice(None), span) if conjugate else (slice(None), slice(None), span)
        weight_copies.append(start(weight_hbm.at[place], weight_ref.at[place], weight_sems.at[k]))
    rows = channels * local_modes
    block = 2 * local_modes
    quads = got_ref.shape[0] // (4 * block)
    groups = channels // 4

    def owner_rows(quad, j):
        first = slot(4 * quad + j) * block
        return slice(first, first + block)

    for pair in range(quads // 2):
        for group in range(groups):
            lanes = slice(group * LANES, (group + 1) * LANES)
            near_half, far_half = [
                [got_ref[owner_rows(2 * pair + i, 2 * half + j), lanes] for i in range(2) for j in range(2)] for half in range(2)
            ]
            sums = [one + other for one, other in zip(near_half, far_half)]
            gaps = [one - other for one, other in zip(near_half, far_half)]
            for parity, parts in enumerate((sums, gaps)):
                for m, part in enumerate(swap_groups(parts)):
                    row = (4 * group + m) * local_modes
                    for side in range(2):
                        field_ref[
                            parity, side * rows + row : side * rows + row + local_modes, pair * LANES : (pair + 1) * LANES
                        ] = part[side * local_modes : (side + 1) * local_modes]
    real = []
    imag = []
    for parity in range(2):
        waves = product(halves(field_ref[parity]), (high_ref[parity], low_ref[parity]), 1, 0)
        real.append(waves[:rows, :LANES] + waves[rows:, LANES:])
        imag.append(waves[rows:, :LANES] - waves[:rows, LANES:])
    for part, pair in enumerate((real, imag)):
        for k, values in enumerate(in_ky_order(*pair)):
            spectra_ref[part, :, :, k * LANES : (k + 1) * LANES] = values.reshape(channels, local_modes, LANES)
    spectra_copy = start(spectra_ref, spectra_hbm, spectra_sem)
    for part in range(weight_sems.shape[0] * 2):
        first_lane = part % 2 * LANES
        first_result = part // 2 * chunk
        span = slice(first_lane, first_lane + LANES)
        ins = [(spectra_ref[0, c, :, span], spectra_ref[1, c, :, span]) for c in range(channels)]
        if first_lane == 0 and (conjugate or first_result > 0):
            weight_copies[part // 2 - (not conjugate)].wait()
        mixing_ref = weight_ref if conjugate or first_result > 0 else head_ref

        def one(step, carry, span=span, ins=ins, first_result=first_result, mixing_ref=mixing_ref):
            result = first_result + step
            total_real = jnp.zeros((local_modes, LANES), jnp.float32)
            total_imag = jnp.zeros((local_modes, LANES), jnp.float32)
            for c, (in_real, in_imag) in enumerate(ins):
                if conjugate:
                    w_real = mixing_ref[0, result, c, :, span]
                    w_imag = mixing_ref[1, result, c, :, span]
                    total_real = total_real + (in_real * w_real + in_imag * w_imag)
                    total_imag = total_imag + (in_imag * w_real - in_real * w_imag)
                else:
                    w_real = mixing_ref[0, c, result, :, span]
                    w_imag = mixing_ref[1, c, result, :, span]
                    total_real = total_real + (in_real * w_real - in_imag * w_imag)
                    total_imag = total_imag + (in_imag * w_real + in_real * w_imag)
            row = pl.multiple_of(result * local_modes, local_modes)
            mixed_ref[0, pl.ds(row, local_modes), span] = total_real
            mixed_ref[1, pl.ds(row, local_modes), span] = total_imag
            return carry

        lax.fori_loop(0, chunk, one, 0, unroll=True)
    out_copies = []
    for first, last in spans_of(groups, -(-groups // 2)):
        begin, end = 4 * first * local_modes, 4 * last * local_modes
        reals = by_ky_parity(mixed_ref[0, begin:end, :LANES], mixed_ref[0, begin:end, LANES:])
        imags = by_ky_parity(mixed_ref[1, begin:end, :LANES], mixed_ref[1, begin:end, LANES:])
        for parity in range(2):
            left = jnp.concatenate([reals[parity], imags[parity]], axis=0)
            right = jnp.concatenate([-imags[parity], reals[parity]], axis=0)
            both = halves(jnp.concatenate([left, right], axis=1))
            field_ref[parity, 2 * begin : 2 * end, :] = product(both, (high_ref[parity], low_ref[parity]), 1, 1)
        for pair in range(quads // 2):
            for group in range(first, last):
                lanes = slice(group * LANES, (group + 1) * LANES)
                for side in range(2):
                    base = 2 * begin + side * (end - begin) + 4 * (group - first) * local_modes
                    sums, gaps = [
                        swap_groups(
                            [
                                field_ref[
                                    parity,
                                    base + m * local_modes : base + (m + 1) * local_modes,
                                    pair * LANES : (pair + 1) * LANES,
                                ]
                                for m in range(4)
                            ]
                        )
                        for parity in range(2)
                    ]
                    for k in range(4):
                        owner = 4 * (2 * pair + k // 2) + k % 2
                        row = slot(owner) * block + side * local_modes
                        other = slot(owner + 2) * block + side * local_modes
                        out_ref[row : row + local_modes, lanes] = sums[k] + gaps[k]
                        out_ref[other : other + local_modes, lanes] = sums[k] - gaps[k]
        place = (slice(None), pl.ds(first * LANES, (last - first) * LANES))
        out_copies.append(start(out_ref.at[place], out_hbm.at[place], out_sems.at[len(out_copies)]))
    spectra_copy.wait()
    for copy in out_copies:
        copy.wait()


def channel_sums(transposed, rows_ref, weight_ref, bias_ref, out_ref, channels):
    height = rows_ref.shape[0] // channels
    for lane in range(0, rows_ref.shape[1], LANES):
        span = slice(lane, lane + LANES)

        def one(step, carry, span=span):
            ins = [rows_ref[pl.ds(pl.multiple_of(i * height + step * 8, 8), 8), span] for i in range(channels)]
            for o in range(channels):
                total = None
                for i in range(channels):
                    factor = weight_ref[i, o] if transposed else weight_ref[o, i]
                    term = ins[i] * factor
                    total = term if total is None else total + term
                if bias_ref is not None:
                    total = total + bias_ref[o]
                out_ref[pl.ds(pl.multiple_of(o * height + step * 8, 8), 8), span] = total
            return carry

        lax.fori_loop(0, height // 8, one, 0)


def local_kernel(field_ref, upstream_ref, weight_ref, bias_ref, out_ref, packed_ref, rows_ref):
    pack_rows(field_ref, rows_ref)
    pack_rows(upstream_ref, packed_ref)
    channel_sums(False, rows_ref, weight_ref, bias_ref, out_ref, field_ref.shape[0])


def middle_kernel(got_ref, local_hbm, upstream_hbm, high_ref, low_ref, out_ref, grad_ref, local_ref, upstream_ref, sems):
    spans = [pl.ds(first, last - first) for first, last in spans_of(local_ref.shape[0], 128)]
    copies = [
        (start(local_hbm.at[span], local_ref.at[span], sems.at[0, k]), start(upstream_hbm.at[span], upstream_ref.at[span], sems.at[1, k]))
        for k, span in enumerate(spans)
    ]
    grad_ref[...] = from_plane_modes(got_ref, high_ref, low_ref)
    for k, span in enumerate(spans):
        rows = slice(span.start, span.start + span.size)
        for copy in copies[k]:
            copy.wait()
        grad_ref[rows, :] = upstream_ref[rows, :] * gelu_slope(grad_ref[rows, :] + local_ref[rows, :])
    to_plane_modes(grad_ref, high_ref, low_ref, out_ref)


def grads_kernel(rows_ref, weight_ref, out_ref):
    channel_sums(True, rows_ref, weight_ref, None, out_ref, weight_ref.shape[0])


def last_kernel(got_ref, local_ref, high_ref, low_ref, out_hbm, rows_ref, out_ref, sems):
    channels, cells_x, cells_y, _ = out_ref.shape
    cells = cells_x * cells_y
    rows_ref[...] = from_plane_modes(got_ref, high_ref, low_ref)
    leaving = []
    for first, last in spans_of(channels, 4):
        rows = slice(first * cells, last * cells)
        rows_ref[rows, :] = rows_ref[rows, :] + local_ref[rows, :]
        for channel in range(first, last):
            for place in range(cells_x):
                row = channel * cells + place * cells_y
                out_ref[channel, place] = rows_ref[row : row + cells_y, :]
        span = pl.ds(first, last - first)
        leaving.append(start(out_ref.at[span], out_hbm.at[span], sems.at[len(leaving)]))
    for copy in leaving:
        copy.wait()


def outer_kernel(first_spectra, second_spectra, first_grads, second_grads, out_ref):
    _, channels, local_modes, modes = first_spectra.shape
    sources = out_ref.shape[1]
    pairs = ((first_spectra, first_grads), (second_spectra, second_grads))

    def one(step, carry):
        source = pl.program_id(0) * sources + step
        for lane in range(0, modes, LANES):
            span = slice(lane, lane + LANES)
            ins = [(spectra[0, source, :, span], spectra[1, source, :, span]) for spectra, _ in pairs]
            for o in range(channels):
                total_real = None
                total_imag = None
                for (_, grads), (in_real, in_imag) in zip(pairs, ins):
                    g_real = grads[0, o, :, span]
                    g_imag = grads[1, o, :, span]
                    real = g_real * in_real + g_imag * in_imag
                    imag = g_imag * in_real - g_real * in_imag
                    total_real = real if total_real is None else total_real + real
                    total_imag = imag if total_imag is None else total_imag + imag
                out_ref[0, step, o, :, span] = total_real
                out_ref[1, step, o, :, span] = total_imag
        return carry

    lax.fori_loop(0, sources, one, 0)


def in_order(own):
    other = lax.ppermute(own, "dp", [(0, 1), (1, 0)])
    first = lax.axis_index("dp") == 0
    return jnp.where(first, own, other), jnp.where(first, other, own)


def far(*values):
    return [pltpu.with_memory_space_constraint(v, pltpu.HBM) for v in values]


def near(*values):
    return [pltpu.with_memory_space_constraint(v, pltpu.VMEM) for v in values]


def on_tiles(cell_values, cotangent, spectral_weight, channel_weight, channel_bias):
    sample_cells = cell_values[0]
    upstream = cotangent[0]
    count_x = lax.axis_size("gx")
    count_y = lax.axis_size("gy")
    owners = count_x * count_y
    channels, cells_x, cells_y, depth_time = sample_cells.shape
    local_modes = spectral_weight.shape[3]
    modes = spectral_weight.shape[4]
    rows = channels * cells_x * cells_y
    plane = [jnp.asarray(t) for t in host_halves(host_plane(owners, local_modes))]
    cross = [jnp.asarray(t) for t in host_halves(host_cross(count_x, count_y, cells_x, cells_y))]
    f32 = jnp.float32
    bf16 = jnp.bfloat16
    whole = pl.BlockSpec(memory_space=pltpu.VMEM)
    scalars = pl.BlockSpec(memory_space=pltpu.SMEM)
    stays = pl.BlockSpec(memory_space=pltpu.HBM)
    copies = pltpu.SemaphoreType.DMA
    vmem = pltpu.VMEM
    sent = (owners * 2 * local_modes, rows)
    cells = (rows, depth_time)
    spectrum = (2, channels, local_modes, modes)
    group = next(g for g in (4, 2, 1) if channels % g == 0)

    def held(shape):
        return pltpu.HBM(shape, f32)

    def trade(values):
        return lax.all_to_all(values, ("gy", "gx"), split_axis=0, concat_axis=0, tiled=True)

    def across(values, *head):
        conjugate = not head

        def body(*refs):
            mode_kernel(*((None,) if conjugate else ()), *refs)

        return pl.pallas_call(
            body,
            out_shape=(held(sent), held(spectrum)),
            in_specs=[*[whole] * len(head), whole, stays, whole, whole],
            out_specs=(stays, stays),
            scratch_shapes=[
                vmem(spectral_weight.shape, f32),
                vmem(sent, f32),
                vmem(spectrum, f32),
                vmem((2, 2 * channels * local_modes, owners * cells_x * cells_y // 2), f32),
                vmem((2, channels * local_modes, modes), f32),
                copies((5,)),
                copies,
                copies((2,)),
            ],
            compiler_params=params(),
            name="unmix_modes" if conjugate else "mix_modes",
        )(*near(*head, values), *far(spectral_weight), *near(*cross))

    front, head = pl.pallas_call(
        front_kernel,
        out_shape=(vmem(sent, f32), vmem((2, channels, channels // 5, local_modes, modes), f32)),
        in_specs=[stays] * 4,
        out_specs=(whole, whole),
        scratch_shapes=[
            vmem(sample_cells.shape, f32),
            vmem(plane[0].shape, bf16),
            vmem(plane[1].shape, bf16),
            vmem(cells, f32),
            copies((2,)),
            copies((-(-channels // 4),)),
            copies,
        ],
        compiler_params=params(),
        name="front",
    )(*far(sample_cells, *plane, spectral_weight))
    got = trade(front)
    local, packed = pl.pallas_call(
        local_kernel,
        out_shape=(held(cells), held(cells)),
        in_specs=[whole, whole, scalars, scalars],
        out_specs=(whole, whole),
        scratch_shapes=[vmem(cells, f32)],
        compiler_params=params(),
        name="local_pre",
    )(*far(sample_cells, upstream), channel_weight, channel_bias)
    mixed, spectra = across(got, head)
    both_spectra = in_order(spectra)
    got, both_spectra = lax.optimization_barrier((trade(mixed), both_spectra))
    front, grad_pre = pl.pallas_call(
        middle_kernel,
        out_shape=(vmem(sent, f32), vmem(cells, f32)),
        in_specs=[whole, stays, stays, whole, whole],
        out_specs=(whole, whole),
        scratch_shapes=[vmem(cells, f32), vmem(cells, f32), copies((2, -(-rows // 128)))],
        compiler_params=params(),
        name="middle",
    )(*near(got), *far(local, packed), *near(*plane))
    got = trade(front)
    back, grad_spectra = across(got)
    both_grads = in_order(grad_spectra)
    got = trade(back)
    local_grad = pl.pallas_call(
        grads_kernel,
        out_shape=held(cells),
        in_specs=[whole, scalars],
        out_specs=whole,
        compiler_params=params(),
        name="local_grad",
    )(*far(grad_pre), channel_weight)
    spectral_grads = pl.pallas_call(
        outer_kernel,
        out_shape=held(spectral_weight.shape),
        grid=(channels // group,),
        in_specs=[whole] * 4,
        out_specs=pl.BlockSpec((2, group, channels, local_modes, modes), lambda i: (0, i, 0, 0, 0)),
        compiler_params=params(),
        name="outer",
    )(*far(*both_spectra), *near(*both_grads))
    cell_grad = pl.pallas_call(
        last_kernel,
        out_shape=held(sample_cells.shape),
        in_specs=[whole] * 4,
        out_specs=stays,
        scratch_shapes=[vmem(cells, f32), vmem(sample_cells.shape, f32), copies((-(-channels // 4),))],
        compiler_params=params(),
        name="last",
    )(*near(got, local_grad, *plane))
    return (cell_grad[None], spectral_grads)


def solution(mesh):
    placed = (
        P("dp", None, "gx", "gy", None),
        P("dp", None, "gx", "gy", None),
        P(None, None, None, ("gx", "gy"), None),
        P(),
        P(),
    )

    def on_any(*args):
        _, channels, cells_x, cells_y, _ = args[0].shape
        fits = args[2].shape[3] == 8 and args[2].shape[4] == 2 * LANES and KX * KY == 2 * LANES and cells_x * cells_y == LANES // 4
        fits = fits and channels % 20 == 0 and args[2].shape[3] == KT and KZ * KT == 16 * 8 and lax.axis_size("dp") == 2
        fits = fits and lax.axis_size("gx") == 4 and lax.axis_size("gy") == 4 and cells_y * 4 == KY
        return on_tiles(*args) if fits else on_device(*args)

    return jax.shard_map(
        on_any,
        mesh=mesh,
        in_specs=placed,
        out_specs=(P("dp", None, "gx", "gy", None), P(None, None, None, ("gx", "gy"), None)),
        check_vma=False,
    )
```

```python
import math

import jax
import jax.numpy as jnp
import numpy as np
from jax import lax
from jax.experimental import pallas as pl
from jax.experimental.pallas import tpu as pltpu
from jax.sharding import PartitionSpec as P

NZ = 32
NT = 16
KX = 16
KY = 16
KZ = 16
KT = 8


highest = lax.Precision.HIGHEST


def gelu_slope(values):
    return (
        0.5 * (1.0 + lax.erf(values * 0.7071067811865476))
        + values * jnp.exp(-0.5 * values * values) * 0.3989422804014327
    )


def signed_freq(number, kept_count):
    return jnp.where(number < kept_count // 2, number, number - kept_count)


def line_table(length, kept_count):
    positions = jnp.arange(length, dtype=jnp.int32)
    frequency = signed_freq(jnp.arange(kept_count, dtype=jnp.int32), kept_count)
    phases = positions[:, None] * frequency[None, :] % length
    angles = phases.astype(jnp.float32) * (-2.0 * math.pi / length)
    return jnp.stack([jnp.cos(angles), jnp.sin(angles)]) / math.sqrt(length)


def block_table(length, kept_count):
    table = line_table(length, kept_count)
    upper = jnp.stack([table[0], table[1]], axis=1)
    lower = jnp.stack([-table[1], table[0]], axis=1)
    return jnp.stack([upper, lower]).reshape(2 * length, 2 * kept_count)


def plane_table(mode_index):
    row_index = jnp.arange(NZ * NT, dtype=jnp.int32)
    depth = row_index // NT
    time_step = row_index % NT
    depth_freq = signed_freq(mode_index // KT, KZ)
    time_freq = signed_freq(mode_index % KT, KT)
    fraction = (depth[:, None] * depth_freq[None, :] % NZ).astype(jnp.float32) / NZ
    fraction = fraction + (time_step[:, None] * time_freq[None, :] % NT).astype(jnp.float32) / NT
    angles = fraction * (-2.0 * math.pi)
    table = jnp.stack([jnp.cos(angles), jnp.sin(angles)]) / math.sqrt(NZ * NT)
    return jnp.moveaxis(table, 0, -1).reshape(NZ * NT, -1)


def line_forward(data, block):
    return jnp.einsum("mpr,pk->mkr", data, block, precision=highest)


def line_adjoint(data, block):
    return jnp.einsum("mkr,pk->mpr", data, block, precision=highest)


def plane_front(real_field, planar, form):
    coeffs = jnp.einsum("cxyn,nk->" + form, real_field, planar, precision=highest)
    return coeffs.reshape(KZ * KT, 2, -1)


def plane_back(stacked, planar, form, first_cells, second_cells, channels):
    rows = stacked.reshape(-1, first_cells, second_cells, channels)
    return jnp.einsum(form + ",nk->cxyn", rows, planar, precision=highest)


def swap_inner(data, first, second, channels):
    leading = data.shape[0]
    moved = jnp.transpose(data.reshape(leading, 2, first, second, channels), (0, 1, 3, 2, 4))
    return moved.reshape(leading, 2, -1)


def mode_mix(weight, spectrum):

    def single(left_arg, right_arg):
        return jnp.einsum("imn,iomn->omn", left_arg, right_arg, precision=highest)

    real_part = single(spectrum[0], weight[0]) - single(spectrum[1], weight[1])
    imag_part = single(spectrum[1], weight[0]) + single(spectrum[0], weight[1])
    return jnp.stack([real_part, imag_part])


def mode_unmix(weight, spectrum):

    def single(left_arg, right_arg):
        return jnp.einsum("omn,iomn->imn", left_arg, right_arg, precision=highest)

    real_part = single(spectrum[0], weight[0]) + single(spectrum[1], weight[1])
    imag_part = single(spectrum[1], weight[0]) - single(spectrum[0], weight[1])
    return jnp.stack([real_part, imag_part])


def mode_outer(grad_spectrum, spectrum):

    def single(left_arg, right_arg):
        return jnp.einsum("omn,imn->iomn", left_arg, right_arg, precision=highest)

    real_part = single(grad_spectrum[0], spectrum[0]) + single(grad_spectrum[1], spectrum[1])
    imag_part = single(grad_spectrum[1], spectrum[0]) - single(grad_spectrum[0], spectrum[1])
    return jnp.stack([real_part, imag_part])


def on_device(cell_values, cotangent, spectral_weight, channel_weight, channel_bias):
    sample_cells = cell_values[0]
    upstream = cotangent[0]
    count_x = lax.axis_size("gx")
    count_y = lax.axis_size("gy")
    channels, cells_x, cells_y, depth_time = sample_cells.shape
    length_x = count_x * cells_x
    length_y = count_y * cells_y
    local_modes = KZ * KT // (count_x * count_y)
    block_x = block_table(length_x, KX)
    block_y = block_table(length_y, KY)
    column = jnp.arange(KZ * KT, dtype=jnp.int32)

    def to_spectrum(last):
        shaped = jnp.transpose(last.reshape(local_modes, 2, KX, KY, channels), (1, 4, 0, 3, 2))
        return shaped.reshape(2, channels, local_modes, KY * KX)

    def from_spectrum(spectrum):
        shaped = spectrum.reshape(2, channels, local_modes, KY, KX)
        return jnp.transpose(shaped, (2, 0, 4, 3, 1)).reshape(local_modes, 2 * KX, KY * channels)

    planar = plane_table(column)

    def forward(real_field):
        gathered = lax.all_to_all(
            plane_front(real_field, planar, "kyxc"),
            ("gx", "gy"),
            split_axis=0,
            concat_axis=2,
            tiled=True,
        )
        arranged = gathered.reshape(local_modes, 2, count_x, count_y, cells_y, cells_x * channels)
        arranged = jnp.transpose(arranged, (0, 1, 3, 4, 2, 5)).reshape(
            local_modes, 2 * length_y, length_x * channels
        )
        along_y = line_forward(arranged, block_y)
        along_y = swap_inner(along_y, KY, length_x, channels).reshape(
            local_modes, 2 * length_x, KY * channels
        )
        along_x = line_forward(along_y, block_x)
        return to_spectrum(along_x)

    def inverse(spectrum):
        back_x = line_adjoint(from_spectrum(spectrum), block_x)
        back_x = swap_inner(back_x, length_x, KY, channels).reshape(
            local_modes, 2 * KY, length_x * channels
        )
        back_y = line_adjoint(back_x, block_y)
        ordered = back_y.reshape(local_modes, 2, count_y, cells_y, count_x, cells_x * channels)
        ordered = jnp.transpose(ordered, (0, 1, 4, 2, 3, 5)).reshape(local_modes, 2, -1)
        spread = lax.all_to_all(ordered, ("gx", "gy"), split_axis=2, concat_axis=0, tiled=True)
        return plane_back(spread, planar, "kyxc", cells_y, cells_x, channels)

    spectra = forward(sample_cells)
    mixed = mode_mix(spectral_weight, spectra)
    pre_act = jnp.einsum("oi,ixyn->oxyn", channel_weight, sample_cells, precision=highest)
    pre_act = pre_act + channel_bias[:, None, None, None] + inverse(mixed)
    grad_pre = upstream * gelu_slope(pre_act)
    grad_spectra = forward(grad_pre)
    back_modes = mode_unmix(spectral_weight, grad_spectra)
    cell_grad = jnp.einsum("oi,oxyn->ixyn", channel_weight, grad_pre, precision=highest) + inverse(
        back_modes
    )
    spectral_grads = lax.psum(mode_outer(grad_spectra, spectra), "dp")
    return (cell_grad[None], spectral_grads)


LANES = 128
VMEM_LIMIT = 24 * 1024 * 1024


def params():
    return pltpu.CompilerParams(vmem_limit_bytes=VMEM_LIMIT)


def halves(values):
    upper = values.astype(jnp.bfloat16)
    return upper, (values - upper.astype(jnp.float32)).astype(jnp.bfloat16)


def host_halves(table):
    upper = table.astype(jnp.bfloat16)
    lower = (table - upper.astype(np.float64)).astype(jnp.bfloat16)
    return upper, lower


def host_freq(number, kept_count):
    return np.where(number < kept_count // 2, number, number - kept_count)


def host_plane(owners, local_modes):
    mode = np.arange(owners * local_modes)
    cell = np.arange(NZ * NT // 2)
    turns = np.outer(host_freq(mode // KT, KZ), cell // NT) / NZ
    turns = turns + np.outer(host_freq(mode % KT, KT), cell % NT) / NT
    angles = 2.0 * np.pi * turns
    table = np.stack([np.cos(angles), -np.sin(angles)]) / np.sqrt(NZ * NT)
    table = table.reshape(2, owners // 2, 2, local_modes, NZ * NT // 2)
    return table.transpose(2, 1, 0, 3, 4).reshape(2, owners * local_modes, NZ * NT // 2)


def host_cross(count_x, count_y, cells_x, cells_y):
    length_x = count_x * cells_x
    length_y = count_y * cells_y
    row = np.arange(length_x * length_y // 2)
    cell = row % (cells_x * cells_y)
    owner = row // (cells_x * cells_y)
    place_x = owner // (count_y // 2) * cells_x + cell // cells_y
    place_y = owner % (count_y // 2) * cells_y + cell % cells_y
    column = np.arange(KY // 2 * KX)
    number_x = column % KX
    block = column // KX
    tables = []
    for number_y in (np.where(block % 2 == 0, block, block + 7), np.where(block % 2 == 1, block, block + 9)):
        turns = np.outer(place_x, host_freq(number_x, KX)) / length_x
        turns = turns + np.outer(place_y, host_freq(number_y, KY)) / length_y
        angles = 2.0 * np.pi * turns
        tables.append(np.concatenate([np.cos(angles), np.sin(angles)], axis=1))
    return np.stack(tables) / np.sqrt(length_x * length_y)


def product(left, right, left_dim, right_dim):
    dims = (((left_dim,), (right_dim,)), ((), ()))

    def single(one, other):
        return lax.dot_general(one, other, dims, preferred_element_type=jnp.float32)

    return single(left[0], right[0]) + (single(left[0], right[1]) + single(left[1], right[0]))


def swap_groups(parts):
    width = LANES // 4
    lane = lax.broadcasted_iota(jnp.int32, parts[0].shape, 1)
    low_half = lane < 2 * width
    low_quarter = lane % (2 * width) < width

    def trade(one, other, mask, shift):
        return (
            jnp.where(mask, one, pltpu.roll(other, shift, 1)),
            jnp.where(mask, pltpu.roll(one, LANES - shift, 1), other),
        )

    first, third = trade(parts[0], parts[2], low_half, 2 * width)
    second, fourth = trade(parts[1], parts[3], low_half, 2 * width)
    first, second = trade(first, second, low_quarter, width)
    third, fourth = trade(third, fourth, low_quarter, width)
    return first, second, third, fourth


def pack_rows(field_ref, rows_ref):
    channels, cells_x, cells_y, _ = field_ref.shape
    for channel in range(channels):
        for place in range(cells_x):
            row = (channel * cells_x + place) * cells_y
            rows_ref[row : row + cells_y, :] = field_ref[channel, place]


def start(source, target, semaphore):
    copy = pltpu.make_async_copy(source, target, semaphore)
    copy.start()
    return copy


def to_plane_modes(rows_ref, high_ref, low_ref, out_ref):
    half = rows_ref.shape[1] // 2
    block = out_ref.shape[0] // 16
    for parity in range(2):
        one, other = rows_ref[:, :half], rows_ref[:, half:]
        values = one - other if parity else one + other
        waves = product((high_ref[parity], low_ref[parity]), halves(values), 1, 1)
        for k in range(8):
            row = slot(2 * k + parity) * block
            out_ref[row : row + block, :] = waves[k * block : (k + 1) * block]


def from_plane_modes(got_ref, high_ref, low_ref):
    block = got_ref.shape[0] // 16
    waves = []
    for parity in range(2):
        rows = [slot(2 * k + parity) * block for k in range(8)]
        parts = [got_ref[row : row + block, :] for row in rows]
        waves.append(product(halves(jnp.concatenate(parts, axis=0)), (high_ref[parity], low_ref[parity]), 0, 0))
    return jnp.concatenate([waves[0] + waves[1], waves[0] - waves[1]], axis=1)


def slot(owner):
    return owner % 4 * 4 + owner // 4


def spans_of(channels, step):
    return [(first, min(first + step, channels)) for first in range(0, channels, step)]


def front_kernel(
    field_hbm, high_hbm, low_hbm, weight_hbm, out_ref, head_ref, field_ref, high_ref, low_ref, rows_ref, table_sems, field_sems, head_sem
):
    channels, cells_x, cells_y, _ = field_ref.shape
    cells = cells_x * cells_y
    pieces = []
    for first, last in spans_of(channels, 4):
        span = pl.ds(first, last - first)
        pieces.append(start(field_hbm.at[span], field_ref.at[span], field_sems.at[len(pieces)]))
        if first == 0:
            tables = [start(high_hbm, high_ref, table_sems.at[0]), start(low_hbm, low_ref, table_sems.at[1])]
    head = start(weight_hbm.at[:, :, pl.ds(0, head_ref.shape[2])], head_ref, head_sem)
    for piece, (first, last) in enumerate(spans_of(channels, 4)):
        pieces[piece].wait()
        for channel in range(first, last):
            for place in range(cells_x):
                row = channel * cells + place * cells_y
                rows_ref[row : row + cells_y, :] = field_ref[channel, place]
    for copy in tables:
        copy.wait()
    to_plane_modes(rows_ref, high_ref, low_ref, out_ref)
    head.wait()


def blocks_even(shape):
    return lax.broadcasted_iota(jnp.int32, shape, 1) // KX % 2 == 0


def in_ky_order(even, odd):
    mask = blocks_even(even.shape)
    low = jnp.where(mask, even, odd)
    high = jnp.where(mask, pltpu.roll(even, LANES - KX, 1), pltpu.roll(odd, KX, 1))
    return low, high


def by_ky_parity(low, high):
    mask = blocks_even(low.shape)
    even = jnp.where(mask, low, pltpu.roll(high, KX, 1))
    odd = jnp.where(mask, pltpu.roll(high, LANES - KX, 1), low)
    return even, odd


def mode_kernel(
    head_ref,
    got_ref,
    weight_hbm,
    high_ref,
    low_ref,
    out_hbm,
    spectra_hbm,
    weight_ref,
    out_ref,
    spectra_ref,
    field_ref,
    mixed_ref,
    weight_sems,
    spectra_sem,
    out_sems,
):
    _, channels, local_modes, modes = spectra_ref.shape
    conjugate = head_ref is None
    chunk = channels // weight_sems.shape[0]
    weight_copies = []
    for k in range(weight_sems.shape[0]):
        if k == 0 and not conjugate:
            continue
        span = pl.ds(k * chunk, chunk)
        place = (slice(None), span) if conjugate else (slice(None), slice(None), span)
        weight_copies.append(start(weight_hbm.at[place], weight_ref.at[place], weight_sems.at[k]))
    rows = channels * local_modes
    block = 2 * local_modes
    quads = got_ref.shape[0] // (4 * block)
    groups = channels // 4

    def owner_rows(quad, j):
        first = slot(4 * quad + j) * block
        return slice(first, first + block)

    for pair in range(quads // 2):
        for group in range(groups):
            lanes = slice(group * LANES, (group + 1) * LANES)
            near_half, far_half = [
                [got_ref[owner_rows(2 * pair + i, 2 * half + j), lanes] for i in range(2) for j in range(2)] for half in range(2)
            ]
            sums = [one + other for one, other in zip(near_half, far_half)]
            gaps = [one - other for one, other in zip(near_half, far_half)]
            for parity, parts in enumerate((sums, gaps)):
                for m, part in enumerate(swap_groups(parts)):
                    row = (4 * group + m) * local_modes
                    for side in range(2):
                        field_ref[
                            parity, side * rows + row : side * rows + row + local_modes, pair * LANES : (pair + 1) * LANES
                        ] = part[side * local_modes : (side + 1) * local_modes]
    real = []
    imag = []
    for parity in range(2):
        waves = product(halves(field_ref[parity]), (high_ref[parity], low_ref[parity]), 1, 0)
        real.append(waves[:rows, :LANES] + waves[rows:, LANES:])
        imag.append(waves[rows:, :LANES] - waves[:rows, LANES:])
    for part, pair in enumerate((real, imag)):
        for k, values in enumerate(in_ky_order(*pair)):
            spectra_ref[part, :, :, k * LANES : (k + 1) * LANES] = values.reshape(channels, local_modes, LANES)
    spectra_copy = start(spectra_ref, spectra_hbm, spectra_sem)
    for part in range(weight_sems.shape[0] * 2):
        first_lane = part % 2 * LANES
        first_result = part // 2 * chunk
        span = slice(first_lane, first_lane + LANES)
        ins = [(spectra_ref[0, c, :, span], spectra_ref[1, c, :, span]) for c in range(channels)]
        if first_lane == 0 and (conjugate or first_result > 0):
            weight_copies[part // 2 - (not conjugate)].wait()
        mixing_ref = weight_ref if conjugate or first_result > 0 else head_ref

        def one(step, carry, span=span, ins=ins, first_result=first_result, mixing_ref=mixing_ref):
            result = first_result + step
            total_real = jnp.zeros((local_modes, LANES), jnp.float32)
            total_imag = jnp.zeros((local_modes, LANES), jnp.float32)
            for c, (in_real, in_imag) in enumerate(ins):
                if conjugate:
                    w_real = mixing_ref[0, result, c, :, span]
                    w_imag = mixing_ref[1, result, c, :, span]
                    total_real = total_real + (in_real * w_real + in_imag * w_imag)
                    total_imag = total_imag + (in_imag * w_real - in_real * w_imag)
                else:
                    w_real = mixing_ref[0, c, result, :, span]
                    w_imag = mixing_ref[1, c, result, :, span]
                    total_real = total_real + (in_real * w_real - in_imag * w_imag)
                    total_imag = total_imag + (in_imag * w_real + in_real * w_imag)
            row = pl.multiple_of(result * local_modes, local_modes)
            mixed_ref[0, pl.ds(row, local_modes), span] = total_real
            mixed_ref[1, pl.ds(row, local_modes), span] = total_imag
            return carry

        lax.fori_loop(0, chunk, one, 0, unroll=True)
    out_copies = []
    for first, last in spans_of(groups, -(-groups // 2)):
        begin, end = 4 * first * local_modes, 4 * last * local_modes
        reals = by_ky_parity(mixed_ref[0, begin:end, :LANES], mixed_ref[0, begin:end, LANES:])
        imags = by_ky_parity(mixed_ref[1, begin:end, :LANES], mixed_ref[1, begin:end, LANES:])
        for parity in range(2):
            left = jnp.concatenate([reals[parity], imags[parity]], axis=0)
            right = jnp.concatenate([-imags[parity], reals[parity]], axis=0)
            both = halves(jnp.concatenate([left, right], axis=1))
            field_ref[parity, 2 * begin : 2 * end, :] = product(both, (high_ref[parity], low_ref[parity]), 1, 1)
        for pair in range(quads // 2):
            for group in range(first, last):
                lanes = slice(group * LANES, (group + 1) * LANES)
                for side in range(2):
                    base = 2 * begin + side * (end - begin) + 4 * (group - first) * local_modes
                    sums, gaps = [
                        swap_groups(
                            [
                                field_ref[
                                    parity,
                                    base + m * local_modes : base + (m + 1) * local_modes,
                                    pair * LANES : (pair + 1) * LANES,
                                ]
                                for m in range(4)
                            ]
                        )
                        for parity in range(2)
                    ]
                    for k in range(4):
                        owner = 4 * (2 * pair + k // 2) + k % 2
                        row = slot(owner) * block + side * local_modes
                        other = slot(owner + 2) * block + side * local_modes
                        out_ref[row : row + local_modes, lanes] = sums[k] + gaps[k]
                        out_ref[other : other + local_modes, lanes] = sums[k] - gaps[k]
        place = (slice(None), pl.ds(first * LANES, (last - first) * LANES))
        out_copies.append(start(out_ref.at[place], out_hbm.at[place], out_sems.at[len(out_copies)]))
    spectra_copy.wait()
    for copy in out_copies:
        copy.wait()


def channel_sums(transposed, rows_ref, weight_ref, bias_ref, out_ref, channels):
    height = rows_ref.shape[0] // channels
    for lane in range(0, rows_ref.shape[1], LANES):
        span = slice(lane, lane + LANES)

        def one(step, carry, span=span):
            ins = [rows_ref[pl.ds(pl.multiple_of(i * height + step * 8, 8), 8), span] for i in range(channels)]
            for o in range(channels):
                total = None
                for i in range(channels):
                    factor = weight_ref[i, o] if transposed else weight_ref[o, i]
                    term = ins[i] * factor
                    total = term if total is None else total + term
                if bias_ref is not None:
                    total = total + bias_ref[o]
                out_ref[pl.ds(pl.multiple_of(o * height + step * 8, 8), 8), span] = total
            return carry

        lax.fori_loop(0, height // 8, one, 0)


def local_kernel(field_ref, upstream_ref, weight_ref, bias_ref, out_ref, packed_ref, rows_ref):
    pack_rows(field_ref, rows_ref)
    pack_rows(upstream_ref, packed_ref)
    channel_sums(False, rows_ref, weight_ref, bias_ref, out_ref, field_ref.shape[0])


def middle_kernel(got_ref, local_hbm, upstream_hbm, high_ref, low_ref, out_ref, grad_ref, local_ref, upstream_ref, sems):
    spans = [pl.ds(first, last - first) for first, last in spans_of(local_ref.shape[0], 128)]
    copies = [
        (start(local_hbm.at[span], local_ref.at[span], sems.at[0, k]), start(upstream_hbm.at[span], upstream_ref.at[span], sems.at[1, k]))
        for k, span in enumerate(spans)
    ]
    grad_ref[...] = from_plane_modes(got_ref, high_ref, low_ref)
    for k, span in enumerate(spans):
        rows = slice(span.start, span.start + span.size)
        for copy in copies[k]:
            copy.wait()
        grad_ref[rows, :] = upstream_ref[rows, :] * gelu_slope(grad_ref[rows, :] + local_ref[rows, :])
    to_plane_modes(grad_ref, high_ref, low_ref, out_ref)


def grads_kernel(rows_ref, weight_ref, out_ref):
    channel_sums(True, rows_ref, weight_ref, None, out_ref, weight_ref.shape[0])


def last_kernel(got_ref, local_ref, high_ref, low_ref, out_hbm, rows_ref, out_ref, sems):
    channels, cells_x, cells_y, _ = out_ref.shape
    cells = cells_x * cells_y
    rows_ref[...] = from_plane_modes(got_ref, high_ref, low_ref)
    leaving = []
    for first, last in spans_of(channels, 4):
        rows = slice(first * cells, last * cells)
        rows_ref[rows, :] = rows_ref[rows, :] + local_ref[rows, :]
        for channel in range(first, last):
            for place in range(cells_x):
                row = channel * cells + place * cells_y
                out_ref[channel, place] = rows_ref[row : row + cells_y, :]
        span = pl.ds(first, last - first)
        leaving.append(start(out_ref.at[span], out_hbm.at[span], sems.at[len(leaving)]))
    for copy in leaving:
        copy.wait()


def outer_kernel(first_spectra, second_spectra, first_grads, second_grads, out_ref):
    _, channels, local_modes, modes = first_spectra.shape
    sources = out_ref.shape[1]
    pairs = ((first_spectra, first_grads), (second_spectra, second_grads))

    def one(step, carry):
        source = pl.program_id(0) * sources + step
        for lane in range(0, modes, LANES):
            span = slice(lane, lane + LANES)
            ins = [(spectra[0, source, :, span], spectra[1, source, :, span]) for spectra, _ in pairs]
            for o in range(channels):
                total_real = None
                total_imag = None
                for (_, grads), (in_real, in_imag) in zip(pairs, ins):
                    g_real = grads[0, o, :, span]
                    g_imag = grads[1, o, :, span]
                    real = g_real * in_real + g_imag * in_imag
                    imag = g_imag * in_real - g_real * in_imag
                    total_real = real if total_real is None else total_real + real
                    total_imag = imag if total_imag is None else total_imag + imag
                out_ref[0, step, o, :, span] = total_real
                out_ref[1, step, o, :, span] = total_imag
        return carry

    lax.fori_loop(0, sources, one, 0)


def in_order(own):
    other = lax.ppermute(own, "dp", [(0, 1), (1, 0)])
    first = lax.axis_index("dp") == 0
    return jnp.where(first, own, other), jnp.where(first, other, own)


def far(*values):
    return [pltpu.with_memory_space_constraint(v, pltpu.HBM) for v in values]


def near(*values):
    return [pltpu.with_memory_space_constraint(v, pltpu.VMEM) for v in values]


def on_tiles(cell_values, cotangent, spectral_weight, channel_weight, channel_bias):
    sample_cells = cell_values[0]
    upstream = cotangent[0]
    count_x = lax.axis_size("gx")
    count_y = lax.axis_size("gy")
    owners = count_x * count_y
    channels, cells_x, cells_y, depth_time = sample_cells.shape
    local_modes = spectral_weight.shape[3]
    modes = spectral_weight.shape[4]
    rows = channels * cells_x * cells_y
    plane = [jnp.asarray(t) for t in host_halves(host_plane(owners, local_modes))]
    cross = [jnp.asarray(t) for t in host_halves(host_cross(count_x, count_y, cells_x, cells_y))]
    f32 = jnp.float32
    bf16 = jnp.bfloat16
    whole = pl.BlockSpec(memory_space=pltpu.VMEM)
    scalars = pl.BlockSpec(memory_space=pltpu.SMEM)
    stays = pl.BlockSpec(memory_space=pltpu.HBM)
    copies = pltpu.SemaphoreType.DMA
    vmem = pltpu.VMEM
    sent = (owners * 2 * local_modes, rows)
    cells = (rows, depth_time)
    spectrum = (2, channels, local_modes, modes)
    group = next(g for g in (4, 2, 1) if channels % g == 0)

    def held(shape):
        return pltpu.HBM(shape, f32)

    def trade(values):
        return lax.all_to_all(values, ("gy", "gx"), split_axis=0, concat_axis=0, tiled=True)

    def across(values, *head):
        conjugate = not head

        def body(*refs):
            mode_kernel(*((None,) if conjugate else ()), *refs)

        return pl.pallas_call(
            body,
            out_shape=(held(sent), held(spectrum)),
            in_specs=[*[whole] * len(head), whole, stays, whole, whole],
            out_specs=(stays, stays),
            scratch_shapes=[
                vmem(spectral_weight.shape, f32),
                vmem(sent, f32),
                vmem(spectrum, f32),
                vmem((2, 2 * channels * local_modes, owners * cells_x * cells_y // 2), f32),
                vmem((2, channels * local_modes, modes), f32),
                copies((5 if conjugate else 4,)),
                copies,
                copies((2,)),
            ],
            compiler_params=params(),
            name="unmix_modes" if conjugate else "mix_modes",
        )(*near(*head, values), *far(spectral_weight), *near(*cross))

    front, head = pl.pallas_call(
        front_kernel,
        out_shape=(vmem(sent, f32), vmem((2, channels, channels // 4, local_modes, modes), f32)),
        in_specs=[stays] * 4,
        out_specs=(whole, whole),
        scratch_shapes=[
            vmem(sample_cells.shape, f32),
            vmem(plane[0].shape, bf16),
            vmem(plane[1].shape, bf16),
            vmem(cells, f32),
            copies((2,)),
            copies((-(-channels // 4),)),
            copies,
        ],
        compiler_params=params(),
        name="front",
    )(*far(sample_cells, *plane, spectral_weight))
    got = trade(front)
    local, packed = pl.pallas_call(
        local_kernel,
        out_shape=(held(cells), held(cells)),
        in_specs=[whole, whole, scalars, scalars],
        out_specs=(whole, whole),
        scratch_shapes=[vmem(cells, f32)],
        compiler_params=params(),
        name="local_pre",
    )(*far(sample_cells, upstream), channel_weight, channel_bias)
    mixed, spectra = across(got, head)
    both_spectra = in_order(spectra)
    got, both_spectra = lax.optimization_barrier((trade(mixed), both_spectra))
    front, grad_pre = pl.pallas_call(
        middle_kernel,
        out_shape=(vmem(sent, f32), vmem(cells, f32)),
        in_specs=[whole, stays, stays, whole, whole],
        out_specs=(whole, whole),
        scratch_shapes=[vmem(cells, f32), vmem(cells, f32), copies((2, -(-rows // 128)))],
        compiler_params=params(),
        name="middle",
    )(*near(got), *far(local, packed), *near(*plane))
    got = trade(front)
    back, grad_spectra = across(got)
    both_grads = in_order(grad_spectra)
    got = trade(back)
    local_grad = pl.pallas_call(
        grads_kernel,
        out_shape=held(cells),
        in_specs=[whole, scalars],
        out_specs=whole,
        compiler_params=params(),
        name="local_grad",
    )(*far(grad_pre), channel_weight)
    spectral_grads = pl.pallas_call(
        outer_kernel,
        out_shape=held(spectral_weight.shape),
        grid=(channels // group,),
        in_specs=[whole] * 4,
        out_specs=pl.BlockSpec((2, group, channels, local_modes, modes), lambda i: (0, i, 0, 0, 0)),
        compiler_params=params(),
        name="outer",
    )(*far(*both_spectra), *near(*both_grads))
    cell_grad = pl.pallas_call(
        last_kernel,
        out_shape=held(sample_cells.shape),
        in_specs=[whole] * 4,
        out_specs=stays,
        scratch_shapes=[vmem(cells, f32), vmem(sample_cells.shape, f32), copies((-(-channels // 4),))],
        compiler_params=params(),
        name="last",
    )(*near(got, local_grad, *plane))
    return (cell_grad[None], spectral_grads)


def solution(mesh):
    placed = (
        P("dp", None, "gx", "gy", None),
        P("dp", None, "gx", "gy", None),
        P(None, None, None, ("gx", "gy"), None),
        P(),
        P(),
    )

    def on_any(*args):
        _, channels, cells_x, cells_y, _ = args[0].shape
        fits = args[2].shape[3] == 8 and args[2].shape[4] == 2 * LANES and KX * KY == 2 * LANES and cells_x * cells_y == LANES // 4
        fits = fits and channels % 20 == 0 and args[2].shape[3] == KT and KZ * KT == 16 * 8 and lax.axis_size("dp") == 2
        fits = fits and lax.axis_size("gx") == 4 and lax.axis_size("gy") == 4 and cells_y * 4 == KY
        return on_tiles(*args) if fits else on_device(*args)

    return jax.shard_map(
        on_any,
        mesh=mesh,
        in_specs=placed,
        out_specs=(P("dp", None, "gx", "gy", None), P(None, None, None, ("gx", "gy"), None)),
        check_vma=False,
    )
```
